32 devices in a mesh: dp: 32 (over z, y, x, core).
Axes of the slice: x: 2, y: 2, z: 4, core: 2. Of those that a mesh axis runs over, the one named last changes fastest.
Arguments:
- latents: bfloat16 [32, 256, 768], P('dp'), may hold values from -6 to 6
- conditioning: bfloat16 [32, 768], P('dp'), may hold values from -3 to 3
- cotangent: bfloat16 [32, 256, 768], P('dp'), may hold values from -6 to 6
- weights: float32 [18, 768, 768], P(None, 'dp'), may hold values from -1 to 1
- biases: float32 [14, 768], P(None, 'dp'), may hold values from -1.8 to 1.8
- momenta: float32 [18, 768, 768], P(None, 'dp'), may hold values from -0.3 to 0.3
- bias_momenta: float32 [14, 768], P(None, 'dp'), may hold values from -1.8 to 1.8
- counts: int32 [32], replicated, may hold values from 0 to 1, as said below
Outputs:
- output: bfloat16 [32, 256, 768], P('dp')
- input_grad: float32 [32, 256, 768], P('dp')
- cond_grad: float32 [32, 768], P('dp')
- weight_grads: float32 [18, 768, 768], P(None, 'dp')
- bias_grads: float32 [14, 768], P(None, 'dp')
- new_weights: float32 [18, 768, 768], P(None, 'dp')
- new_momenta: float32 [18, 768, 768], P(None, 'dp')
- new_biases: float32 [14, 768], P(None, 'dp')
- new_bias_momenta: float32 [14, 768], P(None, 'dp')
The draws below stay inside these ranges and needn't reach their ends.
Inputs may be any that keep to these rules, and one draw needn't show every extreme that they name: Device d's first counts[d] of its 1 slots are live. Exactly 18 devices hold no live latent, every other device holds at least one, and some device holds 1.
All inputs are finite; a program needn't handle non-finite values.
Results may differ from the reference program's by a relative error of at most 0.01.
The reference program's roundings to bfloat16 on the way count: a program that leaves them out, or rounds other values in their place, can miss the bound.
Values may be sent and summed in bfloat16 or wider, within the bound.
No kernel may reach another device: no remote copies, remote signals or barrier semaphores. Data moves between devices by JAX's collectives and lax.ppermute only.
A program may use at most 256 MiB of HBM per device.

```python
import jax
import jax.numpy as jnp
from jax import lax

D = 768
HEADS = 12
FF = 3072
SEQ = 256
LAT_CAP = 1
NS_ITERS = 2
LATENTS = 32
BLOCKS = 18
BIAS_ROWS = 14
N_DP = 32


def draw_counts(key, part):
    shuffled = jax.random.permutation(jax.random.fold_in(key, 11), N_DP)
    placed = jnp.zeros((N_DP,), jnp.int32).at[shuffled].set(jnp.arange(N_DP, dtype=jnp.int32))
    spread = jax.random.randint(jax.random.fold_in(key, 12), (N_DP,), 1, LAT_CAP + 1)
    filled = jnp.where(placed < BLOCKS, 0, jnp.where(placed == BLOCKS, LAT_CAP, spread))
    return filled.astype(jnp.int32)


def draw_weights(key, part):
    normal_values = jax.random.normal(jax.random.fold_in(key, 21), (BLOCKS, D, D), jnp.float32)
    normal_values = jnp.clip(normal_values, -4.0, 4.0)
    block_ids = jnp.arange(BLOCKS)
    first_down = 10 + FF // D
    widths = jnp.where(block_ids == 9, (D // 8) ** (-0.5), jnp.where(block_ids >= first_down, FF ** (-0.5), D ** (-0.5)))
    return (normal_values * widths[:, None, None]).astype(jnp.float32)


def shard_levels(own_key, dims, pieces, low, largest):
    def one(dim, shards_of):
        heights = jax.random.uniform(jax.random.fold_in(jax.random.fold_in(own_key, 6), dim), (shards_of,), jnp.float32, low / len(pieces), largest / len(pieces))
        return jnp.repeat(jnp.exp(heights), dims[dim] // shards_of).reshape((-1,) + (1,) * (len(dims) - dim - 1))

    level = one(*pieces[0])
    for cut in pieces[1:]:
        level = level * one(*cut)
    return level


def gaussian(rng, extent, scale, most, pieces=(), held_as=jnp.bfloat16):
    array = jax.random.normal(rng, extent, jnp.float32) * scale
    if len(pieces) > 0:
        array = shard_levels(rng, extent, pieces, -0.22, 0.18) * array
    return jnp.clip(array, min=-most, max=most).astype(held_as)


def setup_inputs(seed: int = 0) -> dict:
    arg_keys = jax.random.split(jax.random.key(seed), 9)
    return {
        "latents": gaussian(arg_keys[0], (LATENTS, SEQ, D), 1.0, 6.0, ((0, 32),)),
        "conditioning": gaussian(arg_keys[1], (LATENTS, D), 1.0, 3.0, ((0, 32),)),
        "cotangent": gaussian(arg_keys[2], (LATENTS, SEQ, D), 1.0, 6.0, ((0, 32),)),
        "weights": draw_weights(jax.random.fold_in(arg_keys[8], 71), 0),
        "biases": gaussian(arg_keys[4], (BIAS_ROWS, D), 0.3, 1.8, ((1, 32),), jnp.float32),
        "momenta": gaussian(arg_keys[5], (BLOCKS, D, D), 0.05, 0.3, ((1, 32),), jnp.float32),
        "bias_momenta": gaussian(arg_keys[6], (BIAS_ROWS, D), 0.3, 1.8, ((1, 32),), jnp.float32),
        "counts": draw_counts(jax.random.fold_in(arg_keys[8], 71), 0),
    }


COEF_FIRST = 3.4445
COEF_SECOND = -4.775
COEF_THIRD = 2.0315
BETA_WEIGHT = 0.95
BETA_BIAS = 0.9
RATE_WEIGHT = 1.0
RATE_BIAS = 0.1
NORM_EPS = 1e-06

def product(spec, left, right):
    return jnp.einsum(spec, left.astype(jnp.float32), right.astype(jnp.float32))

def gelu_tanh(values):
    return 0.5 * values * (1.0 + jnp.tanh(0.7978845608028654 * (values + 0.044715 * values * values * values)))

def layer_norm(stream):
    centred = stream - lax.optimization_barrier(jnp.mean(stream, axis=-1, keepdims=True))
    inverse = lax.rsqrt(lax.optimization_barrier(jnp.mean(centred * centred, axis=-1, keepdims=True)) + NORM_EPS)
    return (centred * inverse, inverse)

def norm_back(normed, inverse, upstream):
    return inverse * (upstream - lax.optimization_barrier(jnp.mean(upstream, axis=-1, keepdims=True)) - normed * lax.optimization_barrier(jnp.mean(upstream * normed, axis=-1, keepdims=True)))

def forward_latent(operands, matrices, offsets):
    source, condition = operands
    seqlen, features = source.shape
    head_count = HEADS
    head_width = features // head_count
    hidden_blocks = (matrices.shape[0] - 10) // 2
    stream = source.astype(jnp.float32)
    silu_cond = jax.nn.silu(condition.astype(jnp.float32)).astype(jnp.bfloat16)
    modulation = product('d,kde->ke', silu_cond, matrices[:6]) + offsets[:6]
    normed_one, inverse_one = layer_norm(stream)
    attn_input = (normed_one * (1.0 + modulation[1]) + modulation[0]).astype(jnp.bfloat16)
    query = product('sd,de->se', attn_input, matrices[6]) + offsets[6]
    keys = product('sd,de->se', attn_input, matrices[7])
    values = product('sd,de->se', attn_input, matrices[8]) + offsets[7]
    query_b = query.astype(jnp.bfloat16).reshape(seqlen, head_count, head_width)
    keys_b = keys.astype(jnp.bfloat16).reshape(seqlen, head_count, head_width)
    values_b = values.astype(jnp.bfloat16).reshape(seqlen, head_count, head_width)
    scores = product('qhe,khe->hqk', query_b, keys_b) * head_width ** (-0.5)
    log_total = jnp.log(lax.optimization_barrier(jnp.sum(jnp.exp(scores), axis=-1)))
    probs_b = jnp.exp(scores - log_total[..., None]).astype(jnp.bfloat16)
    context = product('hqk,khe->qhe', probs_b, values_b).reshape(seqlen, features).astype(jnp.bfloat16)
    attn_out = product('sd,de->se', context, matrices[9]) + offsets[8]
    middle = stream + modulation[2] * attn_out
    normed_two, inverse_two = layer_norm(middle)
    mlp_input = (normed_two * (1.0 + modulation[4]) + modulation[3]).astype(jnp.bfloat16)
    hidden_pre = product('sd,kde->ske', mlp_input, matrices[10:10 + hidden_blocks]) + offsets[9:9 + hidden_blocks]
    hidden_b = gelu_tanh(hidden_pre).astype(jnp.bfloat16)
    mlp_out = product('ske,ked->sd', hidden_b, matrices[10 + hidden_blocks:]) + offsets[9 + hidden_blocks]
    output = (middle + modulation[5] * mlp_out).astype(jnp.bfloat16)
    kept = (silu_cond, modulation, normed_one, inverse_one, attn_input, query_b, keys_b, values_b, log_total, context, attn_out, normed_two, inverse_two, mlp_input, hidden_pre, hidden_b, mlp_out)
    return (output, kept)

def backward_latent(operands, matrices):
    upstream, condition, kept = operands
    silu_cond, modulation, normed_one, inverse_one, attn_input, query_b, keys_b, values_b, log_total, context, attn_out, normed_two, inverse_two, mlp_input, hidden_pre, hidden_b, mlp_out = kept
    seqlen, head_count, head_width = query_b.shape
    features = head_count * head_width
    hidden_blocks = hidden_pre.shape[1]
    grad_out = upstream.astype(jnp.float32)
    grad_gate_two = lax.optimization_barrier(jnp.sum(grad_out * mlp_out, axis=0))
    grad_mlp = grad_out * modulation[5]
    grad_mlp_b = grad_mlp.astype(jnp.bfloat16)
    grad_down = product('ske,sd->ked', hidden_b, grad_mlp_b)
    grad_hidden = product('sd,ked->ske', grad_mlp_b, matrices[10 + hidden_blocks:])
    gelu_back = jax.vjp(gelu_tanh, hidden_pre)[1]
    grad_pre = gelu_back(grad_hidden)[0]
    grad_pre_b = grad_pre.astype(jnp.bfloat16)
    grad_up = product('sd,ske->kde', mlp_input, grad_pre_b)
    grad_mlp_in = product('ske,kde->sd', grad_pre_b, matrices[10:10 + hidden_blocks])
    grad_shift_two = lax.optimization_barrier(jnp.sum(grad_mlp_in, axis=0))
    grad_scale_two = lax.optimization_barrier(jnp.sum(grad_mlp_in * normed_two, axis=0))
    grad_middle = grad_out + norm_back(normed_two, inverse_two, grad_mlp_in * (1.0 + modulation[4]))
    grad_gate_one = lax.optimization_barrier(jnp.sum(grad_middle * attn_out, axis=0))
    grad_attn = grad_middle * modulation[2]
    grad_attn_b = grad_attn.astype(jnp.bfloat16)
    grad_proj = product('sd,se->de', context, grad_attn_b)
    grad_context = product('se,de->sd', grad_attn_b, matrices[9]).astype(jnp.bfloat16).reshape(seqlen, head_count, head_width)
    scores = product('qhe,khe->hqk', query_b, keys_b) * head_width ** (-0.5)
    probs = jnp.exp(scores - log_total[..., None])
    probs_b = probs.astype(jnp.bfloat16)
    grad_values = product('hqk,qhe->khe', probs_b, grad_context).reshape(seqlen, features)
    grad_probs = product('qhe,khe->hqk', grad_context, values_b)
    row_dot = lax.optimization_barrier(jnp.sum(probs * grad_probs, axis=-1, keepdims=True))
    grad_scores_b = (probs * (grad_probs - row_dot) * head_width ** (-0.5)).astype(jnp.bfloat16)
    grad_query = product('hqk,khe->qhe', grad_scores_b, keys_b).reshape(seqlen, features)
    grad_keys = product('hqk,qhe->khe', grad_scores_b, query_b).reshape(seqlen, features)
    grad_qkv_b = jnp.stack([grad_query, grad_keys, grad_values]).astype(jnp.bfloat16)
    grad_qkv_w = product('sd,kse->kde', attn_input, grad_qkv_b)
    grad_attn_in = product('kse,kde->sd', grad_qkv_b, matrices[6:9])
    grad_shift_one = lax.optimization_barrier(jnp.sum(grad_attn_in, axis=0))
    grad_scale_one = lax.optimization_barrier(jnp.sum(grad_attn_in * normed_one, axis=0))
    grad_source = grad_middle + norm_back(normed_one, inverse_one, grad_attn_in * (1.0 + modulation[1]))
    grad_mod = jnp.stack([grad_shift_one, grad_scale_one, grad_gate_one, grad_shift_two, grad_scale_two, grad_gate_two])
    grad_mod_b = grad_mod.astype(jnp.bfloat16)
    grad_silu = product('ke,kde->d', grad_mod_b, matrices[:6])
    silu_back = jax.vjp(jax.nn.silu, condition.astype(jnp.float32))[1]
    grad_cond = silu_back(grad_silu)[0] * seqlen ** (-0.5)
    grad_mats = jnp.concatenate([grad_qkv_w, grad_proj[None], grad_up, grad_down], axis=0)
    grad_offsets = jnp.concatenate([grad_mod, lax.optimization_barrier(jnp.sum(grad_query, axis=0))[None], lax.optimization_barrier(jnp.sum(grad_values, axis=0))[None], lax.optimization_barrier(jnp.sum(grad_attn, axis=0))[None], lax.optimization_barrier(jnp.sum(grad_pre, axis=0)), lax.optimization_barrier(jnp.sum(grad_mlp, axis=0))[None]], axis=0)
    return (grad_source, grad_cond, grad_mats, grad_offsets, grad_mod_b)

def orthogonalize(block):
    values = block.astype(jnp.float32)
    scaled = (values / (jnp.sqrt(jnp.sum(values * values)) + 1e-07)).astype(jnp.bfloat16)
    for iteration in range(NS_ITERS):
        gram = jnp.dot(scaled, scaled.T, preferred_element_type=jnp.float32).astype(jnp.bfloat16)
        square = jnp.dot(gram, gram, preferred_element_type=jnp.float32)
        mixed = (COEF_SECOND * gram.astype(jnp.float32) + COEF_THIRD * square).astype(jnp.bfloat16)
        scaled = (COEF_FIRST * scaled.astype(jnp.float32) + jnp.dot(mixed, scaled, preferred_element_type=jnp.float32)).astype(jnp.bfloat16)
    return scaled

def reference(latents, conditioning, cotangent, weights, biases, momenta, bias_momenta, counts):
    matrices = weights.astype(jnp.bfloat16)
    offsets = lax.optimization_barrier(biases.astype(jnp.bfloat16)).astype(jnp.float32)
    latent_ids = jnp.arange(LATENTS, dtype=jnp.int32)
    live = (latent_ids % LAT_CAP < counts[latent_ids // LAT_CAP]).astype(jnp.float32)

    def advance(totals, inputs_now):
        mats_sum, offsets_sum = totals
        source, condition, upstream, live_flag = inputs_now
        output, kept = forward_latent((source, condition), matrices, offsets)
        grad_source, grad_cond, grad_mats, grad_offsets, grad_mod_b = backward_latent((upstream, condition, kept), matrices)
        grad_ada = product('d,ke->kde', kept[0], grad_mod_b)
        whole = jnp.concatenate([grad_ada, grad_mats], axis=0)
        alive = live_flag > 0.5
        return ((mats_sum + live_flag * whole, offsets_sum + live_flag * grad_offsets), (jnp.where(alive, output, jnp.zeros_like(output)), jnp.where(alive, grad_source, jnp.zeros_like(grad_source)), jnp.where(alive, grad_cond, jnp.zeros_like(grad_cond))))
    start = (jnp.zeros(weights.shape, jnp.float32), jnp.zeros(biases.shape, jnp.float32))
    (mats_total, offsets_total), (outputs, input_grads, cond_grads) = lax.scan(advance, start, (latents, conditioning, cotangent, live))
    grad_scale = lax.rsqrt((SEQ * jnp.sum(counts)).astype(jnp.float32))
    weight_grads = mats_total * grad_scale
    bias_grads = offsets_total * grad_scale
    new_momenta = BETA_WEIGHT * momenta + weight_grads
    ortho = lax.map(orthogonalize, new_momenta.astype(jnp.bfloat16))
    new_weights = weights - RATE_WEIGHT * ortho.astype(jnp.float32)
    new_bias_momenta = BETA_BIAS * bias_momenta + bias_grads
    new_biases = biases - RATE_BIAS * new_bias_momenta
    return (outputs, input_grads, cond_grads, weight_grads, bias_grads, new_weights, new_momenta, new_biases, new_bias_momenta)
```

```python
import jax
import jax.numpy as jnp
from jax import lax
from jax.sharding import PartitionSpec as P

HEADS = 12
NS_ITERS = 2
ADA = 6
COLOURS = 3

COEF_FIRST = 3.4445
COEF_SECOND = -4.775
COEF_THIRD = 2.0315
BETA_WEIGHT = 0.95
BETA_BIAS = 0.9
RATE_WEIGHT = 1.0
RATE_BIAS = 0.1
NORM_EPS = 1e-06


def product(spec, left, right):
    return jnp.einsum(spec, left, right, preferred_element_type=jnp.float32)


def flip(values, bit):
    devices = lax.axis_size("dp")
    return lax.ppermute(values, "dp", [(i, i ^ (1 << bit)) for i in range(devices)])


def bit_of(myself, bit):
    return (myself >> bit) & 1


def joined(values, other, taken, axis):
    return jnp.where(
        taken == 1, jnp.stack([other, values], axis), jnp.stack([values, other], axis)
    )


def gather_bits(values, order, myself, axis):
    have = []
    for bit in order:
        other = flip(values, bit)
        position = axis + sum(1 for held in have if held > bit)
        values = joined(values, other, bit_of(myself, bit), position)
        have.append(bit)
    return values


def scatter_bits(values, order, myself, axis, sent_as):
    left = sorted(order, reverse=True)
    for bit in order:
        position = axis + left.index(bit)
        left.remove(bit)
        mine = bit_of(myself, bit)
        send = lax.dynamic_index_in_dim(values, 1 - mine, position, keepdims=False)
        keep = lax.dynamic_index_in_dim(values, mine, position, keepdims=False)
        values = keep + flip(send.astype(sent_as), bit).astype(jnp.float32)
    return values


def exchange_bits(values, order, myself):
    devices = values.shape[0]
    tail = values.shape[1:]
    count = len(order)
    values = values.reshape((2,) * count + tail)
    for bit in order:
        position = count - 1 - bit
        mine = bit_of(myself, bit)
        send = lax.dynamic_index_in_dim(values, 1 - mine, position, keepdims=False)
        keep = lax.dynamic_index_in_dim(values, mine, position, keepdims=False)
        values = joined(keep, flip(send, bit), mine, position)
    return values.reshape((devices,) + tail)


def index_bits(devices):
    return devices.bit_length() - 1


def colour_orders(devices):
    chip_bits = list(range(1, index_bits(devices)))
    rest, last = chip_bits[:-1], chip_bits[-1:]
    shifts = [(colour * len(rest)) // COLOURS for colour in range(COLOURS)]
    return [tuple(rest[shift:] + rest[:shift] + last) for shift in shifts]


def gelu_tanh(values):
    return (
        0.5
        * values
        * (1.0 + jnp.tanh(0.7978845608028654 * (values + 0.044715 * values * values * values)))
    )


def layer_norm(stream):
    centred = stream - jnp.mean(stream, axis=-1, keepdims=True)
    inverse = lax.rsqrt(jnp.mean(centred * centred, axis=-1, keepdims=True) + NORM_EPS)
    return (centred * inverse, inverse)


def norm_back(normed, inverse, upstream):
    return inverse * (
        upstream
        - jnp.mean(upstream, axis=-1, keepdims=True)
        - normed * jnp.mean(upstream * normed, axis=-1, keepdims=True)
    )


def forward_latent(source, modulation, attn_w, up_w, down_w, offsets):
    seqlen, features = source.shape
    hidden_blocks = up_w.shape[0]
    head_width = features // HEADS
    stream = source.astype(jnp.float32)
    normed_one, inverse_one = layer_norm(stream)
    attn_input = (normed_one * (1.0 + modulation[1]) + modulation[0]).astype(jnp.bfloat16)
    query = product("sd,de->se", attn_input, attn_w[0]) + offsets[6]
    keys = product("sd,de->se", attn_input, attn_w[1])
    values = product("sd,de->se", attn_input, attn_w[2]) + offsets[7]
    query_b = query.astype(jnp.bfloat16).reshape(seqlen, HEADS, head_width)
    keys_b = keys.astype(jnp.bfloat16).reshape(seqlen, HEADS, head_width)
    values_b = values.astype(jnp.bfloat16).reshape(seqlen, HEADS, head_width)
    scores = product("qhe,khe->hqk", query_b, keys_b) * head_width ** (-0.5)
    log_total = jnp.log(jnp.sum(jnp.exp(scores), axis=-1))
    probs_b = jnp.exp(scores - log_total[..., None]).astype(jnp.bfloat16)
    context = (
        product("hqk,khe->qhe", probs_b, values_b).reshape(seqlen, features).astype(jnp.bfloat16)
    )
    attn_out = product("sd,de->se", context, attn_w[3]) + offsets[8]
    middle = stream + modulation[2] * attn_out
    normed_two, inverse_two = layer_norm(middle)
    mlp_input = (normed_two * (1.0 + modulation[4]) + modulation[3]).astype(jnp.bfloat16)
    hidden_pre = (
        product("sd,kde->kse", mlp_input, up_w) + offsets[9 : 9 + hidden_blocks, None, :]
    )
    hidden_b = gelu_tanh(hidden_pre).astype(jnp.bfloat16)
    mlp_out = product("kse,ked->sd", hidden_b, down_w) + offsets[9 + hidden_blocks]
    output = (middle + modulation[5] * mlp_out).astype(jnp.bfloat16)
    kept = (
        normed_one,
        inverse_one,
        attn_input,
        query_b,
        keys_b,
        values_b,
        log_total,
        context,
        attn_out,
        normed_two,
        inverse_two,
        mlp_input,
        hidden_pre,
        hidden_b,
        mlp_out,
    )
    return (output, kept)


def backward_latent(upstream, modulation, kept, attn_w, up_w, down_w):
    (
        normed_one,
        inverse_one,
        attn_input,
        query_b,
        keys_b,
        values_b,
        log_total,
        context,
        attn_out,
        normed_two,
        inverse_two,
        mlp_input,
        hidden_pre,
        hidden_b,
        mlp_out,
    ) = kept
    seqlen, head_count, head_width = query_b.shape
    features = head_count * head_width
    grad_out = upstream.astype(jnp.float32)
    grad_gate_two = jnp.sum(grad_out * mlp_out, axis=0)
    grad_mlp = grad_out * modulation[5]
    grad_mlp_b = grad_mlp.astype(jnp.bfloat16)
    grad_hidden = product("sd,ked->kse", grad_mlp_b, down_w)
    gelu_back = jax.vjp(gelu_tanh, hidden_pre)[1]
    grad_pre = gelu_back(grad_hidden)[0]
    grad_pre_b = grad_pre.astype(jnp.bfloat16)
    grad_mlp_in = product("kse,kde->sd", grad_pre_b, up_w)
    grad_shift_two = jnp.sum(grad_mlp_in, axis=0)
    grad_scale_two = jnp.sum(grad_mlp_in * normed_two, axis=0)
    grad_middle = grad_out + norm_back(normed_two, inverse_two, grad_mlp_in * (1.0 + modulation[4]))
    grad_gate_one = jnp.sum(grad_middle * attn_out, axis=0)
    grad_attn = grad_middle * modulation[2]
    grad_attn_b = grad_attn.astype(jnp.bfloat16)
    grad_context = (
        product("se,de->sd", grad_attn_b, attn_w[3])
        .astype(jnp.bfloat16)
        .reshape(seqlen, head_count, head_width)
    )
    scores = product("qhe,khe->hqk", query_b, keys_b) * head_width ** (-0.5)
    probs = jnp.exp(scores - log_total[..., None])
    probs_b = probs.astype(jnp.bfloat16)
    grad_values = product("hqk,qhe->khe", probs_b, grad_context).reshape(seqlen, features)
    grad_probs = product("qhe,khe->hqk", grad_context, values_b)
    row_dot = jnp.sum(probs * grad_probs, axis=-1, keepdims=True)
    grad_scores_b = (probs * (grad_probs - row_dot) * head_width ** (-0.5)).astype(jnp.bfloat16)
    grad_query = product("hqk,khe->qhe", grad_scores_b, keys_b).reshape(seqlen, features)
    grad_keys = product("hqk,qhe->khe", grad_scores_b, query_b).reshape(seqlen, features)
    grad_qkv_b = jnp.stack([grad_query, grad_keys, grad_values]).astype(jnp.bfloat16)
    grad_attn_in = product("kse,kde->sd", grad_qkv_b, attn_w[:3])
    grad_shift_one = jnp.sum(grad_attn_in, axis=0)
    grad_scale_one = jnp.sum(grad_attn_in * normed_one, axis=0)
    grad_source = grad_middle + norm_back(
        normed_one, inverse_one, grad_attn_in * (1.0 + modulation[1])
    )
    grad_offsets = jnp.concatenate(
        [
            jnp.stack(
                [
                    grad_shift_one,
                    grad_scale_one,
                    grad_gate_one,
                    grad_shift_two,
                    grad_scale_two,
                    grad_gate_two,
                    jnp.sum(grad_query, axis=0),
                    jnp.sum(grad_values, axis=0),
                    jnp.sum(grad_attn, axis=0),
                ]
            ),
            jnp.sum(grad_pre, axis=1),
            jnp.sum(grad_mlp, axis=0)[None],
        ],
        axis=0,
    )
    return (grad_source, grad_mlp_b, grad_pre_b, grad_attn_b, grad_qkv_b, grad_offsets)


def orthogonalize(block):
    values = block.astype(jnp.float32)
    scaled = (values / (jnp.sqrt(jnp.sum(values * values)) + 1e-07)).astype(jnp.bfloat16)
    for iteration in range(NS_ITERS):
        gram = jnp.dot(scaled, scaled.T, preferred_element_type=jnp.float32).astype(jnp.bfloat16)
        square = jnp.dot(gram, gram, preferred_element_type=jnp.float32)
        mixed = (COEF_SECOND * gram.astype(jnp.float32) + COEF_THIRD * square).astype(jnp.bfloat16)
        scaled = (
            COEF_FIRST * scaled.astype(jnp.float32)
            + jnp.dot(mixed, scaled, preferred_element_type=jnp.float32)
        ).astype(jnp.bfloat16)
    return scaled


def half_columns(values, which):
    width = values.shape[-1] // 2
    return lax.dynamic_slice_in_dim(values, which * width, width, values.ndim - 1)


def on_device(latents, conditioning, cotangent, weights, biases, momenta, bias_momenta, counts):
    _, seqlen, features = latents.shape
    block_count, share, _ = weights.shape
    hidden_blocks = (block_count - 10) // 2
    bias_count = biases.shape[0]
    devices = lax.axis_size("dp")
    myself = lax.axis_index("dp")
    core = bit_of(myself, 0)
    bits = index_bits(devices)
    every = tuple(range(bits))
    orders = colour_orders(devices)
    ranks = jnp.arange(devices, dtype=jnp.int32)
    live_here = jnp.sum(jnp.where(ranks == myself, counts, 0)) > 0

    lowered = weights.astype(jnp.bfloat16)
    ada_w = lowered[:ADA]
    condition = conditioning[0].astype(jnp.float32)
    silu_cond = jax.nn.silu(condition).astype(jnp.bfloat16)
    small = jnp.concatenate([silu_cond, biases.astype(jnp.bfloat16).reshape(-1)])
    small_all = gather_bits(small, every, myself, 0).reshape(devices, -1)
    silu_all = small_all[:, :features]
    offsets = (
        small_all[:, features:]
        .reshape(devices, bias_count, share)
        .transpose(1, 0, 2)
        .reshape(bias_count, features)
        .astype(jnp.float32)
    )
    silu_rows = lax.dynamic_slice_in_dim(silu_all, myself * share, share, 1)
    mod_parts = product("ld,kde->lke", silu_rows, ada_w)
    modulation = (
        scatter_bits(
            mod_parts.reshape((2,) * bits + mod_parts.shape[1:]), every, myself, 0, jnp.float32
        )
        + offsets[:ADA]
    )
    groups = [
        lowered[ADA:10],
        lowered[10 : 10 + hidden_blocks],
        lowered[10 + hidden_blocks :],
    ]
    attn_w, up_w, down_w = [
        gather_bits(group, tuple(reversed(order)) + (0,), myself, 1).reshape(
            group.shape[0], features, features
        )
        for group, order in zip(groups, orders)
    ]

    outputs, kept = forward_latent(latents[0], modulation, attn_w, up_w, down_w, offsets)
    source_grad, grad_mlp_b, grad_pre_b, grad_attn_b, grad_qkv_b, grad_offsets = backward_latent(
        cotangent[0], modulation, kept, attn_w, up_w, down_w
    )
    attn_input, context, mlp_input, hidden_b = kept[2], kept[7], kept[11], kept[13]
    mask_low = live_here.astype(jnp.bfloat16)
    mask_high = live_here.astype(jnp.float32)
    grad_offsets = grad_offsets * mask_high

    def both(left, right):
        right = right * mask_low
        left_other = flip(left, 0)
        right_other = flip(half_columns(right, 1 - core), 0)
        right_mine = half_columns(right, core)
        return (
            jnp.concatenate([left, left_other], axis=-2),
            jnp.concatenate([right_mine, right_other], axis=-2),
        )

    def spread(mats):
        count, _, width = mats.shape
        return mats.reshape((count,) + (2,) * (bits - 1) + (2 * share, width))

    down_left, down_right = both(hidden_b, grad_mlp_b)
    up_left, up_right = both(mlp_input, grad_pre_b)
    proj_left, proj_right = both(context, grad_attn_b)
    qkv_left, qkv_right = both(attn_input, grad_qkv_b)
    down_mats = product("ksd,se->kde", down_left, down_right)
    up_mats = product("sd,kse->kde", up_left, up_right)
    attn_mats = jnp.concatenate(
        [
            product("sd,kse->kde", qkv_left, qkv_right),
            product("sd,se->de", proj_left, proj_right)[None],
        ]
    )
    sums = [
        scatter_bits(spread(mats), order, myself, 1, jnp.bfloat16)
        for mats, order in zip((attn_mats, up_mats, down_mats), (orders[2], orders[1], orders[0]))
    ]
    chip_rows = jnp.concatenate(sums, axis=0)
    rows_mine = lax.dynamic_slice_in_dim(chip_rows, core * share, share, 1)
    rows_other = flip(lax.dynamic_slice_in_dim(chip_rows, (1 - core) * share, share, 1), 0)
    rest_share = jnp.where(
        core == 1,
        jnp.concatenate([rows_other, rows_mine], axis=2),
        jnp.concatenate([rows_mine, rows_other], axis=2),
    )

    grad_mod_b = grad_offsets[:ADA].astype(jnp.bfloat16)
    mod_all = gather_bits(grad_mod_b.reshape(-1), every, myself, 0).reshape(devices, ADA, features)
    ada_share = product("ld,lke->kde", silu_rows, mod_all)
    silu_parts = product("lke,kde->ld", mod_all, ada_w)
    grad_silu = exchange_bits(silu_parts, every, myself).reshape(features)
    silu_back = jax.vjp(jax.nn.silu, condition)[1]
    cond_grad = silu_back(grad_silu)[0] * seqlen ** (-0.5)
    offset_share = scatter_bits(
        grad_offsets.reshape(bias_count, devices, share)
        .transpose(1, 0, 2)
        .reshape((2,) * bits + (bias_count, share)),
        every,
        myself,
        0,
        jnp.float32,
    )

    grad_scale = lax.rsqrt((seqlen * jnp.sum(counts)).astype(jnp.float32))
    weight_grads = jnp.concatenate([ada_share, rest_share], axis=0) * grad_scale
    bias_grads = offset_share * grad_scale
    new_momenta = BETA_WEIGHT * momenta + weight_grads
    new_bias_momenta = BETA_BIAS * bias_momenta + bias_grads
    new_biases = biases - RATE_BIAS * new_bias_momenta

    owners = [(block * devices) // block_count for block in range(block_count)]
    lowered_momenta = new_momenta.astype(jnp.bfloat16)
    empty = jnp.zeros((share, features), jnp.bfloat16)
    outgoing = jnp.stack(
        [
            lowered_momenta[owners.index(rank)] if rank in owners else empty
            for rank in range(devices)
        ]
    )
    incoming = lax.all_to_all(outgoing, "dp", split_axis=0, concat_axis=0, tiled=True)
    ortho = orthogonalize(incoming.reshape(features, features))
    returned = lax.all_to_all(
        ortho.reshape(devices, share, features), "dp", split_axis=0, concat_axis=0, tiled=True
    )
    ortho_local = jnp.stack([returned[owner] for owner in owners])
    new_weights = weights - RATE_WEIGHT * ortho_local.astype(jnp.float32)
    output = jnp.where(live_here, outputs, jnp.zeros_like(outputs))[None]
    input_grad = jnp.where(live_here, source_grad, jnp.zeros_like(source_grad))[None]
    cond_grad = jnp.where(live_here, cond_grad, jnp.zeros_like(cond_grad))[None]
    return (
        output,
        input_grad,
        cond_grad,
        weight_grads,
        bias_grads,
        new_weights,
        new_momenta,
        new_biases,
        new_bias_momenta,
    )


def solution(mesh):
    return jax.shard_map(
        on_device,
        mesh=mesh,
        in_specs=(
            P("dp", None, None),
            P("dp", None),
            P("dp", None, None),
            P(None, "dp", None),
            P(None, "dp"),
            P(None, "dp", None),
            P(None, "dp"),
            P(),
        ),
        out_specs=(
            P("dp", None, None),
            P("dp", None, None),
            P("dp", None),
            P(None, "dp", None),
            P(None, "dp"),
            P(None, "dp", None),
            P(None, "dp", None),
            P(None, "dp"),
            P(None, "dp"),
        ),
        check_vma=False,
    )
```

```python
import jax
import jax.numpy as jnp
from jax import lax
from jax.experimental import pallas as pl
from jax.experimental.pallas import tpu as pltpu
from jax.sharding import PartitionSpec as P

HEADS = 12
NS_ITERS = 2
ADA = 6
COLOURS = 3

COEF_FIRST = 3.4445
COEF_SECOND = -4.775
COEF_THIRD = 2.0315
BETA_WEIGHT = 0.95
BETA_BIAS = 0.9
RATE_WEIGHT = 1.0
RATE_BIAS = 0.1
NORM_EPS = 1e-06


def product(spec, left, right):
    return jnp.einsum(spec, left, right, preferred_element_type=jnp.float32)


def flip(values, bit):
    devices = lax.axis_size("dp")
    return lax.ppermute(values, "dp", [(i, i ^ (1 << bit)) for i in range(devices)])


def bit_of(myself, bit):
    return (myself >> bit) & 1


def joined(values, other, taken, axis):
    return jnp.where(
        taken == 1, jnp.stack([other, values], axis), jnp.stack([values, other], axis)
    )


def gather_bits(values, order, myself, axis):
    have = []
    for bit in order:
        other = flip(values, bit)
        position = axis + sum(1 for held in have if held > bit)
        values = joined(values, other, bit_of(myself, bit), position)
        have.append(bit)
    return values


def scatter_bits(values, order, myself, axis, sent_as):
    left = sorted(order, reverse=True)
    for bit in order:
        position = axis + left.index(bit)
        left.remove(bit)
        mine = bit_of(myself, bit)
        send = lax.dynamic_index_in_dim(values, 1 - mine, position, keepdims=False)
        keep = lax.dynamic_index_in_dim(values, mine, position, keepdims=False)
        values = keep + flip(send.astype(sent_as), bit).astype(jnp.float32)
    return values


def index_bits(devices):
    return devices.bit_length() - 1


def colour_orders(devices):
    chip_bits = list(range(1, index_bits(devices)))
    rest, last = chip_bits[:-1], chip_bits[-1:]
    shifts = [(colour * len(rest)) // COLOURS for colour in range(COLOURS)]
    return [tuple(rest[shift:] + rest[:shift] + last) for shift in shifts]


def contract(left, right, left_dim, right_dim):
    return lax.dot_general(
        left, right, (((left_dim,), (right_dim,)), ((), ())), preferred_element_type=jnp.float32
    )


def layer_norm(stream):
    centred = stream - jnp.mean(stream, axis=-1, keepdims=True)
    inverse = lax.rsqrt(jnp.mean(centred * centred, axis=-1, keepdims=True) + NORM_EPS)
    return (centred * inverse, inverse)


def norm_back(normed, inverse, upstream):
    return inverse * (
        upstream
        - jnp.mean(upstream, axis=-1, keepdims=True)
        - normed * jnp.mean(upstream * normed, axis=-1, keepdims=True)
    )


def column_sum(values):
    return jnp.sum(values, axis=0, keepdims=True)


def scores_of(query, keys, width):
    return contract(query, keys, 1, 1) * width ** (-0.5)


def attention_forward(source_ref, mod_ref, offsets_ref, weights_ref, lefts_ref, qkv_ref, *rest):
    attn_ref, middle_ref = rest
    seqlen, features = source_ref.shape
    width = features // HEADS
    stream = source_ref[...].astype(jnp.float32)
    normed, _ = layer_norm(stream)
    attn_input = (normed * (1.0 + mod_ref[1:2]) + mod_ref[0:1]).astype(jnp.bfloat16)
    lefts_ref[0] = attn_input
    qkv_ref[0] = (contract(attn_input, weights_ref[0], 1, 0) + offsets_ref[6:7]).astype(
        jnp.bfloat16
    )
    qkv_ref[1] = contract(attn_input, weights_ref[1], 1, 0).astype(jnp.bfloat16)
    qkv_ref[2] = (contract(attn_input, weights_ref[2], 1, 0) + offsets_ref[7:8]).astype(
        jnp.bfloat16
    )
    first = lax.broadcasted_iota(jnp.int32, (seqlen, 2 * width), 1) < width
    for pair in range(HEADS // 2):
        columns = slice(2 * width * pair, 2 * width * (pair + 1))
        query, keys, values = qkv_ref[0, :, columns], qkv_ref[1, :, columns], qkv_ref[2, :, columns]
        halves = []
        for mask in (first, jnp.logical_not(first)):
            scores = scores_of(jnp.where(mask, query, jnp.zeros_like(query)), keys, width)
            log_total = jnp.log(jnp.sum(jnp.exp(scores), axis=-1, keepdims=True))
            probs = jnp.exp(scores - log_total).astype(jnp.bfloat16)
            halves.append(contract(probs, values, 1, 0))
        lefts_ref[1, :, columns] = jnp.where(first, *halves).astype(jnp.bfloat16)
    attn_out = contract(lefts_ref[1], weights_ref[3], 1, 0) + offsets_ref[8:9]
    attn_ref[...] = attn_out
    middle = stream + mod_ref[2:3] * attn_out
    middle_ref[...] = middle
    normed_two, _ = layer_norm(middle)
    lefts_ref[2] = (normed_two * (1.0 + mod_ref[4:5]) + mod_ref[3:4]).astype(jnp.bfloat16)


def split_columns(values, core):
    width = values.shape[-1] // 2
    low, high = values[:, :width], values[:, width:]
    return (jnp.where(core == 1, high, low), jnp.where(core == 1, low, high))


def mlp_both_ways(
    place_ref,
    lefts_ref,
    middle_ref,
    attn_ref,
    upstream_ref,
    mod_ref,
    offsets_ref,
    up_ref,
    down_ref,
    output_ref,
    hidden_ref,
    keep_ref,
    send_ref,
    grad_middle_ref,
    grad_attn_ref,
    rows_ref,
    total_ref,
    grad_total_ref,
    grad_mlp_ref,
):
    step = pl.program_id(0)
    last = pl.num_programs(0) - 1
    core, live = place_ref[0], place_ref[1] > 0
    scale = 0.7978845608028654

    @pl.when(step == 0)
    def _():
        total_ref[...] = jnp.zeros_like(total_ref)
        grad_total_ref[...] = jnp.zeros_like(grad_total_ref)
        grad_mlp = jnp.where(live, upstream_ref[...].astype(jnp.float32) * mod_ref[5:6], 0.0)
        grad_mlp_b = grad_mlp.astype(jnp.bfloat16)
        grad_mlp_ref[...] = grad_mlp_b
        keep_ref[0], send_ref[0] = split_columns(grad_mlp_b, core)
        rows_ref[...] = jnp.zeros_like(rows_ref)
        rows_ref[pl.ds(10 + last, 1)] = column_sum(grad_mlp)

    up_w, down_w = up_ref[0], down_ref[0]
    before = contract(lefts_ref[0], up_w, 1, 0) + offsets_ref[pl.ds(9 + step, 1)]
    square = before * before
    bend = jnp.tanh(scale * (before + 0.044715 * square * before))
    hidden = (0.5 * before * (1.0 + bend)).astype(jnp.bfloat16)
    hidden_ref[0] = hidden
    total_ref[...] += contract(hidden, down_w, 1, 0)
    slope = 0.5 * (1.0 + bend) + 0.5 * before * (1.0 - bend * bend) * scale * (
        1.0 + 3.0 * 0.044715 * square
    )
    grad_pre = jnp.where(live, contract(grad_mlp_ref[...], down_w, 1, 1) * slope, 0.0)
    grad_pre_b = grad_pre.astype(jnp.bfloat16)
    keep_ref[step + 1], send_ref[step + 1] = split_columns(grad_pre_b, core)
    rows_ref[pl.ds(9 + step, 1)] = column_sum(grad_pre)
    grad_total_ref[...] += contract(grad_pre_b, up_w, 1, 1)

    @pl.when(step == last)
    def _():
        middle = middle_ref[...]
        grad_out = upstream_ref[...].astype(jnp.float32)
        mlp_out = total_ref[...] + offsets_ref[pl.ds(10 + last, 1)]
        output = middle + mod_ref[5:6] * mlp_out
        output_ref[...] = jnp.where(live, output, 0.0).astype(jnp.bfloat16)
        rows_ref[5:6] = jnp.where(live, column_sum(grad_out * mlp_out), 0.0)
        normed, inverse = layer_norm(middle)
        grad_in = grad_total_ref[...]
        rows_ref[3:4] = column_sum(grad_in)
        rows_ref[4:5] = column_sum(grad_in * normed)
        grad_middle = grad_out + norm_back(normed, inverse, grad_in * (1.0 + mod_ref[4:5]))
        grad_middle = jnp.where(live, grad_middle, 0.0)
        grad_middle_ref[...] = grad_middle
        rows_ref[2:3] = column_sum(grad_middle * attn_ref[...])
        grad_attn = grad_middle * mod_ref[2:3]
        grad_attn_ref[...] = grad_attn.astype(jnp.bfloat16)
        rows_ref[8:9] = column_sum(grad_attn)


def attention_backward(
    place_ref,
    source_ref,
    mod_ref,
    weights_ref,
    qkv_ref,
    grad_middle_ref,
    grad_attn_ref,
    rows_in_ref,
    grad_source_ref,
    keep_ref,
    send_ref,
    rows_ref,
    grads_ref,
    context_ref,
):
    seqlen, features = source_ref.shape
    width = features // HEADS
    core, live = place_ref[0], place_ref[1] > 0
    rows_ref[...] = rows_in_ref[...]
    grad_attn = grad_attn_ref[...]
    keep_ref[3], send_ref[3] = split_columns(grad_attn, core)
    context_ref[...] = contract(grad_attn, weights_ref[3], 1, 1).astype(jnp.bfloat16)
    first = lax.broadcasted_iota(jnp.int32, (seqlen, 2 * width), 1) < width
    for pair in range(HEADS // 2):
        columns = slice(2 * width * pair, 2 * width * (pair + 1))
        query, keys, values = qkv_ref[0, :, columns], qkv_ref[1, :, columns], qkv_ref[2, :, columns]
        upstream = context_ref[:, columns]
        parts = []
        for mask in (first, jnp.logical_not(first)):
            scores = scores_of(jnp.where(mask, query, jnp.zeros_like(query)), keys, width)
            log_total = jnp.log(jnp.sum(jnp.exp(scores), axis=-1, keepdims=True))
            probs = jnp.exp(scores - log_total)
            grad_values = contract(probs.astype(jnp.bfloat16), upstream, 0, 0)
            grad_probs = contract(
                jnp.where(mask, upstream, jnp.zeros_like(upstream)), values, 1, 1
            )
            row_dot = jnp.sum(probs * grad_probs, axis=-1, keepdims=True)
            grad_scores = (probs * (grad_probs - row_dot) * width ** (-0.5)).astype(jnp.bfloat16)
            parts.append(
                (
                    contract(grad_scores, keys, 1, 0),
                    contract(grad_scores, query, 0, 0),
                    grad_values,
                )
            )
        for index in range(3):
            merged = jnp.where(live, jnp.where(first, parts[0][index], parts[1][index]), 0.0)
            grads_ref[index, :, columns] = merged.astype(jnp.bfloat16)
            if index != 1:
                row = 6 if index == 0 else 7
                rows_ref[row : row + 1, columns] = column_sum(merged)
    grad_in = jnp.zeros((seqlen, features), jnp.float32)
    for index in range(3):
        grads = grads_ref[index]
        keep_ref[index], send_ref[index] = split_columns(grads, core)
        grad_in += contract(grads, weights_ref[index], 1, 1)
    normed, inverse = layer_norm(source_ref[...].astype(jnp.float32))
    rows_ref[0:1] = column_sum(grad_in)
    rows_ref[1:2] = column_sum(grad_in * normed)
    grad_source_ref[...] = jnp.where(
        live,
        grad_middle_ref[...] + norm_back(normed, inverse, grad_in * (1.0 + mod_ref[1:2])),
        0.0,
    )


def pair_products(left_ref, left_other_ref, right_ref, right_other_ref, out_ref):
    out_ref[0] = contract(left_ref[0], right_ref[0], 0, 0) + contract(
        left_other_ref[0], right_other_ref[0], 0, 0
    )


def struct(shape, dtype):
    return jax.ShapeDtypeStruct(shape, dtype)


VMEM = pl.BlockSpec(memory_space=pltpu.VMEM)
SMEM = pl.BlockSpec(memory_space=pltpu.SMEM)


def resident(shape):
    zeros = (0,) * len(shape)
    return pl.BlockSpec(shape, lambda step: zeros)


def run_attention_forward(source, modulation, offsets, attn_w):
    seqlen, features = source.shape
    return pl.pallas_call(
        attention_forward,
        name="attention_forward",
        out_shape=(
            struct((3, seqlen, features), jnp.bfloat16),
            struct((3, seqlen, features), jnp.bfloat16),
            struct((seqlen, features), jnp.float32),
            struct((seqlen, features), jnp.float32),
        ),
        in_specs=[VMEM] * 4,
        out_specs=(VMEM,) * 4,
        compiler_params=pltpu.CompilerParams(vmem_limit_bytes=40 << 20),
        cost_estimate=pl.CostEstimate(
            flops=8 * seqlen * features * features + 8 * HEADS * seqlen * seqlen * 128,
            bytes_accessed=attn_w.size * 2 + source.size * 20,
            transcendentals=2 * HEADS * seqlen * seqlen,
        ),
    )(source, modulation, offsets, attn_w)


def run_mlp(place, lefts, middle, attn_out, upstream, modulation, offsets, up_w, down_w):
    seqlen, features = middle.shape
    steps = up_w.shape[0]
    half = features // 2
    whole = (seqlen, features)
    return pl.pallas_call(
        mlp_both_ways,
        name="mlp_both_ways",
        grid=(steps,),
        out_shape=(
            struct(whole, jnp.bfloat16),
            struct((steps,) + whole, jnp.bfloat16),
            struct((steps + 1, seqlen, half), jnp.bfloat16),
            struct((steps + 1, seqlen, half), jnp.bfloat16),
            struct(whole, jnp.float32),
            struct(whole, jnp.bfloat16),
            struct(offsets.shape, jnp.float32),
        ),
        in_specs=[
            SMEM,
            pl.BlockSpec((1,) + whole, lambda step: (2, 0, 0)),
            resident(whole),
            resident(whole),
            resident(whole),
            resident(modulation.shape),
            resident(offsets.shape),
            pl.BlockSpec((1, features, features), lambda step: (step, 0, 0)),
            pl.BlockSpec((1, features, features), lambda step: (step, 0, 0)),
        ],
        out_specs=(
            resident(whole),
            pl.BlockSpec((1,) + whole, lambda step: (step, 0, 0)),
            resident((steps + 1, seqlen, half)),
            resident((steps + 1, seqlen, half)),
            resident(whole),
            resident(whole),
            resident(offsets.shape),
        ),
        scratch_shapes=[
            pltpu.VMEM(whole, jnp.float32),
            pltpu.VMEM(whole, jnp.float32),
            pltpu.VMEM(whole, jnp.bfloat16),
        ],
        compiler_params=pltpu.CompilerParams(vmem_limit_bytes=48 << 20),
        cost_estimate=pl.CostEstimate(
            flops=8 * seqlen * features * features * steps,
            bytes_accessed=up_w.size * 4 + seqlen * features * 40,
            transcendentals=seqlen * features * steps,
        ),
    )(place, lefts, middle, attn_out, upstream, modulation, offsets, up_w, down_w)


def run_attention_backward(place, source, modulation, attn_w, qkv, grad_middle, grad_attn, rows):
    seqlen, features = source.shape
    half = features // 2
    return pl.pallas_call(
        attention_backward,
        name="attention_backward",
        out_shape=(
            struct((seqlen, features), jnp.float32),
            struct((4, seqlen, half), jnp.bfloat16),
            struct((4, seqlen, half), jnp.bfloat16),
            struct(rows.shape, jnp.float32),
        ),
        in_specs=[SMEM] + [VMEM] * 7,
        out_specs=(VMEM,) * 4,
        scratch_shapes=[
            pltpu.VMEM((3, seqlen, features), jnp.bfloat16),
            pltpu.VMEM((seqlen, features), jnp.bfloat16),
        ],
        compiler_params=pltpu.CompilerParams(vmem_limit_bytes=40 << 20),
        cost_estimate=pl.CostEstimate(
            flops=8 * seqlen * features * features + 20 * HEADS * seqlen * seqlen * 128,
            bytes_accessed=attn_w.size * 2 + source.size * 24,
            transcendentals=2 * HEADS * seqlen * seqlen,
        ),
    )(place, source, modulation, attn_w, qkv, grad_middle, grad_attn, rows)


def run_products(lefts, lefts_other, rights, rights_other, left_at, right_at, count):
    _, seqlen, features = lefts.shape
    half = rights.shape[-1]
    left_spec = pl.BlockSpec((1, seqlen, features), lambda step: (left_at(step), 0, 0))
    right_spec = pl.BlockSpec((1, seqlen, half), lambda step: (right_at(step), 0, 0))
    return pl.pallas_call(
        pair_products,
        name="pair_products",
        grid=(count,),
        out_shape=struct((count, features, half), jnp.float32),
        in_specs=[left_spec, left_spec, right_spec, right_spec],
        out_specs=pl.BlockSpec((1, features, half), lambda step: (step, 0, 0)),
        cost_estimate=pl.CostEstimate(
            flops=4 * count * seqlen * features * half,
            bytes_accessed=count * features * half * 6,
            transcendentals=0,
        ),
    )(lefts, lefts_other, rights, rights_other)


def orthogonalize(block):
    values = block.astype(jnp.float32)
    scaled = (values / (jnp.sqrt(jnp.sum(values * values)) + 1e-07)).astype(jnp.bfloat16)
    for iteration in range(NS_ITERS):
        gram = jnp.dot(scaled, scaled.T, preferred_element_type=jnp.float32).astype(jnp.bfloat16)
        square = jnp.dot(gram, gram, preferred_element_type=jnp.float32)
        mixed = (COEF_SECOND * gram.astype(jnp.float32) + COEF_THIRD * square).astype(jnp.bfloat16)
        scaled = (
            COEF_FIRST * scaled.astype(jnp.float32)
            + jnp.dot(mixed, scaled, preferred_element_type=jnp.float32)
        ).astype(jnp.bfloat16)
    return scaled


def all_to_all(values):
    return lax.all_to_all(values, "dp", split_axis=0, concat_axis=0, tiled=True)


def to_all(row):
    devices = lax.axis_size("dp")
    return all_to_all(jnp.broadcast_to(row[None], (devices,) + row.shape))


def on_device(latents, conditioning, cotangent, weights, biases, momenta, bias_momenta, counts):
    _, seqlen, features = latents.shape
    block_count, share, _ = weights.shape
    hidden_blocks = (block_count - 10) // 2
    bias_count = biases.shape[0]
    devices = lax.axis_size("dp")
    myself = lax.axis_index("dp")
    core = bit_of(myself, 0)
    bits = index_bits(devices)
    orders = colour_orders(devices)
    ranks = jnp.arange(devices, dtype=jnp.int32)
    live_here = jnp.sum(jnp.where(ranks == myself, counts, 0)) > 0

    lowered = weights.astype(jnp.bfloat16)
    ada_w = lowered[:ADA]
    condition = conditioning[0].astype(jnp.float32)
    silu_cond = jax.nn.silu(condition).astype(jnp.bfloat16)
    small_all = to_all(jnp.concatenate([silu_cond, biases.astype(jnp.bfloat16).reshape(-1)]))
    silu_all = small_all[:, :features]
    offsets = (
        small_all[:, features:]
        .reshape(devices, bias_count, share)
        .transpose(1, 0, 2)
        .reshape(bias_count, features)
        .astype(jnp.float32)
    )
    silu_rows = lax.dynamic_slice_in_dim(silu_all, myself * share, share, 1)
    mod_parts = product("ld,kde->lke", silu_rows, ada_w).reshape(devices, ADA * features)
    modulation = jnp.sum(all_to_all(mod_parts), axis=0).reshape(ADA, features) + offsets[:ADA]
    groups = [
        lowered[ADA:10],
        lowered[10 : 10 + hidden_blocks],
        lowered[10 + hidden_blocks :],
    ]
    attn_w, up_w, down_w = [
        gather_bits(group, tuple(reversed(order)) + (0,), myself, 1).reshape(
            group.shape[0], features, features
        )
        for group, order in zip(groups, orders)
    ]

    place = jnp.stack([core, live_here.astype(jnp.int32)]).astype(jnp.int32)
    lefts, qkv, attn_out, middle = run_attention_forward(latents[0], modulation, offsets, attn_w)
    lefts_other = flip(lefts, 0)
    output, hidden, mlp_keep, mlp_send, grad_middle, grad_attn, rows = run_mlp(
        place, lefts, middle, attn_out, cotangent[0], modulation, offsets, up_w, down_w
    )
    hidden_other = flip(hidden, 0)
    mlp_other = flip(mlp_send, 0)
    input_grad, attn_keep, attn_send, grad_offsets = run_attention_backward(
        place, latents[0], modulation, attn_w, qkv, grad_middle, grad_attn, rows
    )
    attn_other = flip(attn_send, 0)

    def spread(mats):
        count, _, width = mats.shape
        return mats.reshape((count,) + (2,) * (bits - 1) + (2 * share, width))

    down_mats = run_products(
        hidden, hidden_other, mlp_keep, mlp_other, lambda b: b, lambda b: 0, hidden_blocks
    )
    up_mats = run_products(
        lefts, lefts_other, mlp_keep, mlp_other, lambda b: 2, lambda b: b + 1, hidden_blocks
    )
    attn_mats = run_products(
        lefts, lefts_other, attn_keep, attn_other, lambda b: b // 3, lambda b: b, 4
    )
    sums = [
        scatter_bits(spread(mats), order, myself, 1, jnp.bfloat16)
        for mats, order in zip((attn_mats, up_mats, down_mats), (orders[2], orders[1], orders[0]))
    ]
    chip_rows = jnp.concatenate(sums, axis=0)
    rows_mine = lax.dynamic_slice_in_dim(chip_rows, core * share, share, 1)
    rows_other = flip(lax.dynamic_slice_in_dim(chip_rows, (1 - core) * share, share, 1), 0)
    rest_share = jnp.where(
        core == 1,
        jnp.concatenate([rows_other, rows_mine], axis=2),
        jnp.concatenate([rows_mine, rows_other], axis=2),
    )

    grad_mod_b = grad_offsets[:ADA].astype(jnp.bfloat16).reshape(-1)
    by_holder = (
        grad_offsets.reshape(bias_count, devices, share)
        .transpose(1, 0, 2)
        .reshape(devices, bias_count * share)
    )
    coarse = lax.reduce_precision(by_holder, 8, 7)
    mod_and_offsets = all_to_all(
        jnp.concatenate(
            [
                jnp.broadcast_to(grad_mod_b[None], (devices, ADA * features)),
                coarse.astype(jnp.bfloat16),
                (by_holder - coarse).astype(jnp.bfloat16),
            ],
            axis=1,
        )
    )
    mod_all = mod_and_offsets[:, : ADA * features].reshape(devices, ADA, features)
    offset_share = jnp.sum(
        mod_and_offsets[:, ADA * features :]
        .astype(jnp.float32)
        .reshape(devices * 2, bias_count, share),
        axis=0,
    )
    ada_share = product("ld,lke->kde", silu_rows, mod_all)
    silu_parts = product("lke,kde->ld", mod_all, ada_w)
    grad_silu = all_to_all(silu_parts).reshape(features)
    silu_back = jax.vjp(jax.nn.silu, condition)[1]
    cond_grad = silu_back(grad_silu)[0] * seqlen ** (-0.5)

    grad_scale = lax.rsqrt((seqlen * jnp.sum(counts)).astype(jnp.float32))
    weight_grads = jnp.concatenate([ada_share, rest_share], axis=0) * grad_scale
    bias_grads = offset_share * grad_scale
    new_momenta = BETA_WEIGHT * momenta + weight_grads
    new_bias_momenta = BETA_BIAS * bias_momenta + bias_grads
    new_biases = biases - RATE_BIAS * new_bias_momenta

    owners = [(block * devices) // block_count for block in range(block_count)]
    lowered_momenta = new_momenta.astype(jnp.bfloat16)
    empty = jnp.zeros((share, features), jnp.bfloat16)
    outgoing = jnp.stack(
        [
            lowered_momenta[owners.index(rank)] if rank in owners else empty
            for rank in range(devices)
        ]
    )
    incoming = lax.all_to_all(outgoing, "dp", split_axis=0, concat_axis=0, tiled=True)
    ortho = orthogonalize(incoming.reshape(features, features))
    returned = lax.all_to_all(
        ortho.reshape(devices, share, features), "dp", split_axis=0, concat_axis=0, tiled=True
    )
    ortho_local = jnp.stack([returned[owner] for owner in owners])
    new_weights = weights - RATE_WEIGHT * ortho_local.astype(jnp.float32)
    cond_grad = jnp.where(live_here, cond_grad, jnp.zeros_like(cond_grad))[None]
    return (
        output[None],
        input_grad[None],
        cond_grad,
        weight_grads,
        bias_grads,
        new_weights,
        new_momenta,
        new_biases,
        new_bias_momenta,
    )


def solution(mesh):
    return jax.shard_map(
        on_device,
        mesh=mesh,
        in_specs=(
            P("dp", None, None),
            P("dp", None),
            P("dp", None, None),
            P(None, "dp", None),
            P(None, "dp"),
            P(None, "dp", None),
            P(None, "dp"),
            P(),
        ),
        out_specs=(
            P("dp", None, None),
            P("dp", None, None),
            P("dp", None),
            P(None, "dp", None),
            P(None, "dp"),
            P(None, "dp", None),
            P(None, "dp", None),
            P(None, "dp"),
            P(None, "dp"),
        ),
        check_vma=False,
    )
```

```python
import functools

import jax
import jax.numpy as jnp
from jax import lax
from jax.experimental import pallas as pl
from jax.experimental.pallas import tpu as pltpu
from jax.sharding import PartitionSpec as P

HEADS = 12
NS_ITERS = 2
ADA = 6
COLOURS = 3

COEF_FIRST = 3.4445
COEF_SECOND = -4.775
COEF_THIRD = 2.0315
BETA_WEIGHT = 0.95
BETA_BIAS = 0.9
RATE_WEIGHT = 1.0
RATE_BIAS = 0.1
NORM_EPS = 1e-06


def product(spec, left, right):
    return jnp.einsum(spec, left, right, preferred_element_type=jnp.float32)


def flip(values, bit):
    devices = lax.axis_size("dp")
    return lax.ppermute(values, "dp", [(i, i ^ (1 << bit)) for i in range(devices)])


def bit_of(myself, bit):
    return (myself >> bit) & 1


def joined(values, other, taken, axis):
    return jnp.where(
        taken == 1, jnp.stack([other, values], axis), jnp.stack([values, other], axis)
    )


def gather_all(groups, orders, myself, axis, between):
    have = [[] for _ in groups]
    carried = None
    for stage in range(len(orders[0])):
        others = [flip(group, order[stage]) for group, order in zip(groups, orders)]
        if stage in between:
            carried = between[stage](carried)
            others, carried = lax.optimization_barrier((others, carried))
        else:
            others = lax.optimization_barrier(others)
        for index, order in enumerate(orders):
            bit = order[stage]
            position = axis + sum(1 for held in have[index] if held > bit)
            groups[index] = joined(groups[index], others[index], bit_of(myself, bit), position)
            have[index].append(bit)
    return groups, carried


def split_bit(values, mine, position, sent_as):
    send = lax.dynamic_index_in_dim(values, 1 - mine, position, keepdims=False)
    keep = lax.dynamic_index_in_dim(values, mine, position, keepdims=False)
    return keep, send.astype(sent_as)


def scatter_bits(keep, send, order, myself, axis, spread):
    left = sorted(order, reverse=True)
    left.remove(order[0])
    values = keep + flip(send, order[0]).astype(jnp.float32)
    values = spread(values, len(left))
    for bit in order[1:]:
        position = axis + left.index(bit)
        left.remove(bit)
        keep, send = split_bit(values, bit_of(myself, bit), position, jnp.bfloat16)
        values = keep + flip(send, bit).astype(jnp.float32)
    return values


def index_bits(devices):
    return devices.bit_length() - 1


def colour_orders(devices):
    chip_bits = list(range(1, index_bits(devices)))
    rest, last = chip_bits[:-1], chip_bits[-1:]
    shifts = [(colour * len(rest)) // COLOURS for colour in range(COLOURS)]
    return [tuple(rest[shift:] + rest[:shift] + last) for shift in shifts]


def contract(left, right, left_dim, right_dim):
    return lax.dot_general(
        left, right, (((left_dim,), (right_dim,)), ((), ())), preferred_element_type=jnp.float32
    )


def layer_norm(stream):
    centred = stream - jnp.mean(stream, axis=-1, keepdims=True)
    inverse = lax.rsqrt(jnp.mean(centred * centred, axis=-1, keepdims=True) + NORM_EPS)
    return (centred * inverse, inverse)


def norm_back(normed, inverse, upstream):
    return inverse * (
        upstream
        - jnp.mean(upstream, axis=-1, keepdims=True)
        - normed * jnp.mean(upstream * normed, axis=-1, keepdims=True)
    )


def column_sum(values):
    return jnp.sum(values, axis=0, keepdims=True)


def scores_of(query, keys, width):
    return contract(query, keys, 1, 1) * width ** (-0.5)


def whole_weight(mine_ref, other_ref, index, core):
    mine, other = mine_ref[index], other_ref[index]
    return jnp.concatenate(
        [jnp.where(core == 1, other, mine), jnp.where(core == 1, mine, other)], axis=1
    )


def attention_forward(
    place_ref,
    source_ref,
    mod_ref,
    offsets_ref,
    mine_ref,
    other_ref,
    lefts_ref,
    qkv_ref,
    attn_ref,
    middle_ref,
):
    core = place_ref[0]
    seqlen, features = source_ref.shape
    width = features // HEADS
    stream = source_ref[...].astype(jnp.float32)
    normed, _ = layer_norm(stream)
    attn_input = (normed * (1.0 + mod_ref[1:2]) + mod_ref[0:1]).astype(jnp.bfloat16)
    lefts_ref[0] = attn_input
    qkv_ref[0] = (contract(attn_input, whole_weight(mine_ref, other_ref, 0, core), 1, 0) + offsets_ref[6:7]).astype(
        jnp.bfloat16
    )
    qkv_ref[1] = contract(attn_input, whole_weight(mine_ref, other_ref, 1, core), 1, 0).astype(jnp.bfloat16)
    qkv_ref[2] = (contract(attn_input, whole_weight(mine_ref, other_ref, 2, core), 1, 0) + offsets_ref[7:8]).astype(
        jnp.bfloat16
    )
    first = lax.broadcasted_iota(jnp.int32, (seqlen, 2 * width), 1) < width
    for pair in range(HEADS // 2):
        columns = slice(2 * width * pair, 2 * width * (pair + 1))
        query, keys, values = qkv_ref[0, :, columns], qkv_ref[1, :, columns], qkv_ref[2, :, columns]
        halves = []
        for mask in (first, jnp.logical_not(first)):
            scores = scores_of(jnp.where(mask, query, jnp.zeros_like(query)), keys, width)
            log_total = jnp.log(jnp.sum(jnp.exp(scores), axis=-1, keepdims=True))
            probs = jnp.exp(scores - log_total).astype(jnp.bfloat16)
            halves.append(contract(probs, values, 1, 0))
        lefts_ref[1, :, columns] = jnp.where(first, *halves).astype(jnp.bfloat16)
    attn_out = contract(lefts_ref[1], whole_weight(mine_ref, other_ref, 3, core), 1, 0) + offsets_ref[8:9]
    attn_ref[...] = attn_out
    middle = stream + mod_ref[2:3] * attn_out
    middle_ref[...] = middle
    normed_two, _ = layer_norm(middle)
    lefts_ref[2] = (normed_two * (1.0 + mod_ref[4:5]) + mod_ref[3:4]).astype(jnp.bfloat16)


def split_columns(values, core):
    width = values.shape[-1] // 2
    low, high = values[:, :width], values[:, width:]
    return (jnp.where(core == 1, high, low), jnp.where(core == 1, low, high))


def mlp_both_ways(
    place_ref,
    lefts_ref,
    middle_ref,
    attn_ref,
    upstream_ref,
    mod_ref,
    offsets_ref,
    up_ref,
    up_other_ref,
    down_ref,
    down_other_ref,
    output_ref,
    hidden_ref,
    keep_ref,
    send_ref,
    grad_middle_ref,
    grad_attn_ref,
    rows_ref,
    total_ref,
    grad_total_ref,
    grad_mlp_ref,
):
    step = pl.program_id(0)
    last = pl.num_programs(0) - 1
    core, live = place_ref[0], place_ref[1] > 0
    scale = 0.7978845608028654

    @pl.when(step == 0)
    def _():
        total_ref[...] = jnp.zeros_like(total_ref)
        grad_total_ref[...] = jnp.zeros_like(grad_total_ref)
        grad_mlp = jnp.where(live, upstream_ref[...].astype(jnp.float32) * mod_ref[5:6], 0.0)
        grad_mlp_b = grad_mlp.astype(jnp.bfloat16)
        grad_mlp_ref[...] = grad_mlp_b
        keep_ref[0], send_ref[0] = split_columns(grad_mlp_b, core)
        rows_ref[...] = jnp.zeros_like(rows_ref)
        rows_ref[pl.ds(10 + last, 1)] = column_sum(grad_mlp)

    up_w = whole_weight(up_ref, up_other_ref, 0, core)
    down_w = whole_weight(down_ref, down_other_ref, 0, core)
    before = contract(lefts_ref[0], up_w, 1, 0) + offsets_ref[pl.ds(9 + step, 1)]
    square = before * before
    bend = jnp.tanh(scale * (before + 0.044715 * square * before))
    hidden = (0.5 * before * (1.0 + bend)).astype(jnp.bfloat16)
    hidden_ref[0] = hidden
    total_ref[...] += contract(hidden, down_w, 1, 0)
    slope = 0.5 * (1.0 + bend) + 0.5 * before * (1.0 - bend * bend) * scale * (
        1.0 + 3.0 * 0.044715 * square
    )
    grad_pre = jnp.where(live, contract(grad_mlp_ref[...], down_w, 1, 1) * slope, 0.0)
    grad_pre_b = grad_pre.astype(jnp.bfloat16)
    keep_ref[step + 1], send_ref[step + 1] = split_columns(grad_pre_b, core)
    rows_ref[pl.ds(9 + step, 1)] = column_sum(grad_pre)
    grad_total_ref[...] += contract(grad_pre_b, up_w, 1, 1)

    @pl.when(step == last)
    def _():
        middle = middle_ref[...]
        grad_out = upstream_ref[...].astype(jnp.float32)
        mlp_out = total_ref[...] + offsets_ref[pl.ds(10 + last, 1)]
        output = middle + mod_ref[5:6] * mlp_out
        output_ref[...] = jnp.where(live, output, 0.0).astype(jnp.bfloat16)
        rows_ref[5:6] = jnp.where(live, column_sum(grad_out * mlp_out), 0.0)
        normed, inverse = layer_norm(middle)
        grad_in = grad_total_ref[...]
        rows_ref[3:4] = column_sum(grad_in)
        rows_ref[4:5] = column_sum(grad_in * normed)
        grad_middle = grad_out + norm_back(normed, inverse, grad_in * (1.0 + mod_ref[4:5]))
        grad_middle = jnp.where(live, grad_middle, 0.0)
        grad_middle_ref[...] = grad_middle
        rows_ref[2:3] = column_sum(grad_middle * attn_ref[...])
        grad_attn = grad_middle * mod_ref[2:3]
        grad_attn_ref[...] = grad_attn.astype(jnp.bfloat16)
        rows_ref[8:9] = column_sum(grad_attn)


def attention_backward(
    place_ref,
    source_ref,
    mod_ref,
    mine_ref,
    other_ref,
    qkv_ref,
    grad_middle_ref,
    grad_attn_ref,
    rows_in_ref,
    grad_source_ref,
    keep_ref,
    send_ref,
    rows_ref,
    grads_ref,
    context_ref,
):
    seqlen, features = source_ref.shape
    width = features // HEADS
    core, live = place_ref[0], place_ref[1] > 0
    rows_ref[...] = rows_in_ref[...]
    grad_attn = grad_attn_ref[...]
    keep_ref[3], send_ref[3] = split_columns(grad_attn, core)
    context_ref[...] = contract(
        grad_attn, whole_weight(mine_ref, other_ref, 3, core), 1, 1
    ).astype(jnp.bfloat16)
    first = lax.broadcasted_iota(jnp.int32, (seqlen, 2 * width), 1) < width
    for pair in range(HEADS // 2):
        columns = slice(2 * width * pair, 2 * width * (pair + 1))
        query, keys, values = qkv_ref[0, :, columns], qkv_ref[1, :, columns], qkv_ref[2, :, columns]
        upstream = context_ref[:, columns]
        parts = []
        for mask in (first, jnp.logical_not(first)):
            scores = scores_of(jnp.where(mask, query, jnp.zeros_like(query)), keys, width)
            log_total = jnp.log(jnp.sum(jnp.exp(scores), axis=-1, keepdims=True))
            probs = jnp.exp(scores - log_total)
            grad_values = contract(probs.astype(jnp.bfloat16), upstream, 0, 0)
            grad_probs = contract(
                jnp.where(mask, upstream, jnp.zeros_like(upstream)), values, 1, 1
            )
            row_dot = jnp.sum(probs * grad_probs, axis=-1, keepdims=True)
            grad_scores = (probs * (grad_probs - row_dot) * width ** (-0.5)).astype(jnp.bfloat16)
            parts.append(
                (
                    contract(grad_scores, keys, 1, 0),
                    contract(grad_scores, query, 0, 0),
                    grad_values,
                )
            )
        for index in range(3):
            merged = jnp.where(live, jnp.where(first, parts[0][index], parts[1][index]), 0.0)
            grads_ref[index, :, columns] = merged.astype(jnp.bfloat16)
            if index != 1:
                row = 6 if index == 0 else 7
                rows_ref[row : row + 1, columns] = column_sum(merged)
    grad_in = jnp.zeros((seqlen, features), jnp.float32)
    for index in range(3):
        grads = grads_ref[index]
        keep_ref[index], send_ref[index] = split_columns(grads, core)
        grad_in += contract(grads, whole_weight(mine_ref, other_ref, index, core), 1, 1)
    normed, inverse = layer_norm(source_ref[...].astype(jnp.float32))
    rows_ref[0:1] = column_sum(grad_in)
    rows_ref[1:2] = column_sum(grad_in * normed)
    grad_source_ref[...] = jnp.where(
        live,
        grad_middle_ref[...] + norm_back(normed, inverse, grad_in * (1.0 + mod_ref[1:2])),
        0.0,
    )


def pair_products(
    chunk, mine_ref, left_ref, left_other_ref, right_ref, right_other_ref, keep_ref, send_ref
):
    total = contract(left_ref[0], right_ref[0], 0, 0) + contract(
        left_other_ref[0], right_other_ref[0], 0, 0
    )
    for start in range(0, total.shape[0] // 2, chunk):
        low = total[2 * start : 2 * start + chunk]
        high = total[2 * start + chunk : 2 * start + 2 * chunk]
        mine = mine_ref[0] == 1
        keep_ref[0, start : start + chunk] = jnp.where(mine, high, low)
        send_ref[0, start : start + chunk] = jnp.where(mine, low, high).astype(jnp.bfloat16)


def plain_products(left_ref, left_other_ref, right_ref, right_other_ref, out_ref):
    out_ref[0] = contract(left_ref[0], right_ref[0], 0, 0) + contract(
        left_other_ref[0], right_other_ref[0], 0, 0
    )


def struct(shape, dtype):
    return jax.ShapeDtypeStruct(shape, dtype)


VMEM = pl.BlockSpec(memory_space=pltpu.VMEM)
SMEM = pl.BlockSpec(memory_space=pltpu.SMEM)


def resident(shape):
    zeros = (0,) * len(shape)
    return pl.BlockSpec(shape, lambda step: zeros)


def run_attention_forward(place, source, modulation, offsets, attn_w, attn_w_other):
    seqlen, features = source.shape
    return pl.pallas_call(
        attention_forward,
        name="attention_forward",
        out_shape=(
            struct((3, seqlen, features), jnp.bfloat16),
            struct((3, seqlen, features), jnp.bfloat16),
            struct((seqlen, features), jnp.float32),
            struct((seqlen, features), jnp.float32),
        ),
        in_specs=[SMEM] + [VMEM] * 5,
        out_specs=(VMEM,) * 4,
        compiler_params=pltpu.CompilerParams(vmem_limit_bytes=40 << 20),
        cost_estimate=pl.CostEstimate(
            flops=8 * seqlen * features * features + 8 * HEADS * seqlen * seqlen * 128,
            bytes_accessed=attn_w.size * 4 + source.size * 20,
            transcendentals=2 * HEADS * seqlen * seqlen,
        ),
    )(place, source, modulation, offsets, attn_w, attn_w_other)


def run_mlp(place, lefts, middle, attn_out, upstream, modulation, offsets, up_ws, down_ws):
    seqlen, features = middle.shape
    steps = up_ws[0].shape[0]
    half = features // 2
    whole = (seqlen, features)
    return pl.pallas_call(
        mlp_both_ways,
        name="mlp_both_ways",
        grid=(steps,),
        out_shape=(
            struct(whole, jnp.bfloat16),
            struct((steps,) + whole, jnp.bfloat16),
            struct((steps + 1, seqlen, half), jnp.bfloat16),
            struct((steps + 1, seqlen, half), jnp.bfloat16),
            struct(whole, jnp.float32),
            struct(whole, jnp.bfloat16),
            struct(offsets.shape, jnp.float32),
        ),
        in_specs=[
            SMEM,
            pl.BlockSpec((1,) + whole, lambda step: (2, 0, 0)),
            resident(whole),
            resident(whole),
            resident(whole),
            resident(modulation.shape),
            resident(offsets.shape),
        ]
        + [pl.BlockSpec((1, features, half), lambda step: (step, 0, 0))] * 4,
        out_specs=(
            resident(whole),
            pl.BlockSpec((1,) + whole, lambda step: (step, 0, 0)),
            resident((steps + 1, seqlen, half)),
            resident((steps + 1, seqlen, half)),
            resident(whole),
            resident(whole),
            resident(offsets.shape),
        ),
        scratch_shapes=[
            pltpu.VMEM(whole, jnp.float32),
            pltpu.VMEM(whole, jnp.float32),
            pltpu.VMEM(whole, jnp.bfloat16),
        ],
        compiler_params=pltpu.CompilerParams(vmem_limit_bytes=48 << 20),
        cost_estimate=pl.CostEstimate(
            flops=8 * seqlen * features * features * steps,
            bytes_accessed=up_ws[0].size * 8 + seqlen * features * 40,
            transcendentals=seqlen * features * steps,
        ),
    )(place, lefts, middle, attn_out, upstream, modulation, offsets, *up_ws, *down_ws)


def run_attention_backward(
    place, source, modulation, attn_w, attn_w_other, qkv, grad_middle, grad_attn, rows
):
    seqlen, features = source.shape
    half = features // 2
    return pl.pallas_call(
        attention_backward,
        name="attention_backward",
        out_shape=(
            struct((seqlen, features), jnp.float32),
            struct((4, seqlen, half), jnp.bfloat16),
            struct((4, seqlen, half), jnp.bfloat16),
            struct(rows.shape, jnp.float32),
        ),
        in_specs=[SMEM] + [VMEM] * 8,
        out_specs=(VMEM,) * 4,
        scratch_shapes=[
            pltpu.VMEM((3, seqlen, features), jnp.bfloat16),
            pltpu.VMEM((seqlen, features), jnp.bfloat16),
        ],
        compiler_params=pltpu.CompilerParams(vmem_limit_bytes=40 << 20),
        cost_estimate=pl.CostEstimate(
            flops=8 * seqlen * features * features + 20 * HEADS * seqlen * seqlen * 128,
            bytes_accessed=attn_w.size * 4 + source.size * 24,
            transcendentals=2 * HEADS * seqlen * seqlen,
        ),
    )(place, source, modulation, attn_w, attn_w_other, qkv, grad_middle, grad_attn, rows)


def run_products(lefts, lefts_other, rights, rights_other, left_at, right_at, count, mine, chunk):
    _, seqlen, features = lefts.shape
    width = rights.shape[-1]
    left_spec = pl.BlockSpec((1, seqlen, features), lambda step: (left_at(step), 0, 0))
    right_spec = pl.BlockSpec((1, seqlen, width), lambda step: (right_at(step), 0, 0))
    specs = [left_spec, left_spec, right_spec, right_spec]
    cost = pl.CostEstimate(
        flops=4 * count * seqlen * features * width,
        bytes_accessed=count * features * width * 6,
        transcendentals=0,
    )
    if chunk % 16:
        total = pl.pallas_call(
            plain_products,
            name="plain_products",
            grid=(count,),
            out_shape=struct((count, features, width), jnp.float32),
            in_specs=specs,
            out_specs=pl.BlockSpec((1, features, width), lambda step: (step, 0, 0)),
            cost_estimate=cost,
        )(lefts, lefts_other, rights, rights_other)
        keep, send = split_bit(
            total.reshape(count, features // (2 * chunk), 2, chunk, width), mine, 2, jnp.bfloat16
        )
        shape = (count, features // 2, width)
        return keep.reshape(shape), send.reshape(shape)
    half_spec = pl.BlockSpec((1, features // 2, width), lambda step: (step, 0, 0))
    return pl.pallas_call(
        functools.partial(pair_products, chunk),
        name="pair_products",
        grid=(count,),
        out_shape=(
            struct((count, features // 2, width), jnp.float32),
            struct((count, features // 2, width), jnp.bfloat16),
        ),
        in_specs=[SMEM] + specs,
        out_specs=(half_spec, half_spec),
        cost_estimate=cost,
    )(mine[None], lefts, lefts_other, rights, rights_other)


def orthogonalize(block_ref, out_ref):
    values = block_ref[...].astype(jnp.float32)
    scaled = (values / (jnp.sqrt(jnp.sum(values * values)) + 1e-07)).astype(jnp.bfloat16)
    for iteration in range(NS_ITERS):
        gram = contract(scaled, scaled, 1, 1).astype(jnp.bfloat16)
        square = contract(gram, gram, 1, 0)
        mixed = (COEF_SECOND * gram.astype(jnp.float32) + COEF_THIRD * square).astype(jnp.bfloat16)
        scaled = (
            COEF_FIRST * scaled.astype(jnp.float32) + contract(mixed, scaled, 1, 0)
        ).astype(jnp.bfloat16)
    out_ref[...] = scaled


def run_orthogonalize(block):
    return pl.pallas_call(
        orthogonalize,
        name="orthogonalize",
        out_shape=struct(block.shape, block.dtype),
        in_specs=[VMEM],
        out_specs=VMEM,
        compiler_params=pltpu.CompilerParams(vmem_limit_bytes=40 << 20),
        cost_estimate=pl.CostEstimate(
            flops=6 * NS_ITERS * block.shape[0] ** 3,
            bytes_accessed=4 * block.size,
            transcendentals=0,
        ),
    )(block)


def all_to_all(values):
    return lax.all_to_all(values, "dp", split_axis=0, concat_axis=0, tiled=True)


def to_all(row):
    devices = lax.axis_size("dp")
    return all_to_all(jnp.broadcast_to(row[None], (devices,) + row.shape))


def on_device(latents, conditioning, cotangent, weights, biases, momenta, bias_momenta, counts):
    _, seqlen, features = latents.shape
    block_count, share, _ = weights.shape
    hidden_blocks = (block_count - 10) // 2
    bias_count = biases.shape[0]
    devices = lax.axis_size("dp")
    myself = lax.axis_index("dp")
    core = bit_of(myself, 0)
    bits = index_bits(devices)
    orders = colour_orders(devices)
    ranks = jnp.arange(devices, dtype=jnp.int32)
    live_here = jnp.sum(jnp.where(ranks == myself, counts, 0)) > 0

    lowered = weights.astype(jnp.bfloat16)
    ada_w = lowered[:ADA]
    condition = conditioning[0].astype(jnp.float32)
    silu_cond = jax.nn.silu(condition).astype(jnp.bfloat16)

    def conditions(_):
        return to_all(jnp.concatenate([silu_cond, biases.astype(jnp.bfloat16).reshape(-1)]))

    def partial_products(small_all):
        silu_rows = lax.dynamic_slice_in_dim(small_all[:, :features], myself * share, share, 1)
        mod_parts = product("ld,kde->lke", silu_rows, ada_w).reshape(devices, ADA * features)
        return small_all, silu_rows, mod_parts

    def modulations(carried):
        small_all, silu_rows, mod_parts = carried
        return small_all, silu_rows, all_to_all(mod_parts)

    half = features // 2
    rest = lowered[ADA:]
    columns_mine = lax.dynamic_slice_in_dim(rest, core * half, half, 2)
    columns_other = flip(lax.dynamic_slice_in_dim(rest, (1 - core) * half, half, 2), 0)
    chip_rows = jnp.where(
        core == 1,
        jnp.concatenate([columns_other, columns_mine], axis=1),
        jnp.concatenate([columns_mine, columns_other], axis=1),
    )
    bounds = [0, 10 - ADA, 10 - ADA + hidden_blocks, block_count - ADA]
    stages = bits - 1
    between = {0: lambda _: partial_products(conditions(None)), stages - 2: modulations}
    groups, (small_all, silu_rows, mod_sums) = gather_all(
        [chip_rows[low:high] for low, high in zip(bounds[:-1], bounds[1:])],
        [tuple(reversed(order)) for order in orders],
        myself,
        1,
        between,
    )
    offsets = (
        small_all[:, features:]
        .reshape(devices, bias_count, share)
        .transpose(1, 0, 2)
        .reshape(bias_count, features)
        .astype(jnp.float32)
    )
    modulation = jnp.sum(mod_sums, axis=0).reshape(ADA, features) + offsets[:ADA]
    attn_ws, up_ws, down_ws = [
        (group, flip(group, 0))
        for group in [group.reshape(-1, features, half) for group in groups]
    ]

    place = jnp.stack([core, live_here.astype(jnp.int32)]).astype(jnp.int32)
    lefts, qkv, attn_out, middle = run_attention_forward(
        place, latents[0], modulation, offsets, *attn_ws
    )
    lefts_other = flip(lefts, 0)
    output, hidden, mlp_keep, mlp_send, grad_middle, grad_attn, rows = run_mlp(
        place, lefts, middle, attn_out, cotangent[0], modulation, offsets, up_ws, down_ws
    )
    hidden_other = flip(hidden, 0)
    mlp_other = flip(mlp_send, 0)
    input_grad, attn_keep, attn_send, grad_offsets = run_attention_backward(
        place, latents[0], modulation, *attn_ws, qkv, grad_middle, grad_attn, rows
    )
    attn_other = flip(attn_send, 0)

    def spread(mats, count):
        return mats.reshape((mats.shape[0],) + (2,) * count + (2 * share, half))

    def reduced(left, left_other, right, right_other, left_at, right_at, count, order):
        keep, send = run_products(
            left,
            left_other,
            right,
            right_other,
            left_at,
            right_at,
            count,
            bit_of(myself, order[0]),
            share << order[0],
        )
        return scatter_bits(keep, send, order, myself, 1, spread)

    down_sums = reduced(
        hidden, hidden_other, mlp_keep, mlp_other, lambda b: b, lambda b: 0, hidden_blocks, orders[0]
    )
    up_sums = reduced(
        lefts, lefts_other, mlp_keep, mlp_other, lambda b: 2, lambda b: b + 1, hidden_blocks, orders[1]
    )
    attn_sums = reduced(
        lefts, lefts_other, attn_keep, attn_other, lambda b: b // 3, lambda b: b, 4, orders[2]
    )
    sums = [attn_sums, up_sums, down_sums]
    chip_rows = jnp.concatenate(sums, axis=0)
    rows_mine = lax.dynamic_slice_in_dim(chip_rows, core * share, share, 1)
    rows_other = flip(lax.dynamic_slice_in_dim(chip_rows, (1 - core) * share, share, 1), 0)
    rest_share = jnp.where(
        core == 1,
        jnp.concatenate([rows_other, rows_mine], axis=2),
        jnp.concatenate([rows_mine, rows_other], axis=2),
    )

    grad_mod_b = grad_offsets[:ADA].astype(jnp.bfloat16).reshape(-1)
    by_holder = (
        grad_offsets.reshape(bias_count, devices, share)
        .transpose(1, 0, 2)
        .reshape(devices, bias_count * share)
    )
    coarse = lax.reduce_precision(by_holder, 8, 7)
    mod_and_offsets = all_to_all(
        jnp.concatenate(
            [
                jnp.broadcast_to(grad_mod_b[None], (devices, ADA * features)),
                coarse.astype(jnp.bfloat16),
                (by_holder - coarse).astype(jnp.bfloat16),
            ],
            axis=1,
        )
    )
    mod_all = mod_and_offsets[:, : ADA * features].reshape(devices, ADA, features)
    offset_share = jnp.sum(
        mod_and_offsets[:, ADA * features :]
        .astype(jnp.float32)
        .reshape(devices * 2, bias_count, share),
        axis=0,
    )
    ada_share = product("ld,lke->kde", silu_rows, mod_all)
    silu_parts = product("lke,kde->ld", mod_all, ada_w)
    grad_silu = all_to_all(silu_parts).reshape(features)

    grad_scale = lax.rsqrt((seqlen * jnp.sum(counts)).astype(jnp.float32))
    weight_grads = jnp.concatenate([ada_share, rest_share], axis=0) * grad_scale
    bias_grads = offset_share * grad_scale
    new_momenta = BETA_WEIGHT * momenta + weight_grads
    new_bias_momenta = BETA_BIAS * bias_momenta + bias_grads
    new_biases = biases - RATE_BIAS * new_bias_momenta

    outgoing = jnp.pad(
        new_momenta.astype(jnp.bfloat16), ((0, devices - block_count), (0, 0), (0, 0))
    )
    outgoing, grad_silu = lax.optimization_barrier((outgoing, grad_silu))
    ortho = run_orthogonalize(all_to_all(outgoing).reshape(features, features))
    ortho_local = all_to_all(ortho.reshape(devices, share, features))[:block_count]
    silu_back = jax.vjp(jax.nn.silu, condition)[1]
    cond_grad = silu_back(grad_silu)[0] * seqlen ** (-0.5)
    new_weights = weights - RATE_WEIGHT * ortho_local.astype(jnp.float32)
    cond_grad = jnp.where(live_here, cond_grad, jnp.zeros_like(cond_grad))[None]
    return (
        output[None],
        input_grad[None],
        cond_grad,
        weight_grads,
        bias_grads,
        new_weights,
        new_momenta,
        new_biases,
        new_bias_momenta,
    )


def solution(mesh):
    return jax.shard_map(
        on_device,
        mesh=mesh,
        in_specs=(
            P("dp", None, None),
            P("dp", None),
            P("dp", None, None),
            P(None, "dp", None),
            P(None, "dp"),
            P(None, "dp", None),
            P(None, "dp"),
            P(),
        ),
        out_specs=(
            P("dp", None, None),
            P("dp", None, None),
            P("dp", None),
            P(None, "dp", None),
            P(None, "dp"),
            P(None, "dp", None),
            P(None, "dp", None),
            P(None, "dp"),
            P(None, "dp"),
        ),
        check_vma=False,
    )
```

```python
import functools

import jax
import jax.numpy as jnp
from jax import lax
from jax.experimental import pallas as pl
from jax.experimental.pallas import tpu as pltpu
from jax.sharding import PartitionSpec as P

HEADS = 12
NS_ITERS = 2
ADA = 6
COLOURS = 3

COEF_FIRST = 3.4445
COEF_SECOND = -4.775
COEF_THIRD = 2.0315
BETA_WEIGHT = 0.95
BETA_BIAS = 0.9
RATE_WEIGHT = 1.0
RATE_BIAS = 0.1
NORM_EPS = 1e-06


def product(spec, left, right):
    return jnp.einsum(spec, left, right, preferred_element_type=jnp.float32)


def flip(values, bit):
    devices = lax.axis_size("dp")
    return lax.ppermute(values, "dp", [(i, i ^ (1 << bit)) for i in range(devices)])


def bit_of(myself, bit):
    return (myself >> bit) & 1


def joined(values, other, taken, axis):
    return jnp.where(
        taken == 1, jnp.stack([other, values], axis), jnp.stack([values, other], axis)
    )


def gather_all(groups, orders, myself, axis, between):
    have = [[] for _ in groups]
    carried = None
    for stage in range(len(orders[0])):
        others = [flip(group, order[stage]) for group, order in zip(groups, orders)]
        if stage in between:
            carried = between[stage](carried)
            others, carried = lax.optimization_barrier((others, carried))
        else:
            others = lax.optimization_barrier(others)
        for index, order in enumerate(orders):
            bit = order[stage]
            position = axis + sum(1 for held in have[index] if held > bit)
            groups[index] = joined(groups[index], others[index], bit_of(myself, bit), position)
            have[index].append(bit)
    return groups, carried


def split_bit(values, mine, position, sent_as):
    send = lax.dynamic_index_in_dim(values, 1 - mine, position, keepdims=False)
    keep = lax.dynamic_index_in_dim(values, mine, position, keepdims=False)
    return keep, send.astype(sent_as)


def scatter_all(halves, orders, myself, axis, spread, between):
    left = [sorted(order, reverse=True) for order in orders]
    carried = None
    totals = []
    for stage in range(len(orders[0])):
        others = [flip(send, order[stage]) for (_, send), order in zip(halves, orders)]
        if stage in between:
            carried = between[stage](carried)
            others, carried = lax.optimization_barrier((others, carried))
        totals = [
            keep + other.astype(jnp.float32) for (keep, _), other in zip(halves, others)
        ]
        for index, order in enumerate(orders):
            left[index].remove(order[stage])
            if stage == 0:
                totals[index] = spread(totals[index], len(left[index]))
            if left[index]:
                bit = order[stage + 1]
                position = axis + left[index].index(bit)
                halves[index] = split_bit(
                    totals[index], bit_of(myself, bit), position, jnp.bfloat16
                )
    return totals, carried


def index_bits(devices):
    return devices.bit_length() - 1


def colour_orders(devices):
    chip_bits = list(range(1, index_bits(devices)))
    rest, last = chip_bits[:-1], chip_bits[-1:]
    shifts = [(colour * len(rest)) // COLOURS for colour in range(COLOURS)]
    return [tuple(rest[shift:] + rest[:shift] + last) for shift in shifts]


def contract(left, right, left_dim, right_dim):
    return lax.dot_general(
        left, right, (((left_dim,), (right_dim,)), ((), ())), preferred_element_type=jnp.float32
    )


def layer_norm(stream):
    centred = stream - jnp.mean(stream, axis=-1, keepdims=True)
    inverse = lax.rsqrt(jnp.mean(centred * centred, axis=-1, keepdims=True) + NORM_EPS)
    return (centred * inverse, inverse)


def norm_back(normed, inverse, upstream):
    return inverse * (
        upstream
        - jnp.mean(upstream, axis=-1, keepdims=True)
        - normed * jnp.mean(upstream * normed, axis=-1, keepdims=True)
    )


def column_sum(values):
    return jnp.sum(values, axis=0, keepdims=True)


def scores_of(query, keys, width):
    return contract(query, keys, 1, 1) * width ** (-0.5)


def whole_weight(mine_ref, other_ref, index, core):
    mine, other = mine_ref[index], other_ref[index]
    return jnp.concatenate(
        [jnp.where(core == 1, other, mine), jnp.where(core == 1, mine, other)], axis=1
    )


def attention_forward(
    place_ref,
    source_ref,
    mod_ref,
    offsets_ref,
    mine_ref,
    other_ref,
    lefts_ref,
    qkv_ref,
    attn_ref,
    middle_ref,
):
    core = place_ref[0]
    seqlen, features = source_ref.shape
    width = features // HEADS
    stream = source_ref[...].astype(jnp.float32)
    normed, _ = layer_norm(stream)
    attn_input = (normed * (1.0 + mod_ref[1:2]) + mod_ref[0:1]).astype(jnp.bfloat16)
    lefts_ref[0] = attn_input
    qkv_ref[0] = (contract(attn_input, whole_weight(mine_ref, other_ref, 0, core), 1, 0) + offsets_ref[6:7]).astype(
        jnp.bfloat16
    )
    qkv_ref[1] = contract(attn_input, whole_weight(mine_ref, other_ref, 1, core), 1, 0).astype(jnp.bfloat16)
    qkv_ref[2] = (contract(attn_input, whole_weight(mine_ref, other_ref, 2, core), 1, 0) + offsets_ref[7:8]).astype(
        jnp.bfloat16
    )
    first = lax.broadcasted_iota(jnp.int32, (seqlen, 2 * width), 1) < width
    for pair in range(HEADS // 2):
        columns = slice(2 * width * pair, 2 * width * (pair + 1))
        query, keys, values = qkv_ref[0, :, columns], qkv_ref[1, :, columns], qkv_ref[2, :, columns]
        halves = []
        for mask in (first, jnp.logical_not(first)):
            scores = scores_of(jnp.where(mask, query, jnp.zeros_like(query)), keys, width)
            log_total = jnp.log(jnp.sum(jnp.exp(scores), axis=-1, keepdims=True))
            probs = jnp.exp(scores - log_total).astype(jnp.bfloat16)
            halves.append(contract(probs, values, 1, 0))
        lefts_ref[1, :, columns] = jnp.where(first, *halves).astype(jnp.bfloat16)
    attn_out = contract(lefts_ref[1], whole_weight(mine_ref, other_ref, 3, core), 1, 0) + offsets_ref[8:9]
    attn_ref[...] = attn_out
    middle = stream + mod_ref[2:3] * attn_out
    middle_ref[...] = middle
    normed_two, _ = layer_norm(middle)
    lefts_ref[2] = (normed_two * (1.0 + mod_ref[4:5]) + mod_ref[3:4]).astype(jnp.bfloat16)


def split_columns(values, core):
    width = values.shape[-1] // 2
    low, high = values[:, :width], values[:, width:]
    return (jnp.where(core == 1, high, low), jnp.where(core == 1, low, high))


def mlp_both_ways(
    place_ref,
    lefts_ref,
    middle_ref,
    attn_ref,
    upstream_ref,
    mod_ref,
    offsets_ref,
    up_ref,
    up_other_ref,
    down_ref,
    down_other_ref,
    output_ref,
    hidden_ref,
    keep_ref,
    send_ref,
    grad_middle_ref,
    grad_attn_ref,
    rows_ref,
    total_ref,
    grad_total_ref,
    grad_mlp_ref,
):
    step = pl.program_id(0)
    last = pl.num_programs(0) - 1
    core, live = place_ref[0], place_ref[1] > 0
    scale = 0.7978845608028654

    @pl.when(step == 0)
    def _():
        total_ref[...] = jnp.zeros_like(total_ref)
        grad_total_ref[...] = jnp.zeros_like(grad_total_ref)
        grad_mlp = jnp.where(live, upstream_ref[...].astype(jnp.float32) * mod_ref[5:6], 0.0)
        grad_mlp_b = grad_mlp.astype(jnp.bfloat16)
        grad_mlp_ref[...] = grad_mlp_b
        keep_ref[0], send_ref[0] = split_columns(grad_mlp_b, core)
        rows_ref[...] = jnp.zeros_like(rows_ref)
        rows_ref[pl.ds(10 + last, 1)] = column_sum(grad_mlp)

    up_w = whole_weight(up_ref, up_other_ref, 0, core)
    down_w = whole_weight(down_ref, down_other_ref, 0, core)
    before = contract(lefts_ref[0], up_w, 1, 0) + offsets_ref[pl.ds(9 + step, 1)]
    square = before * before
    bend = jnp.tanh(scale * (before + 0.044715 * square * before))
    hidden = (0.5 * before * (1.0 + bend)).astype(jnp.bfloat16)
    hidden_ref[0] = hidden
    total_ref[...] += contract(hidden, down_w, 1, 0)
    slope = 0.5 * (1.0 + bend) + 0.5 * before * (1.0 - bend * bend) * scale * (
        1.0 + 3.0 * 0.044715 * square
    )
    grad_pre = jnp.where(live, contract(grad_mlp_ref[...], down_w, 1, 1) * slope, 0.0)
    grad_pre_b = grad_pre.astype(jnp.bfloat16)
    keep_ref[step + 1], send_ref[step + 1] = split_columns(grad_pre_b, core)
    rows_ref[pl.ds(9 + step, 1)] = column_sum(grad_pre)
    grad_total_ref[...] += contract(grad_pre_b, up_w, 1, 1)

    @pl.when(step == last)
    def _():
        middle = middle_ref[...]
        grad_out = upstream_ref[...].astype(jnp.float32)
        mlp_out = total_ref[...] + offsets_ref[pl.ds(10 + last, 1)]
        output = middle + mod_ref[5:6] * mlp_out
        output_ref[...] = jnp.where(live, output, 0.0).astype(jnp.bfloat16)
        rows_ref[5:6] = jnp.where(live, column_sum(grad_out * mlp_out), 0.0)
        normed, inverse = layer_norm(middle)
        grad_in = grad_total_ref[...]
        rows_ref[3:4] = column_sum(grad_in)
        rows_ref[4:5] = column_sum(grad_in * normed)
        grad_middle = grad_out + norm_back(normed, inverse, grad_in * (1.0 + mod_ref[4:5]))
        grad_middle = jnp.where(live, grad_middle, 0.0)
        grad_middle_ref[...] = grad_middle
        rows_ref[2:3] = column_sum(grad_middle * attn_ref[...])
        grad_attn = grad_middle * mod_ref[2:3]
        grad_attn_ref[...] = grad_attn.astype(jnp.bfloat16)
        rows_ref[8:9] = column_sum(grad_attn)


def attention_backward(
    place_ref,
    source_ref,
    mod_ref,
    mine_ref,
    other_ref,
    qkv_ref,
    grad_middle_ref,
    grad_attn_ref,
    rows_in_ref,
    grad_source_ref,
    keep_ref,
    send_ref,
    rows_ref,
    grads_ref,
    context_ref,
):
    seqlen, features = source_ref.shape
    width = features // HEADS
    core, live = place_ref[0], place_ref[1] > 0
    rows_ref[...] = rows_in_ref[...]
    grad_attn = grad_attn_ref[...]
    keep_ref[3], send_ref[3] = split_columns(grad_attn, core)
    context_ref[...] = contract(
        grad_attn, whole_weight(mine_ref, other_ref, 3, core), 1, 1
    ).astype(jnp.bfloat16)
    first = lax.broadcasted_iota(jnp.int32, (seqlen, 2 * width), 1) < width
    for pair in range(HEADS // 2):
        columns = slice(2 * width * pair, 2 * width * (pair + 1))
        query, keys, values = qkv_ref[0, :, columns], qkv_ref[1, :, columns], qkv_ref[2, :, columns]
        upstream = context_ref[:, columns]
        parts = []
        for mask in (first, jnp.logical_not(first)):
            scores = scores_of(jnp.where(mask, query, jnp.zeros_like(query)), keys, width)
            log_total = jnp.log(jnp.sum(jnp.exp(scores), axis=-1, keepdims=True))
            probs = jnp.exp(scores - log_total)
            grad_values = contract(probs.astype(jnp.bfloat16), upstream, 0, 0)
            grad_probs = contract(
                jnp.where(mask, upstream, jnp.zeros_like(upstream)), values, 1, 1
            )
            row_dot = jnp.sum(probs * grad_probs, axis=-1, keepdims=True)
            grad_scores = (probs * (grad_probs - row_dot) * width ** (-0.5)).astype(jnp.bfloat16)
            parts.append(
                (
                    contract(grad_scores, keys, 1, 0),
                    contract(grad_scores, query, 0, 0),
                    grad_values,
                )
            )
        for index in range(3):
            merged = jnp.where(live, jnp.where(first, parts[0][index], parts[1][index]), 0.0)
            grads_ref[index, :, columns] = merged.astype(jnp.bfloat16)
            if index != 1:
                row = 6 if index == 0 else 7
                rows_ref[row : row + 1, columns] = column_sum(merged)
    grad_in = jnp.zeros((seqlen, features), jnp.float32)
    for index in range(3):
        grads = grads_ref[index]
        keep_ref[index], send_ref[index] = split_columns(grads, core)
        grad_in += contract(grads, whole_weight(mine_ref, other_ref, index, core), 1, 1)
    normed, inverse = layer_norm(source_ref[...].astype(jnp.float32))
    rows_ref[0:1] = column_sum(grad_in)
    rows_ref[1:2] = column_sum(grad_in * normed)
    grad_source_ref[...] = jnp.where(
        live,
        grad_middle_ref[...] + norm_back(normed, inverse, grad_in * (1.0 + mod_ref[1:2])),
        0.0,
    )


def pair_products(
    chunk, mine_ref, left_ref, left_other_ref, right_ref, right_other_ref, keep_ref, send_ref
):
    total = contract(left_ref[0], right_ref[0], 0, 0) + contract(
        left_other_ref[0], right_other_ref[0], 0, 0
    )
    for start in range(0, total.shape[0] // 2, chunk):
        low = total[2 * start : 2 * start + chunk]
        high = total[2 * start + chunk : 2 * start + 2 * chunk]
        mine = mine_ref[0] == 1
        keep_ref[0, start : start + chunk] = jnp.where(mine, high, low)
        send_ref[0, start : start + chunk] = jnp.where(mine, low, high).astype(jnp.bfloat16)


def plain_products(left_ref, left_other_ref, right_ref, right_other_ref, out_ref):
    out_ref[0] = contract(left_ref[0], right_ref[0], 0, 0) + contract(
        left_other_ref[0], right_other_ref[0], 0, 0
    )


def struct(shape, dtype):
    return jax.ShapeDtypeStruct(shape, dtype)


VMEM = pl.BlockSpec(memory_space=pltpu.VMEM)
SMEM = pl.BlockSpec(memory_space=pltpu.SMEM)


def resident(shape):
    zeros = (0,) * len(shape)
    return pl.BlockSpec(shape, lambda step: zeros)


def run_attention_forward(place, source, modulation, offsets, attn_w, attn_w_other):
    seqlen, features = source.shape
    return pl.pallas_call(
        attention_forward,
        name="attention_forward",
        out_shape=(
            struct((3, seqlen, features), jnp.bfloat16),
            struct((3, seqlen, features), jnp.bfloat16),
            struct((seqlen, features), jnp.float32),
            struct((seqlen, features), jnp.float32),
        ),
        in_specs=[SMEM] + [VMEM] * 5,
        out_specs=(VMEM,) * 4,
        compiler_params=pltpu.CompilerParams(vmem_limit_bytes=40 << 20),
        cost_estimate=pl.CostEstimate(
            flops=8 * seqlen * features * features + 8 * HEADS * seqlen * seqlen * 128,
            bytes_accessed=attn_w.size * 4 + source.size * 20,
            transcendentals=2 * HEADS * seqlen * seqlen,
        ),
    )(place, source, modulation, offsets, attn_w, attn_w_other)


def run_mlp(place, lefts, middle, attn_out, upstream, modulation, offsets, up_ws, down_ws):
    seqlen, features = middle.shape
    steps = up_ws[0].shape[0]
    half = features // 2
    whole = (seqlen, features)
    return pl.pallas_call(
        mlp_both_ways,
        name="mlp_both_ways",
        grid=(steps,),
        out_shape=(
            struct(whole, jnp.bfloat16),
            struct((steps,) + whole, jnp.bfloat16),
            struct((steps + 1, seqlen, half), jnp.bfloat16),
            struct((steps + 1, seqlen, half), jnp.bfloat16),
            struct(whole, jnp.float32),
            struct(whole, jnp.bfloat16),
            struct(offsets.shape, jnp.float32),
        ),
        in_specs=[
            SMEM,
            pl.BlockSpec((1,) + whole, lambda step: (2, 0, 0)),
            resident(whole),
            resident(whole),
            resident(whole),
            resident(modulation.shape),
            resident(offsets.shape),
        ]
        + [pl.BlockSpec((1, features, half), lambda step: (step, 0, 0))] * 4,
        out_specs=(
            resident(whole),
            pl.BlockSpec((1,) + whole, lambda step: (step, 0, 0)),
            resident((steps + 1, seqlen, half)),
            resident((steps + 1, seqlen, half)),
            resident(whole),
            resident(whole),
            resident(offsets.shape),
        ),
        scratch_shapes=[
            pltpu.VMEM(whole, jnp.float32),
            pltpu.VMEM(whole, jnp.float32),
            pltpu.VMEM(whole, jnp.bfloat16),
        ],
        compiler_params=pltpu.CompilerParams(vmem_limit_bytes=48 << 20),
        cost_estimate=pl.CostEstimate(
            flops=8 * seqlen * features * features * steps,
            bytes_accessed=up_ws[0].size * 8 + seqlen * features * 40,
            transcendentals=seqlen * features * steps,
        ),
    )(place, lefts, middle, attn_out, upstream, modulation, offsets, *up_ws, *down_ws)


def run_attention_backward(
    place, source, modulation, attn_w, attn_w_other, qkv, grad_middle, grad_attn, rows
):
    seqlen, features = source.shape
    half = features // 2
    return pl.pallas_call(
        attention_backward,
        name="attention_backward",
        out_shape=(
            struct((seqlen, features), jnp.float32),
            struct((4, seqlen, half), jnp.bfloat16),
            struct((4, seqlen, half), jnp.bfloat16),
            struct(rows.shape, jnp.float32),
        ),
        in_specs=[SMEM] + [VMEM] * 8,
        out_specs=(VMEM,) * 4,
        scratch_shapes=[
            pltpu.VMEM((3, seqlen, features), jnp.bfloat16),
            pltpu.VMEM((seqlen, features), jnp.bfloat16),
        ],
        compiler_params=pltpu.CompilerParams(vmem_limit_bytes=40 << 20),
        cost_estimate=pl.CostEstimate(
            flops=8 * seqlen * features * features + 20 * HEADS * seqlen * seqlen * 128,
            bytes_accessed=attn_w.size * 4 + source.size * 24,
            transcendentals=2 * HEADS * seqlen * seqlen,
        ),
    )(place, source, modulation, attn_w, attn_w_other, qkv, grad_middle, grad_attn, rows)


def run_products(lefts, lefts_other, rights, rights_other, left_at, right_at, count, mine, chunk):
    _, seqlen, features = lefts.shape
    width = rights.shape[-1]
    left_spec = pl.BlockSpec((1, seqlen, features), lambda step: (left_at(step), 0, 0))
    right_spec = pl.BlockSpec((1, seqlen, width), lambda step: (right_at(step), 0, 0))
    specs = [left_spec, left_spec, right_spec, right_spec]
    cost = pl.CostEstimate(
        flops=4 * count * seqlen * features * width,
        bytes_accessed=count * features * width * 6,
        transcendentals=0,
    )
    if chunk % 16:
        total = pl.pallas_call(
            plain_products,
            name="plain_products",
            grid=(count,),
            out_shape=struct((count, features, width), jnp.float32),
            in_specs=specs,
            out_specs=pl.BlockSpec((1, features, width), lambda step: (step, 0, 0)),
            cost_estimate=cost,
        )(lefts, lefts_other, rights, rights_other)
        keep, send = split_bit(
            total.reshape(count, features // (2 * chunk), 2, chunk, width), mine, 2, jnp.bfloat16
        )
        shape = (count, features // 2, width)
        return keep.reshape(shape), send.reshape(shape)
    half_spec = pl.BlockSpec((1, features // 2, width), lambda step: (step, 0, 0))
    return pl.pallas_call(
        functools.partial(pair_products, chunk),
        name="pair_products",
        grid=(count,),
        out_shape=(
            struct((count, features // 2, width), jnp.float32),
            struct((count, features // 2, width), jnp.bfloat16),
        ),
        in_specs=[SMEM] + specs,
        out_specs=(half_spec, half_spec),
        cost_estimate=cost,
    )(mine[None], lefts, lefts_other, rights, rights_other)


def muon_steps(block):
    values = block.astype(jnp.float32)
    scaled = (values / (jnp.sqrt(jnp.sum(values * values)) + 1e-07)).astype(jnp.bfloat16)
    for iteration in range(NS_ITERS):
        gram = contract(scaled, scaled, 1, 1).astype(jnp.bfloat16)
        square = contract(gram, gram, 1, 0)
        mixed = (COEF_SECOND * gram.astype(jnp.float32) + COEF_THIRD * square).astype(jnp.bfloat16)
        scaled = (
            COEF_FIRST * scaled.astype(jnp.float32) + contract(mixed, scaled, 1, 0)
        ).astype(jnp.bfloat16)
    return scaled


def orthogonalize_halves(place_ref, mine_ref, other_ref, out_ref):
    core = place_ref[0]
    scaled = muon_steps(whole_weight(mine_ref, other_ref, slice(None), core))
    out_ref[...] = split_columns(scaled, core)[0]


def orthogonalize_whole(block_ref, out_ref):
    out_ref[0] = muon_steps(block_ref[0])


def muon_cost(count, rows):
    return pl.CostEstimate(
        flops=6 * count * NS_ITERS * rows**3, bytes_accessed=4 * count * rows**2, transcendentals=0
    )


def run_orthogonalize_halves(place, mine, other):
    return pl.pallas_call(
        orthogonalize_halves,
        name="orthogonalize_halves",
        out_shape=struct(mine.shape, mine.dtype),
        in_specs=[SMEM, VMEM, VMEM],
        out_specs=VMEM,
        compiler_params=pltpu.CompilerParams(vmem_limit_bytes=40 << 20),
        cost_estimate=muon_cost(1, mine.shape[0]),
    )(place, mine, other)


def run_orthogonalize_whole(blocks):
    spec = pl.BlockSpec((1,) + blocks.shape[1:], lambda step: (step, 0, 0))
    return pl.pallas_call(
        orthogonalize_whole,
        name="orthogonalize_whole",
        grid=(blocks.shape[0],),
        out_shape=struct(blocks.shape, blocks.dtype),
        in_specs=[spec],
        out_specs=spec,
        compiler_params=pltpu.CompilerParams(vmem_limit_bytes=40 << 20),
        cost_estimate=muon_cost(*blocks.shape[:2]),
    )(blocks)


def all_to_all(values):
    return lax.all_to_all(values, "dp", split_axis=0, concat_axis=0, tiled=True)


def to_all(row):
    devices = lax.axis_size("dp")
    return all_to_all(jnp.broadcast_to(row[None], (devices,) + row.shape))


def on_device(latents, conditioning, cotangent, weights, biases, momenta, bias_momenta, counts):
    _, seqlen, features = latents.shape
    block_count, share, _ = weights.shape
    hidden_blocks = (block_count - 10) // 2
    bias_count = biases.shape[0]
    devices = lax.axis_size("dp")
    myself = lax.axis_index("dp")
    core = bit_of(myself, 0)
    bits = index_bits(devices)
    orders = colour_orders(devices)
    ranks = jnp.arange(devices, dtype=jnp.int32)
    live_here = jnp.sum(jnp.where(ranks == myself, counts, 0)) > 0

    lowered = weights.astype(jnp.bfloat16)
    ada_w = lowered[:ADA]
    condition = conditioning[0].astype(jnp.float32)
    silu_cond = jax.nn.silu(condition).astype(jnp.bfloat16)

    half = features // 2
    rest = lowered[ADA:]
    columns_mine = lax.dynamic_slice_in_dim(rest, core * half, half, 2)
    columns_other = flip(lax.dynamic_slice_in_dim(rest, (1 - core) * half, half, 2), 0)
    chip_rows = jnp.where(
        core == 1,
        jnp.concatenate([columns_other, columns_mine], axis=1),
        jnp.concatenate([columns_mine, columns_other], axis=1),
    )
    bounds = [0, 10 - ADA, 10 - ADA + hidden_blocks, block_count - ADA]
    stages = bits - 1
    conditions = jnp.concatenate([silu_cond, biases.astype(jnp.bfloat16).reshape(-1)])
    chip_rows, conditions = lax.optimization_barrier((chip_rows, conditions))

    def partial_products(small_all):
        silu_rows = lax.dynamic_slice_in_dim(small_all[:, :features], myself * share, share, 1)
        mod_parts = product("ld,kde->lke", silu_rows, ada_w).reshape(devices, ADA * features)
        return small_all, silu_rows, mod_parts

    def modulations(carried):
        small_all, silu_rows, mod_parts = carried
        return small_all, silu_rows, all_to_all(mod_parts)

    between = {0: lambda _: to_all(conditions), 1: partial_products, stages - 1: modulations}
    groups, (small_all, silu_rows, mod_sums) = gather_all(
        [chip_rows[low:high] for low, high in zip(bounds[:-1], bounds[1:])],
        [tuple(reversed(order)) for order in orders],
        myself,
        1,
        between,
    )
    offsets = (
        small_all[:, features:]
        .reshape(devices, bias_count, share)
        .transpose(1, 0, 2)
        .reshape(bias_count, features)
        .astype(jnp.float32)
    )
    modulation = jnp.sum(mod_sums, axis=0).reshape(ADA, features) + offsets[:ADA]
    attn_ws, up_ws, down_ws = [
        (group, flip(group, 0))
        for group in [group.reshape(-1, features, half) for group in groups]
    ]

    place = jnp.stack([core, live_here.astype(jnp.int32)]).astype(jnp.int32)
    lefts, qkv, attn_out, middle = run_attention_forward(
        place, latents[0], modulation, offsets, *attn_ws
    )
    lefts_other = flip(lefts, 0)
    output, hidden, mlp_keep, mlp_send, grad_middle, grad_attn, rows = run_mlp(
        place, lefts, middle, attn_out, cotangent[0], modulation, offsets, up_ws, down_ws
    )
    hidden_other = flip(hidden, 0)
    mlp_other = flip(mlp_send, 0)
    def spread(mats, count):
        return mats.reshape((mats.shape[0],) + (2,) * count + (2 * share, half))

    def products(left, left_other, right, right_other, left_at, right_at, count, order):
        return run_products(
            left,
            left_other,
            right,
            right_other,
            left_at,
            right_at,
            count,
            bit_of(myself, order[0]),
            share << order[0],
        )

    down_halves = products(
        hidden, hidden_other, mlp_keep, mlp_other, lambda b: b, lambda b: 0, hidden_blocks, orders[0]
    )
    up_halves = products(
        lefts, lefts_other, mlp_keep, mlp_other, lambda b: 2, lambda b: b + 1, hidden_blocks, orders[1]
    )
    down_halves, up_halves, grad_attn = lax.optimization_barrier(
        (down_halves, up_halves, grad_attn)
    )
    input_grad, attn_keep, attn_send, grad_offsets = run_attention_backward(
        place, latents[0], modulation, *attn_ws, qkv, grad_middle, grad_attn, rows
    )
    attn_other = flip(attn_send, 0)
    attn_halves = products(
        lefts, lefts_other, attn_keep, attn_other, lambda b: b // 3, lambda b: b, 4, orders[2]
    )

    grad_mod_b = grad_offsets[:ADA].astype(jnp.bfloat16).reshape(-1)
    by_holder = (
        grad_offsets.reshape(bias_count, devices, share)
        .transpose(1, 0, 2)
        .reshape(devices, bias_count * share)
    )
    coarse = lax.reduce_precision(by_holder, 8, 7)
    mod_and_offsets = jnp.concatenate(
        [
            jnp.broadcast_to(grad_mod_b[None], (devices, ADA * features)),
            coarse.astype(jnp.bfloat16),
            (by_holder - coarse).astype(jnp.bfloat16),
        ],
        axis=1,
    )

    chips = devices // 2
    extra = max(0, block_count - chips)
    assert extra % 2 == 0 and extra <= ADA
    main = block_count - extra
    grad_scale = lax.rsqrt((seqlen * jnp.sum(counts)).astype(jnp.float32))
    early_bits = list(reversed(range(1, bits)))

    def gather_early(early_rows, low, high):
        for bit in early_bits[low:high]:
            position = 1 + sum(1 for held in early_bits[: early_bits.index(bit)] if held > bit)
            early_rows = joined(early_rows, flip(early_rows, bit), bit_of(myself, bit), position)
        return early_rows

    def start_early(mod_and_offsets):
        mod_all = mod_and_offsets[:, : ADA * features].reshape(devices, ADA, features)
        ada_share = product("ld,lke->kde", silu_rows, mod_all)
        if not extra:
            return mod_and_offsets, mod_all, ada_share, ()
        early = BETA_WEIGHT * momenta[:extra] + ada_share[:extra] * grad_scale
        early = early.astype(jnp.bfloat16).reshape(2, extra // 2, share, features)
        early_mine = lax.dynamic_index_in_dim(early, core, 0, keepdims=False)
        early_other = flip(lax.dynamic_index_in_dim(early, 1 - core, 0, keepdims=False), 0)
        early_rows = joined(early_mine, early_other, core, 1)
        early_rows = early_rows.reshape(extra // 2, 2 * share, features)
        return mod_and_offsets, mod_all, ada_share, gather_early(early_rows, 0, 1)

    def conditioning_grads(carried):
        mod_and_offsets, mod_all, ada_share, early_rows = carried
        grad_silu = all_to_all(product("lke,kde->ld", mod_all, ada_w))
        if extra:
            early_rows = gather_early(early_rows, 1, 3)
        return mod_and_offsets, ada_share, early_rows, grad_silu

    sums, (mod_and_offsets, ada_share, early_rows, grad_silu) = scatter_all(
        [attn_halves, up_halves, down_halves],
        [orders[2], orders[1], orders[0]],
        myself,
        1,
        spread,
        {1: lambda _: all_to_all(mod_and_offsets), 2: start_early, stages - 1: conditioning_grads},
    )
    chip_rows = jnp.concatenate(sums, axis=0)
    rows_mine = lax.dynamic_slice_in_dim(chip_rows, core * share, share, 1)
    rows_other = flip(lax.dynamic_slice_in_dim(chip_rows, (1 - core) * share, share, 1), 0)
    rest_share = jnp.where(
        core == 1,
        jnp.concatenate([rows_other, rows_mine], axis=2),
        jnp.concatenate([rows_mine, rows_other], axis=2),
    )

    offset_share = jnp.sum(
        mod_and_offsets[:, ADA * features :]
        .astype(jnp.float32)
        .reshape(devices * 2, bias_count, share),
        axis=0,
    )

    weight_grads = jnp.concatenate([ada_share, rest_share], axis=0) * grad_scale
    bias_grads = offset_share * grad_scale
    new_momenta = BETA_WEIGHT * momenta + weight_grads
    new_bias_momenta = BETA_BIAS * bias_momenta + bias_grads
    new_biases = biases - RATE_BIAS * new_bias_momenta

    lowered_momenta = new_momenta.astype(jnp.bfloat16)
    outgoing = (
        lowered_momenta[extra:]
        .reshape(main, share, 2, half)
        .transpose(0, 2, 1, 3)
        .reshape(2 * main, share, half)
    )
    outgoing = jnp.pad(outgoing, ((0, devices - 2 * main), (0, 0), (0, 0)))
    columns_mine = all_to_all(outgoing).reshape(features, half)
    ortho_half = run_orthogonalize_halves(place, columns_mine, flip(columns_mine, 0))
    ortho_local = (
        all_to_all(ortho_half.reshape(devices, share, half))[: 2 * main]
        .reshape(main, 2, share, half)
        .transpose(0, 2, 1, 3)
        .reshape(main, share, features)
    )
    if extra:
        early_rows = gather_early(early_rows, 3, len(early_bits))
        early_ortho = run_orthogonalize_whole(early_rows.reshape(extra // 2, features, features))
        chip_ortho = lax.dynamic_slice_in_dim(
            early_ortho, (myself - core) * share, 2 * share, 1
        ).reshape(extra // 2, 2, share, features)
        ortho_mine = lax.dynamic_index_in_dim(chip_ortho, core, 1, keepdims=False)
        ortho_other = flip(
            lax.dynamic_index_in_dim(chip_ortho, 1 - core, 1, keepdims=False), 0
        )
        early_local = joined(ortho_mine, ortho_other, core, 0).reshape(extra, share, features)
        ortho_local = jnp.concatenate([early_local, ortho_local])
    silu_back = jax.vjp(jax.nn.silu, condition)[1]
    cond_grad = silu_back(grad_silu.reshape(features))[0] * seqlen ** (-0.5)
    new_weights = weights - RATE_WEIGHT * ortho_local.astype(jnp.float32)
    cond_grad = jnp.where(live_here, cond_grad, jnp.zeros_like(cond_grad))[None]
    return (
        output[None],
        input_grad[None],
        cond_grad,
        weight_grads,
        bias_grads,
        new_weights,
        new_momenta,
        new_biases,
        new_bias_momenta,
    )


def solution(mesh):
    return jax.shard_map(
        on_device,
        mesh=mesh,
        in_specs=(
            P("dp", None, None),
            P("dp", None),
            P("dp", None, None),
            P(None, "dp", None),
            P(None, "dp"),
            P(None, "dp", None),
            P(None, "dp"),
            P(),
        ),
        out_specs=(
            P("dp", None, None),
            P("dp", None, None),
            P("dp", None),
            P(None, "dp", None),
            P(None, "dp"),
            P(None, "dp", None),
            P(None, "dp", None),
            P(None, "dp"),
            P(None, "dp"),
        ),
        check_vma=False,
    )
```

```python
import functools

import jax
import jax.numpy as jnp
from jax import lax
from jax.experimental import pallas as pl
from jax.experimental.pallas import tpu as pltpu
from jax.sharding import PartitionSpec as P


HEADS = 12
NS_ITERS = 2
ADA = 6
COLOURS = 3

COEF_FIRST = 3.4445
COEF_SECOND = -4.775
COEF_THIRD = 2.0315
BETA_WEIGHT = 0.95
BETA_BIAS = 0.9
RATE_WEIGHT = 1.0
RATE_BIAS = 0.1
NORM_EPS = 1e-06


def product(spec, left, right):
    return jnp.einsum(spec, left, right, preferred_element_type=jnp.float32)


def flip(values, bit):
    devices = lax.axis_size("dp")
    return lax.ppermute(values, "dp", [(i, i ^ (1 << bit)) for i in range(devices)])


def bit_of(myself, bit):
    return (myself >> bit) & 1


def joined(values, other, taken, axis):
    return jnp.where(
        taken == 1, jnp.stack([other, values], axis), jnp.stack([values, other], axis)
    )


def gather_all(groups, orders, myself, axis, between):
    have = [[] for _ in groups]
    carried = None
    for stage in range(len(orders[0])):
        others = [flip(group, order[stage]) for group, order in zip(groups, orders)]
        if stage in between:
            carried = between[stage](carried)
            others, carried = lax.optimization_barrier((others, carried))
        else:
            others = lax.optimization_barrier(others)
        for index, order in enumerate(orders):
            bit = order[stage]
            position = axis + sum(1 for held in have[index] if held > bit)
            groups[index] = joined(groups[index], others[index], bit_of(myself, bit), position)
            have[index].append(bit)
    return groups, carried


def gather_step(values, order, bit, myself):
    held = order[: order.index(bit)]
    position = 1 + sum(1 for before in held if before > bit)
    return joined(values, flip(values, bit), bit_of(myself, bit), position)


def flip_by_core(values, first_bit, second_bit):
    devices = lax.axis_size("dp")
    return lax.ppermute(
        values, "dp", [(i, i ^ (1 << (second_bit if i & 1 else first_bit))) for i in range(devices)]
    )


def corner_rows(near, far, order, myself):
    high, low = bit_of(myself, order[-2]), bit_of(myself, order[-1])
    core = bit_of(myself, 0)
    first, second = jnp.where(core == 1, low, high), jnp.where(core == 1, high, low)
    axis = len(order) - 1
    pairs = [
        joined(pair[0], pair[1], first, axis) for pair in (near, far)
    ]
    by_first = joined(pairs[0], pairs[1], second, axis)
    return jnp.where(core == 1, by_first, jnp.swapaxes(by_first, axis, axis + 1))


def split_bit(values, mine, position):
    send = lax.dynamic_index_in_dim(values, 1 - mine, position, keepdims=False)
    keep = lax.dynamic_index_in_dim(values, mine, position, keepdims=False)
    return keep, send


def scatter_all(halves, orders, myself, axis, spread, between):
    left = [sorted(order, reverse=True) for order in orders]
    carried = None
    totals = [None for _ in orders]
    for stage in range(len(orders[0])):
        others = [flip(send, order[stage]) for (_, send), order in zip(halves, orders)]
        if stage in between:
            carried = between[stage](carried)
            others, carried = lax.optimization_barrier((others, carried))
        for index, order in enumerate(orders):
            left[index].remove(order[stage])
            keep, other = halves[index][0], others[index]
            if stage == 0:
                keep, other = spread(keep, len(left[index])), spread(other, len(left[index]))
            if not left[index]:
                totals[index] = keep + other.astype(jnp.float32)
                continue
            bit = order[stage + 1]
            mine, position = bit_of(myself, bit), axis + left[index].index(bit)
            keep, send = split_bit(keep, mine, position)
            keep_other, send_other = split_bit(other, mine, position)
            halves[index] = (
                keep + keep_other.astype(jnp.float32),
                (send + send_other.astype(jnp.float32)).astype(jnp.bfloat16),
            )
    return totals, carried


def index_bits(devices):
    return devices.bit_length() - 1


def colour_orders(devices):
    chip_bits = list(range(1, index_bits(devices)))
    rest, last = chip_bits[:-1], chip_bits[-1:]
    shifts = [(colour * len(rest)) // COLOURS for colour in range(COLOURS)]
    return [tuple(rest[shift:] + rest[:shift] + last) for shift in shifts]


def contract(left, right, left_dim, right_dim):
    return lax.dot_general(
        left, right, (((left_dim,), (right_dim,)), ((), ())), preferred_element_type=jnp.float32
    )


def layer_norm(stream):
    centred = stream - jnp.mean(stream, axis=-1, keepdims=True)
    inverse = lax.rsqrt(jnp.mean(centred * centred, axis=-1, keepdims=True) + NORM_EPS)
    return (centred * inverse, inverse)


def norm_back(normed, inverse, upstream):
    return inverse * (
        upstream
        - jnp.mean(upstream, axis=-1, keepdims=True)
        - normed * jnp.mean(upstream * normed, axis=-1, keepdims=True)
    )


def column_sum(values):
    return jnp.sum(values, axis=0, keepdims=True)


def scores_of(query, keys, width):
    return contract(query, keys, 1, 1) * width ** (-0.5)


def whole_weight(mine_ref, other_ref, index, core):
    mine, other = mine_ref[index], other_ref[index]
    return jnp.concatenate(
        [jnp.where(core == 1, other, mine), jnp.where(core == 1, mine, other)], axis=1
    )


def attention_forward(
    place_ref,
    source_ref,
    mod_ref,
    offsets_ref,
    mine_ref,
    other_ref,
    lefts_ref,
    qkv_ref,
    attn_ref,
    middle_ref,
):
    core = place_ref[0]
    seqlen, features = source_ref.shape
    width = features // HEADS
    stream = source_ref[...].astype(jnp.float32)
    normed, _ = layer_norm(stream)
    attn_input = (normed * (1.0 + mod_ref[1:2]) + mod_ref[0:1]).astype(jnp.bfloat16)
    lefts_ref[0] = attn_input
    qkv_ref[0] = (contract(attn_input, whole_weight(mine_ref, other_ref, 0, core), 1, 0) + offsets_ref[6:7]).astype(
        jnp.bfloat16
    )
    qkv_ref[1] = contract(attn_input, whole_weight(mine_ref, other_ref, 1, core), 1, 0).astype(jnp.bfloat16)
    qkv_ref[2] = (contract(attn_input, whole_weight(mine_ref, other_ref, 2, core), 1, 0) + offsets_ref[7:8]).astype(
        jnp.bfloat16
    )
    first = lax.broadcasted_iota(jnp.int32, (seqlen, 2 * width), 1) < width
    for pair in range(HEADS // 2):
        columns = slice(2 * width * pair, 2 * width * (pair + 1))
        query, keys, values = qkv_ref[0, :, columns], qkv_ref[1, :, columns], qkv_ref[2, :, columns]
        halves = []
        for mask in (first, jnp.logical_not(first)):
            scores = scores_of(jnp.where(mask, query, jnp.zeros_like(query)), keys, width)
            log_total = jnp.log(jnp.sum(jnp.exp(scores), axis=-1, keepdims=True))
            probs = jnp.exp(scores - log_total).astype(jnp.bfloat16)
            halves.append(contract(probs, values, 1, 0))
        lefts_ref[1, :, columns] = jnp.where(first, *halves).astype(jnp.bfloat16)
    attn_out = contract(lefts_ref[1], whole_weight(mine_ref, other_ref, 3, core), 1, 0) + offsets_ref[8:9]
    attn_ref[...] = attn_out
    middle = stream + mod_ref[2:3] * attn_out
    middle_ref[...] = middle
    normed_two, _ = layer_norm(middle)
    lefts_ref[2] = (normed_two * (1.0 + mod_ref[4:5]) + mod_ref[3:4]).astype(jnp.bfloat16)


def split_columns(values, core):
    width = values.shape[-1] // 2
    low, high = values[:, :width], values[:, width:]
    return (jnp.where(core == 1, high, low), jnp.where(core == 1, low, high))


def mlp_both_ways(
    place_ref,
    lefts_ref,
    middle_ref,
    attn_ref,
    upstream_ref,
    mod_ref,
    offsets_ref,
    up_ref,
    up_other_ref,
    down_ref,
    down_other_ref,
    output_ref,
    hidden_ref,
    keep_ref,
    send_ref,
    grad_middle_ref,
    grad_attn_ref,
    rows_ref,
    total_ref,
    grad_total_ref,
    grad_mlp_ref,
):
    step = pl.program_id(0)
    last = pl.num_programs(0) - 1
    core, live = place_ref[0], place_ref[1] > 0
    scale = 0.7978845608028654

    @pl.when(step == 0)
    def _():
        total_ref[...] = jnp.zeros_like(total_ref)
        grad_total_ref[...] = jnp.zeros_like(grad_total_ref)
        grad_mlp = jnp.where(live, upstream_ref[...].astype(jnp.float32) * mod_ref[5:6], 0.0)
        grad_mlp_b = grad_mlp.astype(jnp.bfloat16)
        grad_mlp_ref[...] = grad_mlp_b
        keep_ref[0], send_ref[0] = split_columns(grad_mlp_b, core)
        rows_ref[...] = jnp.zeros_like(rows_ref)
        rows_ref[pl.ds(10 + last, 1)] = column_sum(grad_mlp)

    up_w = whole_weight(up_ref, up_other_ref, 0, core)
    down_w = whole_weight(down_ref, down_other_ref, 0, core)
    before = contract(lefts_ref[0], up_w, 1, 0) + offsets_ref[pl.ds(9 + step, 1)]
    square = before * before
    bend = jnp.tanh(scale * (before + 0.044715 * square * before))
    hidden = (0.5 * before * (1.0 + bend)).astype(jnp.bfloat16)
    hidden_ref[0] = hidden
    total_ref[...] += contract(hidden, down_w, 1, 0)
    slope = 0.5 * (1.0 + bend) + 0.5 * before * (1.0 - bend * bend) * scale * (
        1.0 + 3.0 * 0.044715 * square
    )
    grad_pre = jnp.where(live, contract(grad_mlp_ref[...], down_w, 1, 1) * slope, 0.0)
    grad_pre_b = grad_pre.astype(jnp.bfloat16)
    keep_ref[step + 1], send_ref[step + 1] = split_columns(grad_pre_b, core)
    rows_ref[pl.ds(9 + step, 1)] = column_sum(grad_pre)
    grad_total_ref[...] += contract(grad_pre_b, up_w, 1, 1)

    @pl.when(step == last)
    def _():
        middle = middle_ref[...]
        grad_out = upstream_ref[...].astype(jnp.float32)
        mlp_out = total_ref[...] + offsets_ref[pl.ds(10 + last, 1)]
        output = middle + mod_ref[5:6] * mlp_out
        output_ref[...] = jnp.where(live, output, 0.0).astype(jnp.bfloat16)
        rows_ref[5:6] = jnp.where(live, column_sum(grad_out * mlp_out), 0.0)
        normed, inverse = layer_norm(middle)
        grad_in = grad_total_ref[...]
        rows_ref[3:4] = column_sum(grad_in)
        rows_ref[4:5] = column_sum(grad_in * normed)
        grad_middle = grad_out + norm_back(normed, inverse, grad_in * (1.0 + mod_ref[4:5]))
        grad_middle = jnp.where(live, grad_middle, 0.0)
        grad_middle_ref[...] = grad_middle
        rows_ref[2:3] = column_sum(grad_middle * attn_ref[...])
        grad_attn = grad_middle * mod_ref[2:3]
        grad_attn_ref[...] = grad_attn.astype(jnp.bfloat16)
        rows_ref[8:9] = column_sum(grad_attn)


def attention_backward(
    place_ref,
    source_ref,
    mod_ref,
    mine_ref,
    other_ref,
    qkv_ref,
    grad_middle_ref,
    grad_attn_ref,
    rows_in_ref,
    grad_source_ref,
    keep_ref,
    send_ref,
    rows_ref,
    grads_ref,
    context_ref,
):
    seqlen, features = source_ref.shape
    width = features // HEADS
    core, live = place_ref[0], place_ref[1] > 0
    rows_ref[...] = rows_in_ref[...]
    grad_attn = grad_attn_ref[...]
    keep_ref[3], send_ref[3] = split_columns(grad_attn, core)
    context_ref[...] = contract(
        grad_attn, whole_weight(mine_ref, other_ref, 3, core), 1, 1
    ).astype(jnp.bfloat16)
    first = lax.broadcasted_iota(jnp.int32, (seqlen, 2 * width), 1) < width
    for pair in range(HEADS // 2):
        columns = slice(2 * width * pair, 2 * width * (pair + 1))
        query, keys, values = qkv_ref[0, :, columns], qkv_ref[1, :, columns], qkv_ref[2, :, columns]
        upstream = context_ref[:, columns]
        parts = []
        for mask in (first, jnp.logical_not(first)):
            scores = scores_of(jnp.where(mask, query, jnp.zeros_like(query)), keys, width)
            log_total = jnp.log(jnp.sum(jnp.exp(scores), axis=-1, keepdims=True))
            probs = jnp.exp(scores - log_total)
            grad_values = contract(probs.astype(jnp.bfloat16), upstream, 0, 0)
            grad_probs = contract(
                jnp.where(mask, upstream, jnp.zeros_like(upstream)), values, 1, 1
            )
            row_dot = jnp.sum(probs * grad_probs, axis=-1, keepdims=True)
            grad_scores = (probs * (grad_probs - row_dot) * width ** (-0.5)).astype(jnp.bfloat16)
            parts.append(
                (
                    contract(grad_scores, keys, 1, 0),
                    contract(grad_scores, query, 0, 0),
                    grad_values,
                )
            )
        for index in range(3):
            merged = jnp.where(live, jnp.where(first, parts[0][index], parts[1][index]), 0.0)
            grads_ref[index, :, columns] = merged.astype(jnp.bfloat16)
            if index != 1:
                row = 6 if index == 0 else 7
                rows_ref[row : row + 1, columns] = column_sum(merged)
    grad_in = jnp.zeros((seqlen, features), jnp.float32)
    for index in range(3):
        grads = grads_ref[index]
        keep_ref[index], send_ref[index] = split_columns(grads, core)
        grad_in += contract(grads, whole_weight(mine_ref, other_ref, index, core), 1, 1)
    normed, inverse = layer_norm(source_ref[...].astype(jnp.float32))
    rows_ref[0:1] = column_sum(grad_in)
    rows_ref[1:2] = column_sum(grad_in * normed)
    grad_source_ref[...] = jnp.where(
        live,
        grad_middle_ref[...] + norm_back(normed, inverse, grad_in * (1.0 + mod_ref[1:2])),
        0.0,
    )


def pair_products(
    chunk, mine_ref, left_ref, left_other_ref, right_ref, right_other_ref, keep_ref, send_ref
):
    total = contract(left_ref[0], right_ref[0], 0, 0) + contract(
        left_other_ref[0], right_other_ref[0], 0, 0
    )
    for start in range(0, total.shape[0] // 2, chunk):
        low = total[2 * start : 2 * start + chunk]
        high = total[2 * start + chunk : 2 * start + 2 * chunk]
        mine = mine_ref[0] == 1
        keep_ref[0, start : start + chunk] = jnp.where(mine, high, low)
        send_ref[0, start : start + chunk] = jnp.where(mine, low, high).astype(jnp.bfloat16)


def plain_products(left_ref, left_other_ref, right_ref, right_other_ref, out_ref):
    out_ref[0] = contract(left_ref[0], right_ref[0], 0, 0) + contract(
        left_other_ref[0], right_other_ref[0], 0, 0
    )


def struct(shape, dtype):
    return jax.ShapeDtypeStruct(shape, dtype)


VMEM = pl.BlockSpec(memory_space=pltpu.VMEM)
SMEM = pl.BlockSpec(memory_space=pltpu.SMEM)


def resident(shape):
    zeros = (0,) * len(shape)
    return pl.BlockSpec(shape, lambda step: zeros)


def run_attention_forward(place, source, modulation, offsets, attn_w, attn_w_other):
    seqlen, features = source.shape
    return pl.pallas_call(
        attention_forward,
        name="attention_forward",
        out_shape=(
            struct((3, seqlen, features), jnp.bfloat16),
            struct((3, seqlen, features), jnp.bfloat16),
            struct((seqlen, features), jnp.float32),
            struct((seqlen, features), jnp.float32),
        ),
        in_specs=[SMEM] + [VMEM] * 5,
        out_specs=(VMEM,) * 4,
        compiler_params=pltpu.CompilerParams(vmem_limit_bytes=24 << 20),
        cost_estimate=pl.CostEstimate(
            flops=8 * seqlen * features * features + 8 * HEADS * seqlen * seqlen * 128,
            bytes_accessed=attn_w.size * 4 + source.size * 20,
            transcendentals=2 * HEADS * seqlen * seqlen,
        ),
    )(place, source, modulation, offsets, attn_w, attn_w_other)


def run_mlp(place, lefts, middle, attn_out, upstream, modulation, offsets, up_ws, down_ws):
    seqlen, features = middle.shape
    steps = up_ws[0].shape[0]
    half = features // 2
    whole = (seqlen, features)
    return pl.pallas_call(
        mlp_both_ways,
        name="mlp_both_ways",
        grid=(steps,),
        out_shape=(
            struct(whole, jnp.bfloat16),
            struct((steps,) + whole, jnp.bfloat16),
            struct((steps + 1, seqlen, half), jnp.bfloat16),
            struct((steps + 1, seqlen, half), jnp.bfloat16),
            struct(whole, jnp.float32),
            struct(whole, jnp.bfloat16),
            struct(offsets.shape, jnp.float32),
        ),
        in_specs=[
            SMEM,
            pl.BlockSpec((1,) + whole, lambda step: (2, 0, 0)),
            resident(whole),
            resident(whole),
            resident(whole),
            resident(modulation.shape),
            resident(offsets.shape),
        ]
        + [pl.BlockSpec((1, features, half), lambda step: (step, 0, 0))] * 4,
        out_specs=(
            resident(whole),
            pl.BlockSpec((1,) + whole, lambda step: (step, 0, 0)),
            resident((steps + 1, seqlen, half)),
            resident((steps + 1, seqlen, half)),
            resident(whole),
            resident(whole),
            resident(offsets.shape),
        ),
        scratch_shapes=[
            pltpu.VMEM(whole, jnp.float32),
            pltpu.VMEM(whole, jnp.float32),
            pltpu.VMEM(whole, jnp.bfloat16),
        ],
        compiler_params=pltpu.CompilerParams(vmem_limit_bytes=28 << 20),
        cost_estimate=pl.CostEstimate(
            flops=8 * seqlen * features * features * steps,
            bytes_accessed=up_ws[0].size * 8 + seqlen * features * 40,
            transcendentals=seqlen * features * steps,
        ),
    )(place, lefts, middle, attn_out, upstream, modulation, offsets, *up_ws, *down_ws)


def run_attention_backward(
    place, source, modulation, attn_w, attn_w_other, qkv, grad_middle, grad_attn, rows
):
    seqlen, features = source.shape
    half = features // 2
    return pl.pallas_call(
        attention_backward,
        name="attention_backward",
        out_shape=(
            struct((seqlen, features), jnp.float32),
            struct((4, seqlen, half), jnp.bfloat16),
            struct((4, seqlen, half), jnp.bfloat16),
            struct(rows.shape, jnp.float32),
        ),
        in_specs=[SMEM] + [VMEM] * 8,
        out_specs=(VMEM,) * 4,
        scratch_shapes=[
            pltpu.VMEM((3, seqlen, features), jnp.bfloat16),
            pltpu.VMEM((seqlen, features), jnp.bfloat16),
        ],
        compiler_params=pltpu.CompilerParams(vmem_limit_bytes=24 << 20),
        cost_estimate=pl.CostEstimate(
            flops=8 * seqlen * features * features + 20 * HEADS * seqlen * seqlen * 128,
            bytes_accessed=attn_w.size * 4 + source.size * 24,
            transcendentals=2 * HEADS * seqlen * seqlen,
        ),
    )(place, source, modulation, attn_w, attn_w_other, qkv, grad_middle, grad_attn, rows)


def run_products(lefts, lefts_other, rights, rights_other, left_at, right_at, count, mine, chunk):
    _, seqlen, features = lefts.shape
    width = rights.shape[-1]
    left_spec = pl.BlockSpec((1, seqlen, features), lambda step: (left_at(step), 0, 0))
    right_spec = pl.BlockSpec((1, seqlen, width), lambda step: (right_at(step), 0, 0))
    specs = [left_spec, left_spec, right_spec, right_spec]
    cost = pl.CostEstimate(
        flops=4 * count * seqlen * features * width,
        bytes_accessed=count * features * width * 6,
        transcendentals=0,
    )
    if chunk % 16:
        total = pl.pallas_call(
            plain_products,
            name="plain_products",
            grid=(count,),
            out_shape=struct((count, features, width), jnp.float32),
            in_specs=specs,
            out_specs=pl.BlockSpec((1, features, width), lambda step: (step, 0, 0)),
            cost_estimate=cost,
        )(lefts, lefts_other, rights, rights_other)
        keep, send = split_bit(
            total.reshape(count, features // (2 * chunk), 2, chunk, width), mine, 2
        )
        shape = (count, features // 2, width)
        return keep.reshape(shape), send.reshape(shape).astype(jnp.bfloat16)
    half_spec = pl.BlockSpec((1, features // 2, width), lambda step: (step, 0, 0))
    return pl.pallas_call(
        functools.partial(pair_products, chunk),
        name="pair_products",
        grid=(count,),
        out_shape=(
            struct((count, features // 2, width), jnp.float32),
            struct((count, features // 2, width), jnp.bfloat16),
        ),
        in_specs=[SMEM] + specs,
        out_specs=(half_spec, half_spec),
        cost_estimate=cost,
    )(mine[None], lefts, lefts_other, rights, rights_other)


def muon_steps(block):
    values = block.astype(jnp.float32)
    scaled = (values / (jnp.sqrt(jnp.sum(values * values)) + 1e-07)).astype(jnp.bfloat16)
    for _ in range(NS_ITERS):
        gram = contract(scaled, scaled, 1, 1).astype(jnp.bfloat16)
        square = contract(gram, gram, 1, 0)
        mixed = (COEF_SECOND * gram.astype(jnp.float32) + COEF_THIRD * square).astype(jnp.bfloat16)
        scaled = (
            COEF_FIRST * scaled.astype(jnp.float32) + contract(mixed, scaled, 1, 0)
        ).astype(jnp.bfloat16)
    return scaled


def orthogonalize_halves(place_ref, mine_ref, other_ref, out_ref):
    core = place_ref[0]
    scaled = muon_steps(whole_weight(mine_ref, other_ref, slice(None), core))
    out_ref[...] = split_columns(scaled, core)[0]


def orthogonalize_whole(block_ref, out_ref):
    out_ref[0] = muon_steps(block_ref[0])


def muon_cost(count, rows):
    return pl.CostEstimate(
        flops=6 * count * NS_ITERS * rows**3, bytes_accessed=4 * count * rows**2, transcendentals=0
    )


def run_orthogonalize_halves(place, mine, other):
    return pl.pallas_call(
        orthogonalize_halves,
        name="orthogonalize_halves",
        out_shape=struct(mine.shape, mine.dtype),
        in_specs=[SMEM, VMEM, VMEM],
        out_specs=VMEM,
        compiler_params=pltpu.CompilerParams(vmem_limit_bytes=24 << 20),
        cost_estimate=muon_cost(1, mine.shape[0]),
    )(place, mine, other)


def run_orthogonalize_whole(blocks):
    spec = pl.BlockSpec((1,) + blocks.shape[1:], lambda step: (step, 0, 0))
    return pl.pallas_call(
        orthogonalize_whole,
        name="orthogonalize_whole",
        grid=(blocks.shape[0],),
        out_shape=struct(blocks.shape, blocks.dtype),
        in_specs=[spec],
        out_specs=spec,
        compiler_params=pltpu.CompilerParams(vmem_limit_bytes=24 << 20),
        cost_estimate=muon_cost(*blocks.shape[:2]),
    )(blocks)


def all_to_all(values):
    return lax.all_to_all(values, "dp", split_axis=0, concat_axis=0, tiled=True)


def to_all(row):
    devices = lax.axis_size("dp")
    return all_to_all(jnp.broadcast_to(row[None], (devices,) + row.shape))


def on_device(latents, conditioning, cotangent, weights, biases, momenta, bias_momenta, counts):
    _, seqlen, features = latents.shape
    block_count, share, _ = weights.shape
    hidden_blocks = (block_count - 10) // 2
    bias_count = biases.shape[0]
    devices = lax.axis_size("dp")
    myself = lax.axis_index("dp")
    core = bit_of(myself, 0)
    bits = index_bits(devices)
    orders = colour_orders(devices)
    ranks = jnp.arange(devices, dtype=jnp.int32)
    live_here = jnp.sum(jnp.where(ranks == myself, counts, 0)) > 0

    lowered = weights.astype(jnp.bfloat16)
    ada_w = lowered[:ADA]
    condition = conditioning[0].astype(jnp.float32)
    silu_cond = jax.nn.silu(condition).astype(jnp.bfloat16)

    half = features // 2
    rest = lowered[ADA:]
    columns_mine = lax.dynamic_slice_in_dim(rest, core * half, half, 2)
    columns_other = lax.dynamic_slice_in_dim(rest, (1 - core) * half, half, 2)
    columns_other = flip(columns_other, 0)
    chip_rows = jnp.where(
        core == 1,
        jnp.concatenate([columns_other, columns_mine], axis=1),
        jnp.concatenate([columns_mine, columns_other], axis=1),
    )
    bounds = [0, 10 - ADA, 10 - ADA + hidden_blocks, block_count - ADA]
    stages = bits - 1
    conditions = jnp.concatenate([silu_cond, biases.astype(jnp.bfloat16).reshape(-1)])
    small_all = to_all(conditions)

    def partial_products(small_all):
        silu_rows = lax.dynamic_slice_in_dim(small_all[:, :features], myself * share, share, 1)
        mod_parts = product("ld,kde->lke", silu_rows, ada_w).reshape(devices, ADA * features)
        return small_all, silu_rows, mod_parts

    def modulations(carried):
        small_all, silu_rows, mod_parts = carried
        return small_all, silu_rows, all_to_all(mod_parts)

    between = {0: lambda _: small_all, 1: partial_products, stages - 1: modulations}
    groups, (small_all, silu_rows, mod_sums) = gather_all(
        [chip_rows[low:high] for low, high in zip(bounds[:-1], bounds[1:])],
        [tuple(reversed(order)) for order in orders],
        myself,
        1,
        between,
    )
    offsets = (
        small_all[:, features:]
        .reshape(devices, bias_count, share)
        .transpose(1, 0, 2)
        .reshape(bias_count, features)
        .astype(jnp.float32)
    )
    modulation = jnp.sum(mod_sums, axis=0).reshape(ADA, features) + offsets[:ADA]
    attn_ws, up_ws, down_ws = [
        (group, flip(group, 0))
        for group in [group.reshape(-1, features, half) for group in groups]
    ]

    place = jnp.stack([core, live_here.astype(jnp.int32)]).astype(jnp.int32)
    lefts, qkv, attn_out, middle = run_attention_forward(
        place, latents[0], modulation, offsets, *attn_ws
    )
    lefts_other = flip(lefts, 0)
    output, hidden, mlp_keep, mlp_send, grad_middle, grad_attn, rows = run_mlp(
        place, lefts, middle, attn_out, cotangent[0], modulation, offsets, up_ws, down_ws
    )
    hidden_other = flip(hidden, 0)
    mlp_other = flip(mlp_send, 0)

    def spread(mats, count):
        return mats.reshape((mats.shape[0],) + (2,) * count + (2 * share, half))

    def products(left, left_other, right, right_other, left_at, right_at, count, order):
        return run_products(
            left,
            left_other,
            right,
            right_other,
            left_at,
            right_at,
            count,
            bit_of(myself, order[0]),
            share << order[0],
        )

    down_halves = products(
        hidden, hidden_other, mlp_keep, mlp_other, lambda b: b, lambda b: 0, hidden_blocks, orders[0]
    )
    up_halves = products(
        lefts, lefts_other, mlp_keep, mlp_other, lambda b: 2, lambda b: b + 1, hidden_blocks, orders[1]
    )
    input_grad, attn_keep, attn_send, grad_offsets = run_attention_backward(
        place, latents[0], modulation, *attn_ws, qkv, grad_middle, grad_attn, rows
    )
    attn_other = flip(attn_send, 0)
    attn_halves = products(
        lefts, lefts_other, attn_keep, attn_other, lambda b: b // 3, lambda b: b, 4, orders[2]
    )

    grad_mod_b = grad_offsets[:ADA].astype(jnp.bfloat16).reshape(-1)
    by_holder = (
        grad_offsets.reshape(bias_count, devices, share)
        .transpose(1, 0, 2)
        .reshape(devices, bias_count * share)
    )
    coarse = lax.reduce_precision(by_holder, 8, 7)
    mod_and_offsets = jnp.concatenate(
        [
            jnp.broadcast_to(grad_mod_b[None], (devices, ADA * features)),
            coarse.astype(jnp.bfloat16),
            (by_holder - coarse).astype(jnp.bfloat16),
        ],
        axis=1,
    )

    chips = devices // 2
    extra = max(0, block_count - chips)
    assert extra % 2 == 0 and extra <= ADA
    main = block_count - extra
    grad_scale = lax.rsqrt((seqlen * jnp.sum(counts)).astype(jnp.float32))

    def conditioning_grads(mod_and_offsets):
        mod_all = mod_and_offsets[:, : ADA * features].reshape(devices, ADA, features)
        silu_parts = product("lke,kde->ld", mod_all, ada_w)
        return mod_and_offsets, mod_all, all_to_all(silu_parts)

    sums, (mod_and_offsets, mod_all, grad_silu) = scatter_all(
        [attn_halves, up_halves, down_halves],
        [orders[2], orders[1], orders[0]],
        myself,
        1,
        spread,
        {1: lambda _: all_to_all(mod_and_offsets), stages - 1: conditioning_grads},
    )
    chip_rows = jnp.concatenate(sums, axis=0)
    rows_mine = lax.dynamic_slice_in_dim(chip_rows, core * share, share, 1)
    rows_other = flip(lax.dynamic_slice_in_dim(chip_rows, (1 - core) * share, share, 1), 0)

    ada_share = product("ld,lke->kde", silu_rows, mod_all)
    early_rows = ()
    if extra:
        early = BETA_WEIGHT * momenta[:extra] + ada_share[:extra] * grad_scale
        early = early.astype(jnp.bfloat16).reshape(2, extra // 2, share, features)
        early_mine = lax.dynamic_index_in_dim(early, core, 0, keepdims=False)
        early_other = flip(lax.dynamic_index_in_dim(early, 1 - core, 0, keepdims=False), 0)
        early_rows = joined(early_mine, early_other, core, 1)
        early_rows = early_rows.reshape(extra // 2, 2 * share, features)
        rows_other, early_rows = lax.optimization_barrier((rows_other, early_rows))
    offset_share = jnp.sum(
        mod_and_offsets[:, ADA * features :]
        .astype(jnp.float32)
        .reshape(devices * 2, bias_count, share),
        axis=0,
    )

    rest_share = jnp.where(
        core == 1,
        jnp.concatenate([rows_other, rows_mine], axis=2),
        jnp.concatenate([rows_mine, rows_other], axis=2),
    )
    weight_grads = jnp.concatenate([ada_share, rest_share], axis=0) * grad_scale
    bias_grads = offset_share * grad_scale
    new_momenta = BETA_WEIGHT * momenta + weight_grads
    new_bias_momenta = BETA_BIAS * bias_momenta + bias_grads
    new_biases = biases - RATE_BIAS * new_bias_momenta

    lowered_momenta = new_momenta.astype(jnp.bfloat16)
    outgoing = (
        lowered_momenta[extra:]
        .reshape(main, share, 2, half)
        .transpose(0, 2, 1, 3)
        .reshape(2 * main, share, half)
    )
    outgoing = jnp.pad(outgoing, ((0, devices - 2 * main), (0, 0), (0, 0)))
    columns_mine = all_to_all(outgoing).reshape(features, half)
    early_bits = tuple(reversed(range(1, bits)))
    if extra:
        for bit in early_bits[:-2]:
            early_rows = gather_step(early_rows, early_bits, bit, myself)
        columns_mine, early_rows = lax.optimization_barrier((columns_mine, early_rows))
        early_rows = jnp.stack(
            [early_rows, flip_by_core(early_rows, early_bits[-2], early_bits[-1])]
        )
    ortho_half = run_orthogonalize_halves(place, columns_mine, flip(columns_mine, 0))
    if extra:
        ortho_half, early_rows = lax.optimization_barrier((ortho_half, early_rows))
    ortho_local = (
        all_to_all(ortho_half.reshape(devices, share, half))[: 2 * main]
        .reshape(main, 2, share, half)
        .transpose(0, 2, 1, 3)
        .reshape(main, share, features)
    )
    if extra:
        early_rows = corner_rows(
            early_rows, flip_by_core(early_rows, early_bits[-1], early_bits[-2]), early_bits, myself
        )
        early_ortho = run_orthogonalize_whole(early_rows.reshape(extra // 2, features, features))
        chip_ortho = lax.dynamic_slice_in_dim(
            early_ortho, (myself - core) * share, 2 * share, 1
        ).reshape(extra // 2, 2, share, features)
        ortho_mine = lax.dynamic_index_in_dim(chip_ortho, core, 1, keepdims=False)
        ortho_other = flip(
            lax.dynamic_index_in_dim(chip_ortho, 1 - core, 1, keepdims=False), 0
        )
        early_local = joined(ortho_mine, ortho_other, core, 0).reshape(extra, share, features)
        ortho_local = jnp.concatenate([early_local, ortho_local])
    silu_back = jax.vjp(jax.nn.silu, condition)[1]
    cond_grad = silu_back(grad_silu.reshape(features))[0] * seqlen ** (-0.5)
    new_weights = weights - RATE_WEIGHT * ortho_local.astype(jnp.float32)
    cond_grad = jnp.where(live_here, cond_grad, jnp.zeros_like(cond_grad))[None]
    return (
        output[None],
        input_grad[None],
        cond_grad,
        weight_grads,
        bias_grads,
        new_weights,
        new_momenta,
        new_biases,
        new_bias_momenta,
    )


def solution(mesh):
    return jax.shard_map(
        on_device,
        mesh=mesh,
        in_specs=(
            P("dp", None, None),
            P("dp", None),
            P("dp", None, None),
            P(None, "dp", None),
            P(None, "dp"),
            P(None, "dp", None),
            P(None, "dp"),
            P(),
        ),
        out_specs=(
            P("dp", None, None),
            P("dp", None, None),
            P("dp", None),
            P(None, "dp", None),
            P(None, "dp"),
            P(None, "dp", None),
            P(None, "dp", None),
            P(None, "dp"),
            P(None, "dp"),
        ),
        check_vma=False,
    )
```

```python
import functools

import jax
import jax.numpy as jnp
from jax import lax
from jax.experimental import pallas as pl
from jax.experimental.pallas import tpu as pltpu
from jax.sharding import PartitionSpec as P


HEADS = 12
NS_ITERS = 2
ADA = 6
COLOURS = 3

COEF_FIRST = 3.4445
COEF_SECOND = -4.775
COEF_THIRD = 2.0315
BETA_WEIGHT = 0.95
BETA_BIAS = 0.9
RATE_WEIGHT = 1.0
RATE_BIAS = 0.1
NORM_EPS = 1e-06


def product(spec, left, right):
    return jnp.einsum(spec, left, right, preferred_element_type=jnp.float32)


def flip(values, bit):
    devices = lax.axis_size("dp")
    return lax.ppermute(values, "dp", [(i, i ^ (1 << bit)) for i in range(devices)])


def bit_of(myself, bit):
    return (myself >> bit) & 1


def joined(values, other, taken, axis):
    return jnp.where(
        taken == 1, jnp.stack([other, values], axis), jnp.stack([values, other], axis)
    )


def gather_all(groups, orders, myself, first_too, last_too):
    carried = first_too
    for stage in range(len(orders[0])):
        others = [flip(group, order[stage]) for group, order in zip(groups, orders)]
        if stage == len(orders[0]) - 1:
            carried = last_too(carried)
        if stage in (0, len(orders[0]) - 1):
            others[-1], carried = lax.optimization_barrier((others[-1], carried))
        for index, order in enumerate(orders):
            bit = order[stage]
            groups[index] = joined(groups[index], others[index], bit_of(myself, bit), 0)
    return groups, carried


def split_bit(values, mine, position, sent_as):
    send = lax.dynamic_index_in_dim(values, 1 - mine, position, keepdims=False)
    keep = lax.dynamic_index_in_dim(values, mine, position, keepdims=False)
    return keep, send.astype(sent_as)


def scatter_all(halves, orders, myself, axis, spread, between):
    left = [sorted(order, reverse=True) for order in orders]
    carried = None
    totals = []
    for stage in range(len(orders[0])):
        others = [flip(send, order[stage]) for (_, send), order in zip(halves, orders)]
        if stage in between:
            carried = between[stage](carried)
            others[-1], carried = lax.optimization_barrier((others[-1], carried))
        totals = [
            keep + other.astype(jnp.float32) for (keep, _), other in zip(halves, others)
        ]
        for index, order in enumerate(orders):
            left[index].remove(order[stage])
            if stage == 0:
                totals[index] = spread(totals[index], len(left[index]))
            if left[index]:
                bit = order[stage + 1]
                position = axis + left[index].index(bit)
                halves[index] = split_bit(
                    totals[index], bit_of(myself, bit), position, jnp.bfloat16
                )
    return totals, carried


def index_bits(devices):
    return devices.bit_length() - 1


def colour_orders(devices):
    chip_bits = list(range(1, index_bits(devices)))
    rest, last = chip_bits[:-1], chip_bits[-1:]
    shifts = [(colour * len(rest)) // COLOURS for colour in range(COLOURS)]
    return [tuple(rest[shift:] + rest[:shift] + last) for shift in shifts]


def contract(left, right, left_dim, right_dim):
    return lax.dot_general(
        left, right, (((left_dim,), (right_dim,)), ((), ())), preferred_element_type=jnp.float32
    )


def layer_norm(stream):
    centred = stream - jnp.mean(stream, axis=-1, keepdims=True)
    inverse = lax.rsqrt(jnp.mean(centred * centred, axis=-1, keepdims=True) + NORM_EPS)
    return (centred * inverse, inverse)


def norm_back(normed, inverse, upstream):
    return inverse * (
        upstream
        - jnp.mean(upstream, axis=-1, keepdims=True)
        - normed * jnp.mean(upstream * normed, axis=-1, keepdims=True)
    )


def column_sum(values):
    return jnp.sum(values, axis=0, keepdims=True)


def scores_of(query, keys, width):
    return contract(query, keys, 1, 1) * width ** (-0.5)


def chunk_places(order):
    count = len(order)
    return [
        sum(((chip >> (bit - 1)) & 1) << place for place, bit in enumerate(order))
        for chip in range(1 << count)
    ]


def whole_weight(mine_ref, other_ref, index, core, order):
    places = chunk_places(order) if order else [0]
    mine, other = [
        jnp.concatenate([ref[place, index] for place in places], axis=0)
        for ref in (mine_ref, other_ref)
    ]
    return jnp.concatenate(
        [jnp.where(core == 1, other, mine), jnp.where(core == 1, mine, other)], axis=1
    )


def attention_forward(
    order,
    place_ref,
    source_ref,
    mod_ref,
    offsets_ref,
    mine_ref,
    other_ref,
    lefts_ref,
    qkv_ref,
    attn_ref,
    middle_ref,
):
    core = place_ref[0]
    seqlen, features = source_ref.shape
    width = features // HEADS
    stream = source_ref[...].astype(jnp.float32)
    normed, _ = layer_norm(stream)
    attn_input = (normed * (1.0 + mod_ref[1:2]) + mod_ref[0:1]).astype(jnp.bfloat16)
    lefts_ref[0] = attn_input
    qkv_ref[0] = (contract(attn_input, whole_weight(mine_ref, other_ref, 0, core, order), 1, 0) + offsets_ref[6:7]).astype(
        jnp.bfloat16
    )
    qkv_ref[1] = contract(attn_input, whole_weight(mine_ref, other_ref, 1, core, order), 1, 0).astype(jnp.bfloat16)
    qkv_ref[2] = (contract(attn_input, whole_weight(mine_ref, other_ref, 2, core, order), 1, 0) + offsets_ref[7:8]).astype(
        jnp.bfloat16
    )
    first = lax.broadcasted_iota(jnp.int32, (seqlen, 2 * width), 1) < width
    for pair in range(HEADS // 2):
        columns = slice(2 * width * pair, 2 * width * (pair + 1))
        query, keys, values = qkv_ref[0, :, columns], qkv_ref[1, :, columns], qkv_ref[2, :, columns]
        halves = []
        for mask in (first, jnp.logical_not(first)):
            scores = scores_of(jnp.where(mask, query, jnp.zeros_like(query)), keys, width)
            log_total = jnp.log(jnp.sum(jnp.exp(scores), axis=-1, keepdims=True))
            probs = jnp.exp(scores - log_total).astype(jnp.bfloat16)
            halves.append(contract(probs, values, 1, 0))
        lefts_ref[1, :, columns] = jnp.where(first, *halves).astype(jnp.bfloat16)
    attn_out = contract(lefts_ref[1], whole_weight(mine_ref, other_ref, 3, core, order), 1, 0) + offsets_ref[8:9]
    attn_ref[...] = attn_out
    middle = stream + mod_ref[2:3] * attn_out
    middle_ref[...] = middle
    normed_two, _ = layer_norm(middle)
    lefts_ref[2] = (normed_two * (1.0 + mod_ref[4:5]) + mod_ref[3:4]).astype(jnp.bfloat16)


def split_columns(values, core):
    width = values.shape[-1] // 2
    low, high = values[:, :width], values[:, width:]
    return (jnp.where(core == 1, high, low), jnp.where(core == 1, low, high))


def mlp_both_ways(
    up_order,
    down_order,
    place_ref,
    lefts_ref,
    middle_ref,
    attn_ref,
    upstream_ref,
    mod_ref,
    offsets_ref,
    up_ref,
    up_other_ref,
    down_ref,
    down_other_ref,
    output_ref,
    hidden_ref,
    keep_ref,
    send_ref,
    grad_middle_ref,
    grad_attn_ref,
    rows_ref,
    total_ref,
    grad_total_ref,
    grad_mlp_ref,
):
    step = pl.program_id(0)
    last = pl.num_programs(0) - 1
    core, live = place_ref[0], place_ref[1] > 0
    scale = 0.7978845608028654

    @pl.when(step == 0)
    def _():
        total_ref[...] = jnp.zeros_like(total_ref)
        grad_total_ref[...] = jnp.zeros_like(grad_total_ref)
        grad_mlp = jnp.where(live, upstream_ref[...].astype(jnp.float32) * mod_ref[5:6], 0.0)
        grad_mlp_b = grad_mlp.astype(jnp.bfloat16)
        grad_mlp_ref[...] = grad_mlp_b
        keep_ref[0], send_ref[0] = split_columns(grad_mlp_b, core)
        rows_ref[...] = jnp.zeros_like(rows_ref)
        rows_ref[pl.ds(10 + last, 1)] = column_sum(grad_mlp)

    up_w = whole_weight(up_ref, up_other_ref, 0, core, up_order)
    down_w = whole_weight(down_ref, down_other_ref, 0, core, down_order)
    before = contract(lefts_ref[0], up_w, 1, 0) + offsets_ref[pl.ds(9 + step, 1)]
    square = before * before
    bend = jnp.tanh(scale * (before + 0.044715 * square * before))
    hidden = (0.5 * before * (1.0 + bend)).astype(jnp.bfloat16)
    hidden_ref[0] = hidden
    total_ref[...] += contract(hidden, down_w, 1, 0)
    slope = 0.5 * (1.0 + bend) + 0.5 * before * (1.0 - bend * bend) * scale * (
        1.0 + 3.0 * 0.044715 * square
    )
    grad_pre = jnp.where(live, contract(grad_mlp_ref[...], down_w, 1, 1) * slope, 0.0)
    grad_pre_b = grad_pre.astype(jnp.bfloat16)
    keep_ref[step + 1], send_ref[step + 1] = split_columns(grad_pre_b, core)
    rows_ref[pl.ds(9 + step, 1)] = column_sum(grad_pre)
    grad_total_ref[...] += contract(grad_pre_b, up_w, 1, 1)

    @pl.when(step == last)
    def _():
        middle = middle_ref[...]
        grad_out = upstream_ref[...].astype(jnp.float32)
        mlp_out = total_ref[...] + offsets_ref[pl.ds(10 + last, 1)]
        output = middle + mod_ref[5:6] * mlp_out
        output_ref[...] = jnp.where(live, output, 0.0).astype(jnp.bfloat16)
        rows_ref[5:6] = jnp.where(live, column_sum(grad_out * mlp_out), 0.0)
        normed, inverse = layer_norm(middle)
        grad_in = grad_total_ref[...]
        rows_ref[3:4] = column_sum(grad_in)
        rows_ref[4:5] = column_sum(grad_in * normed)
        grad_middle = grad_out + norm_back(normed, inverse, grad_in * (1.0 + mod_ref[4:5]))
        grad_middle = jnp.where(live, grad_middle, 0.0)
        grad_middle_ref[...] = grad_middle
        rows_ref[2:3] = column_sum(grad_middle * attn_ref[...])
        grad_attn = grad_middle * mod_ref[2:3]
        grad_attn_ref[...] = grad_attn.astype(jnp.bfloat16)
        rows_ref[8:9] = column_sum(grad_attn)


def attention_backward(
    order,
    place_ref,
    source_ref,
    mod_ref,
    mine_ref,
    other_ref,
    qkv_ref,
    grad_middle_ref,
    grad_attn_ref,
    rows_in_ref,
    grad_source_ref,
    keep_ref,
    send_ref,
    rows_ref,
    grads_ref,
    context_ref,
):
    seqlen, features = source_ref.shape
    width = features // HEADS
    core, live = place_ref[0], place_ref[1] > 0
    rows_ref[...] = rows_in_ref[...]
    grad_attn = grad_attn_ref[...]
    keep_ref[3], send_ref[3] = split_columns(grad_attn, core)
    context_ref[...] = contract(
        grad_attn, whole_weight(mine_ref, other_ref, 3, core, order), 1, 1
    ).astype(jnp.bfloat16)
    first = lax.broadcasted_iota(jnp.int32, (seqlen, 2 * width), 1) < width
    for pair in range(HEADS // 2):
        columns = slice(2 * width * pair, 2 * width * (pair + 1))
        query, keys, values = qkv_ref[0, :, columns], qkv_ref[1, :, columns], qkv_ref[2, :, columns]
        upstream = context_ref[:, columns]
        parts = []
        for mask in (first, jnp.logical_not(first)):
            scores = scores_of(jnp.where(mask, query, jnp.zeros_like(query)), keys, width)
            log_total = jnp.log(jnp.sum(jnp.exp(scores), axis=-1, keepdims=True))
            probs = jnp.exp(scores - log_total)
            grad_values = contract(probs.astype(jnp.bfloat16), upstream, 0, 0)
            grad_probs = contract(
                jnp.where(mask, upstream, jnp.zeros_like(upstream)), values, 1, 1
            )
            row_dot = jnp.sum(probs * grad_probs, axis=-1, keepdims=True)
            grad_scores = (probs * (grad_probs - row_dot) * width ** (-0.5)).astype(jnp.bfloat16)
            parts.append(
                (
                    contract(grad_scores, keys, 1, 0),
                    contract(grad_scores, query, 0, 0),
                    grad_values,
                )
            )
        for index in range(3):
            merged = jnp.where(live, jnp.where(first, parts[0][index], parts[1][index]), 0.0)
            grads_ref[index, :, columns] = merged.astype(jnp.bfloat16)
            if index != 1:
                row = 6 if index == 0 else 7
                rows_ref[row : row + 1, columns] = column_sum(merged)
    grad_in = jnp.zeros((seqlen, features), jnp.float32)
    for index in range(3):
        grads = grads_ref[index]
        keep_ref[index], send_ref[index] = split_columns(grads, core)
        grad_in += contract(grads, whole_weight(mine_ref, other_ref, index, core, order), 1, 1)
    normed, inverse = layer_norm(source_ref[...].astype(jnp.float32))
    rows_ref[0:1] = column_sum(grad_in)
    rows_ref[1:2] = column_sum(grad_in * normed)
    grad_source_ref[...] = jnp.where(
        live,
        grad_middle_ref[...] + norm_back(normed, inverse, grad_in * (1.0 + mod_ref[1:2])),
        0.0,
    )


def pair_products(
    chunk, mine_ref, left_ref, left_other_ref, right_ref, right_other_ref, keep_ref, send_ref
):
    total = contract(left_ref[0], right_ref[0], 0, 0) + contract(
        left_other_ref[0], right_other_ref[0], 0, 0
    )
    for start in range(0, total.shape[0] // 2, chunk):
        low = total[2 * start : 2 * start + chunk]
        high = total[2 * start + chunk : 2 * start + 2 * chunk]
        mine = mine_ref[0] == 1
        keep_ref[0, start : start + chunk] = jnp.where(mine, high, low)
        send_ref[0, start : start + chunk] = jnp.where(mine, low, high).astype(jnp.bfloat16)


def plain_products(left_ref, left_other_ref, right_ref, right_other_ref, out_ref):
    out_ref[0] = contract(left_ref[0], right_ref[0], 0, 0) + contract(
        left_other_ref[0], right_other_ref[0], 0, 0
    )


def struct(shape, dtype):
    return jax.ShapeDtypeStruct(shape, dtype)


VMEM = pl.BlockSpec(memory_space=pltpu.VMEM)
SMEM = pl.BlockSpec(memory_space=pltpu.SMEM)


def resident(shape):
    zeros = (0,) * len(shape)
    return pl.BlockSpec(shape, lambda step: zeros)


def run_attention_forward(order, place, source, modulation, offsets, attn_w, attn_w_other):
    seqlen, features = source.shape
    return pl.pallas_call(
        functools.partial(attention_forward, order),
        name="attention_forward",
        out_shape=(
            struct((3, seqlen, features), jnp.bfloat16),
            struct((3, seqlen, features), jnp.bfloat16),
            struct((seqlen, features), jnp.float32),
            struct((seqlen, features), jnp.float32),
        ),
        in_specs=[SMEM] + [VMEM] * 5,
        out_specs=(VMEM,) * 4,
        compiler_params=pltpu.CompilerParams(vmem_limit_bytes=24 << 20),
        cost_estimate=pl.CostEstimate(
            flops=8 * seqlen * features * features + 8 * HEADS * seqlen * seqlen * 128,
            bytes_accessed=attn_w.size * 4 + source.size * 20,
            transcendentals=2 * HEADS * seqlen * seqlen,
        ),
    )(place, source, modulation, offsets, attn_w, attn_w_other)


def run_mlp(mlp_orders, place, lefts, middle, attn_out, upstream, modulation, offsets, up_ws, down_ws):
    seqlen, features = middle.shape
    chips, steps, rows, _ = up_ws[0].shape
    half = features // 2
    whole = (seqlen, features)
    return pl.pallas_call(
        functools.partial(mlp_both_ways, *mlp_orders),
        name="mlp_both_ways",
        grid=(steps,),
        out_shape=(
            struct(whole, jnp.bfloat16),
            struct((steps,) + whole, jnp.bfloat16),
            struct((steps + 1, seqlen, half), jnp.bfloat16),
            struct((steps + 1, seqlen, half), jnp.bfloat16),
            struct(whole, jnp.float32),
            struct(whole, jnp.bfloat16),
            struct(offsets.shape, jnp.float32),
        ),
        in_specs=[
            SMEM,
            pl.BlockSpec((1,) + whole, lambda step: (2, 0, 0)),
            resident(whole),
            resident(whole),
            resident(whole),
            resident(modulation.shape),
            resident(offsets.shape),
        ]
        + [pl.BlockSpec((chips, 1, rows, half), lambda step: (0, step, 0, 0))] * 4,
        out_specs=(
            resident(whole),
            pl.BlockSpec((1,) + whole, lambda step: (step, 0, 0)),
            resident((steps + 1, seqlen, half)),
            resident((steps + 1, seqlen, half)),
            resident(whole),
            resident(whole),
            resident(offsets.shape),
        ),
        scratch_shapes=[
            pltpu.VMEM(whole, jnp.float32),
            pltpu.VMEM(whole, jnp.float32),
            pltpu.VMEM(whole, jnp.bfloat16),
        ],
        compiler_params=pltpu.CompilerParams(vmem_limit_bytes=28 << 20),
        cost_estimate=pl.CostEstimate(
            flops=8 * seqlen * features * features * steps,
            bytes_accessed=up_ws[0].size * 8 + seqlen * features * 40,
            transcendentals=seqlen * features * steps,
        ),
    )(place, lefts, middle, attn_out, upstream, modulation, offsets, *up_ws, *down_ws)


def run_attention_backward(
    order, place, source, modulation, attn_w, attn_w_other, qkv, grad_middle, grad_attn, rows
):
    seqlen, features = source.shape
    half = features // 2
    return pl.pallas_call(
        functools.partial(attention_backward, order),
        name="attention_backward",
        out_shape=(
            struct((seqlen, features), jnp.float32),
            struct((4, seqlen, half), jnp.bfloat16),
            struct((4, seqlen, half), jnp.bfloat16),
            struct(rows.shape, jnp.float32),
        ),
        in_specs=[SMEM] + [VMEM] * 8,
        out_specs=(VMEM,) * 4,
        scratch_shapes=[
            pltpu.VMEM((3, seqlen, features), jnp.bfloat16),
            pltpu.VMEM((seqlen, features), jnp.bfloat16),
        ],
        compiler_params=pltpu.CompilerParams(vmem_limit_bytes=24 << 20),
        cost_estimate=pl.CostEstimate(
            flops=8 * seqlen * features * features + 20 * HEADS * seqlen * seqlen * 128,
            bytes_accessed=attn_w.size * 4 + source.size * 24,
            transcendentals=2 * HEADS * seqlen * seqlen,
        ),
    )(place, source, modulation, attn_w, attn_w_other, qkv, grad_middle, grad_attn, rows)


def run_products(lefts, lefts_other, rights, rights_other, left_at, right_at, count, mine, chunk):
    _, seqlen, features = lefts.shape
    width = rights.shape[-1]
    left_spec = pl.BlockSpec((1, seqlen, features), lambda step: (left_at(step), 0, 0))
    right_spec = pl.BlockSpec((1, seqlen, width), lambda step: (right_at(step), 0, 0))
    specs = [left_spec, left_spec, right_spec, right_spec]
    cost = pl.CostEstimate(
        flops=4 * count * seqlen * features * width,
        bytes_accessed=count * features * width * 6,
        transcendentals=0,
    )
    if chunk % 16:
        total = pl.pallas_call(
            plain_products,
            name="plain_products",
            grid=(count,),
            out_shape=struct((count, features, width), jnp.float32),
            in_specs=specs,
            out_specs=pl.BlockSpec((1, features, width), lambda step: (step, 0, 0)),
            cost_estimate=cost,
        )(lefts, lefts_other, rights, rights_other)
        keep, send = split_bit(
            total.reshape(count, features // (2 * chunk), 2, chunk, width), mine, 2, jnp.bfloat16
        )
        shape = (count, features // 2, width)
        return keep.reshape(shape), send.reshape(shape)
    half_spec = pl.BlockSpec((1, features // 2, width), lambda step: (step, 0, 0))
    return pl.pallas_call(
        functools.partial(pair_products, chunk),
        name="pair_products",
        grid=(count,),
        out_shape=(
            struct((count, features // 2, width), jnp.float32),
            struct((count, features // 2, width), jnp.bfloat16),
        ),
        in_specs=[SMEM] + specs,
        out_specs=(half_spec, half_spec),
        cost_estimate=cost,
    )(mine[None], lefts, lefts_other, rights, rights_other)


def orthogonalize(block_ref, out_ref):
    values = block_ref[...].astype(jnp.float32)
    scaled = (values / (jnp.sqrt(jnp.sum(values * values)) + 1e-07)).astype(jnp.bfloat16)
    for _ in range(NS_ITERS):
        gram = contract(scaled, scaled, 1, 1).astype(jnp.bfloat16)
        square = contract(gram, gram, 1, 0)
        mixed = (COEF_SECOND * gram.astype(jnp.float32) + COEF_THIRD * square).astype(jnp.bfloat16)
        scaled = (
            COEF_FIRST * scaled.astype(jnp.float32) + contract(mixed, scaled, 1, 0)
        ).astype(jnp.bfloat16)
    out_ref[...] = scaled


def run_orthogonalize(block):
    return pl.pallas_call(
        orthogonalize,
        name="orthogonalize",
        out_shape=struct(block.shape, block.dtype),
        in_specs=[VMEM],
        out_specs=VMEM,
        compiler_params=pltpu.CompilerParams(vmem_limit_bytes=24 << 20),
        cost_estimate=pl.CostEstimate(
            flops=6 * NS_ITERS * block.shape[0] ** 3,
            bytes_accessed=4 * block.size,
            transcendentals=0,
        ),
    )(block)


def all_to_all(values):
    return lax.all_to_all(values, "dp", split_axis=0, concat_axis=0, tiled=True)


def to_all(row):
    devices = lax.axis_size("dp")
    return all_to_all(jnp.broadcast_to(row[None], (devices,) + row.shape))


def on_device(latents, conditioning, cotangent, weights, biases, momenta, bias_momenta, counts):
    _, seqlen, features = latents.shape
    block_count, share, _ = weights.shape
    hidden_blocks = (block_count - 10) // 2
    bias_count = biases.shape[0]
    devices = lax.axis_size("dp")
    myself = lax.axis_index("dp")
    core = bit_of(myself, 0)
    bits = index_bits(devices)
    orders = colour_orders(devices)
    ranks = jnp.arange(devices, dtype=jnp.int32)
    live_here = jnp.sum(jnp.where(ranks == myself, counts, 0)) > 0

    lowered = weights.astype(jnp.bfloat16)
    ada_w = lowered[:ADA]
    condition = conditioning[0].astype(jnp.float32)
    silu_cond = jax.nn.silu(condition).astype(jnp.bfloat16)

    half = features // 2
    rest = lowered[ADA:]
    columns_mine = lax.dynamic_slice_in_dim(rest, core * half, half, 2)
    columns_other = lax.dynamic_slice_in_dim(rest, (1 - core) * half, half, 2)
    columns_other = flip(columns_other, 0)
    chip_rows = jnp.where(
        core == 1,
        jnp.concatenate([columns_other, columns_mine], axis=1),
        jnp.concatenate([columns_mine, columns_other], axis=1),
    )
    bounds = [0, 10 - ADA, 10 - ADA + hidden_blocks, block_count - ADA]
    stages = bits - 1
    small_all = to_all(
        jnp.concatenate([silu_cond, biases.astype(jnp.bfloat16).reshape(-1)])
    )

    def modulations(small_all):
        silu_rows = lax.dynamic_slice_in_dim(small_all[:, :features], myself * share, share, 1)
        mod_parts = product("ld,kde->lke", silu_rows, ada_w).reshape(devices, ADA * features)
        return small_all, silu_rows, all_to_all(mod_parts)

    groups, (small_all, silu_rows, mod_sums) = gather_all(
        [chip_rows[low:high] for low, high in zip(bounds[:-1], bounds[1:])],
        [tuple(reversed(order)) for order in orders],
        myself,
        small_all,
        modulations,
    )
    offsets = (
        small_all[:, features:]
        .reshape(devices, bias_count, share)
        .transpose(1, 0, 2)
        .reshape(bias_count, features)
        .astype(jnp.float32)
    )
    modulation = jnp.sum(mod_sums, axis=0).reshape(ADA, features) + offsets[:ADA]
    rows = 2 * share
    held_orders = [tuple(reversed(order)) for order in orders]
    pairs = []
    for index, order in enumerate(held_orders):
        group = groups[index].reshape(devices // 2, -1, rows, half)
        if rows % 16:
            group = jnp.stack([group[place] for place in chunk_places(order)], axis=1)
            group = group.reshape(1, -1, features, half)
            held_orders[index] = ()
        pairs.append((group, flip(group, 0)))
    attn_ws, up_ws, down_ws = pairs

    place = jnp.stack([core, live_here.astype(jnp.int32)]).astype(jnp.int32)
    lefts, qkv, attn_out, middle = run_attention_forward(
        held_orders[0], place, latents[0], modulation, offsets, *attn_ws
    )
    lefts_other = flip(lefts, 0)
    output, hidden, mlp_keep, mlp_send, grad_middle, grad_attn, rows = run_mlp(
        held_orders[1:], place, lefts, middle, attn_out, cotangent[0], modulation, offsets, up_ws, down_ws
    )
    hidden_other = flip(hidden, 0)
    mlp_other = flip(mlp_send, 0)

    def spread(mats, count):
        return mats.reshape((mats.shape[0],) + (2,) * count + (2 * share, half))

    def products(left, left_other, right, right_other, left_at, right_at, count, order):
        return run_products(
            left,
            left_other,
            right,
            right_other,
            left_at,
            right_at,
            count,
            bit_of(myself, order[0]),
            share << order[0],
        )

    down_halves = products(
        hidden, hidden_other, mlp_keep, mlp_other, lambda b: b, lambda b: 0, hidden_blocks, orders[0]
    )
    up_halves = products(
        lefts, lefts_other, mlp_keep, mlp_other, lambda b: 2, lambda b: b + 1, hidden_blocks, orders[1]
    )
    input_grad, attn_keep, attn_send, grad_offsets = run_attention_backward(
        held_orders[0], place, latents[0], modulation, *attn_ws, qkv, grad_middle, grad_attn, rows
    )
    attn_other = flip(attn_send, 0)
    attn_halves = products(
        lefts, lefts_other, attn_keep, attn_other, lambda b: b // 3, lambda b: b, 4, orders[2]
    )

    grad_mod_b = grad_offsets[:ADA].astype(jnp.bfloat16).reshape(-1)
    by_holder = (
        grad_offsets.reshape(bias_count, devices, share)
        .transpose(1, 0, 2)
        .reshape(devices, bias_count * share)
    )
    coarse = lax.reduce_precision(by_holder, 8, 7)
    mod_and_offsets = jnp.concatenate(
        [
            jnp.broadcast_to(grad_mod_b[None], (devices, ADA * features)),
            coarse.astype(jnp.bfloat16),
            (by_holder - coarse).astype(jnp.bfloat16),
        ],
        axis=1,
    )
    mod_and_offsets = all_to_all(mod_and_offsets)

    def conditioning_grads(mod_and_offsets):
        mod_all = mod_and_offsets[:, : ADA * features].reshape(devices, ADA, features)
        silu_parts = product("lke,kde->ld", mod_all, ada_w)
        return mod_and_offsets, mod_all, all_to_all(silu_parts)

    sums, (mod_and_offsets, mod_all, grad_silu) = scatter_all(
        [attn_halves, up_halves, down_halves],
        [orders[2], orders[1], orders[0]],
        myself,
        1,
        spread,
        {stages - 1: lambda _: conditioning_grads(mod_and_offsets)},
    )
    chip_rows = jnp.concatenate(sums, axis=0)
    rows_mine = lax.dynamic_slice_in_dim(chip_rows, core * share, share, 1)
    rows_other = flip(lax.dynamic_slice_in_dim(chip_rows, (1 - core) * share, share, 1), 0)
    rest_share = jnp.where(
        core == 1,
        jnp.concatenate([rows_other, rows_mine], axis=2),
        jnp.concatenate([rows_mine, rows_other], axis=2),
    )

    ada_share = product("ld,lke->kde", silu_rows, mod_all)
    offset_share = jnp.sum(
        mod_and_offsets[:, ADA * features :]
        .astype(jnp.float32)
        .reshape(devices * 2, bias_count, share),
        axis=0,
    )

    grad_scale = lax.rsqrt((seqlen * jnp.sum(counts)).astype(jnp.float32))
    weight_grads = jnp.concatenate([ada_share, rest_share], axis=0) * grad_scale
    bias_grads = offset_share * grad_scale
    new_momenta = BETA_WEIGHT * momenta + weight_grads
    new_bias_momenta = BETA_BIAS * bias_momenta + bias_grads
    new_biases = biases - RATE_BIAS * new_bias_momenta

    outgoing = jnp.pad(
        new_momenta.astype(jnp.bfloat16), ((0, devices - block_count), (0, 0), (0, 0))
    )
    ortho = run_orthogonalize(all_to_all(outgoing).reshape(features, features))
    ortho_local = all_to_all(ortho.reshape(devices, share, features))[:block_count]
    silu_back = jax.vjp(jax.nn.silu, condition)[1]
    cond_grad = silu_back(grad_silu.reshape(features))[0] * seqlen ** (-0.5)
    new_weights = weights - RATE_WEIGHT * ortho_local.astype(jnp.float32)
    cond_grad = jnp.where(live_here, cond_grad, jnp.zeros_like(cond_grad))[None]
    return (
        output[None],
        input_grad[None],
        cond_grad,
        weight_grads,
        bias_grads,
        new_weights,
        new_momenta,
        new_biases,
        new_bias_momenta,
    )


def solution(mesh):
    return jax.shard_map(
        on_device,
        mesh=mesh,
        in_specs=(
            P("dp", None, None),
            P("dp", None),
            P("dp", None, None),
            P(None, "dp", None),
            P(None, "dp"),
            P(None, "dp", None),
            P(None, "dp"),
            P(),
        ),
        out_specs=(
            P("dp", None, None),
            P("dp", None, None),
            P("dp", None),
            P(None, "dp", None),
            P(None, "dp"),
            P(None, "dp", None),
            P(None, "dp", None),
            P(None, "dp"),
            P(None, "dp"),
        ),
        check_vma=False,
    )
```

```python
import functools

import jax
import jax.numpy as jnp
from jax import lax
from jax.experimental import pallas as pl
from jax.experimental.pallas import tpu as pltpu
from jax.sharding import PartitionSpec as P


HEADS = 12
NS_ITERS = 2
ADA = 6
COLOURS = 3

COEF_FIRST = 3.4445
COEF_SECOND = -4.775
COEF_THIRD = 2.0315
BETA_WEIGHT = 0.95
BETA_BIAS = 0.9
RATE_WEIGHT = 1.0
RATE_BIAS = 0.1
NORM_EPS = 1e-06


def product(spec, left, right):
    return jnp.einsum(spec, left, right, preferred_element_type=jnp.float32)


def flip(values, bit):
    devices = lax.axis_size("dp")
    return lax.ppermute(values, "dp", [(i, i ^ (1 << bit)) for i in range(devices)])


def bit_of(myself, bit):
    return (myself >> bit) & 1


def joined(values, other, taken, axis):
    return jnp.where(
        taken == 1, jnp.stack([other, values], axis), jnp.stack([values, other], axis)
    )


def gather_all(groups, orders, myself, first_too, last_too):
    carried = first_too
    for stage in range(len(orders[0])):
        others = [flip(group, order[stage]) for group, order in zip(groups, orders)]
        if stage == len(orders[0]) - 1:
            carried = last_too(carried)
        if stage in (0, len(orders[0]) - 1):
            others[-1], carried = lax.optimization_barrier((others[-1], carried))
        for index, order in enumerate(orders):
            bit = order[stage]
            groups[index] = joined(groups[index], others[index], bit_of(myself, bit), 0)
    return groups, carried


def gather_step(values, order, bit, myself):
    held = order[: order.index(bit)]
    position = 1 + sum(1 for before in held if before > bit)
    return joined(values, flip(values, bit), bit_of(myself, bit), position)


def flip_by_core(values, first_bit, second_bit):
    devices = lax.axis_size("dp")
    return lax.ppermute(
        values, "dp", [(i, i ^ (1 << (second_bit if i & 1 else first_bit))) for i in range(devices)]
    )


def corner_rows(near, far, order, myself):
    high, low = bit_of(myself, order[-2]), bit_of(myself, order[-1])
    core = bit_of(myself, 0)
    first, second = jnp.where(core == 1, low, high), jnp.where(core == 1, high, low)
    axis = len(order) - 1
    pairs = [
        joined(pair[0], pair[1], first, axis) for pair in (near, far)
    ]
    by_first = joined(pairs[0], pairs[1], second, axis)
    return jnp.where(core == 1, by_first, jnp.swapaxes(by_first, axis, axis + 1))


def split_bit(values, mine, position, sent_as):
    send = lax.dynamic_index_in_dim(values, 1 - mine, position, keepdims=False)
    keep = lax.dynamic_index_in_dim(values, mine, position, keepdims=False)
    return keep, send.astype(sent_as)


def scatter_all(halves, orders, myself, axis, spread, between):
    left = [sorted(order, reverse=True) for order in orders]
    carried = None
    totals = []
    for stage in range(len(orders[0])):
        others = [flip(send, order[stage]) for (_, send), order in zip(halves, orders)]
        if stage in between:
            carried = between[stage](carried)
            others[-1], carried = lax.optimization_barrier((others[-1], carried))
        totals = [
            keep + other.astype(jnp.float32) for (keep, _), other in zip(halves, others)
        ]
        for index, order in enumerate(orders):
            left[index].remove(order[stage])
            if stage == 0:
                totals[index] = spread(totals[index], len(left[index]))
            if left[index]:
                bit = order[stage + 1]
                position = axis + left[index].index(bit)
                halves[index] = split_bit(
                    totals[index], bit_of(myself, bit), position, jnp.bfloat16
                )
    return totals, carried


def index_bits(devices):
    return devices.bit_length() - 1


def colour_orders(devices):
    chip_bits = list(range(1, index_bits(devices)))
    rest, last = chip_bits[:-1], chip_bits[-1:]
    shifts = [(colour * len(rest)) // COLOURS for colour in range(COLOURS)]
    return [tuple(rest[shift:] + rest[:shift] + last) for shift in shifts]


def contract(left, right, left_dim, right_dim):
    return lax.dot_general(
        left, right, (((left_dim,), (right_dim,)), ((), ())), preferred_element_type=jnp.float32
    )


def layer_norm(stream):
    centred = stream - jnp.mean(stream, axis=-1, keepdims=True)
    inverse = lax.rsqrt(jnp.mean(centred * centred, axis=-1, keepdims=True) + NORM_EPS)
    return (centred * inverse, inverse)


def norm_back(normed, inverse, upstream):
    return inverse * (
        upstream
        - jnp.mean(upstream, axis=-1, keepdims=True)
        - normed * jnp.mean(upstream * normed, axis=-1, keepdims=True)
    )


def column_sum(values):
    return jnp.sum(values, axis=0, keepdims=True)


def scores_of(query, keys, width):
    return contract(query, keys, 1, 1) * width ** (-0.5)


def chunk_places(order):
    count = len(order)
    return [
        sum(((chip >> (bit - 1)) & 1) << place for place, bit in enumerate(order))
        for chip in range(1 << count)
    ]


def whole_weight(mine_ref, other_ref, index, core, order):
    places = chunk_places(order) if order else [0]
    mine, other = [
        jnp.concatenate([ref[place, index] for place in places], axis=0)
        for ref in (mine_ref, other_ref)
    ]
    return jnp.concatenate(
        [jnp.where(core == 1, other, mine), jnp.where(core == 1, mine, other)], axis=1
    )


def attention_forward(
    order,
    place_ref,
    source_ref,
    mod_ref,
    offsets_ref,
    mine_ref,
    other_ref,
    lefts_ref,
    qkv_ref,
    attn_ref,
    middle_ref,
):
    core = place_ref[0]
    seqlen, features = source_ref.shape
    width = features // HEADS
    stream = source_ref[...].astype(jnp.float32)
    normed, _ = layer_norm(stream)
    attn_input = (normed * (1.0 + mod_ref[1:2]) + mod_ref[0:1]).astype(jnp.bfloat16)
    lefts_ref[0] = attn_input
    qkv_ref[0] = (contract(attn_input, whole_weight(mine_ref, other_ref, 0, core, order), 1, 0) + offsets_ref[6:7]).astype(
        jnp.bfloat16
    )
    qkv_ref[1] = contract(attn_input, whole_weight(mine_ref, other_ref, 1, core, order), 1, 0).astype(jnp.bfloat16)
    qkv_ref[2] = (contract(attn_input, whole_weight(mine_ref, other_ref, 2, core, order), 1, 0) + offsets_ref[7:8]).astype(
        jnp.bfloat16
    )
    first = lax.broadcasted_iota(jnp.int32, (seqlen, 2 * width), 1) < width
    for pair in range(HEADS // 2):
        columns = slice(2 * width * pair, 2 * width * (pair + 1))
        query, keys, values = qkv_ref[0, :, columns], qkv_ref[1, :, columns], qkv_ref[2, :, columns]
        halves = []
        for mask in (first, jnp.logical_not(first)):
            scores = scores_of(jnp.where(mask, query, jnp.zeros_like(query)), keys, width)
            log_total = jnp.log(jnp.sum(jnp.exp(scores), axis=-1, keepdims=True))
            probs = jnp.exp(scores - log_total).astype(jnp.bfloat16)
            halves.append(contract(probs, values, 1, 0))
        lefts_ref[1, :, columns] = jnp.where(first, *halves).astype(jnp.bfloat16)
    attn_out = contract(lefts_ref[1], whole_weight(mine_ref, other_ref, 3, core, order), 1, 0) + offsets_ref[8:9]
    attn_ref[...] = attn_out
    middle = stream + mod_ref[2:3] * attn_out
    middle_ref[...] = middle
    normed_two, _ = layer_norm(middle)
    lefts_ref[2] = (normed_two * (1.0 + mod_ref[4:5]) + mod_ref[3:4]).astype(jnp.bfloat16)


def split_columns(values, core):
    width = values.shape[-1] // 2
    low, high = values[:, :width], values[:, width:]
    return (jnp.where(core == 1, high, low), jnp.where(core == 1, low, high))


def mlp_both_ways(
    up_order,
    down_order,
    place_ref,
    lefts_ref,
    middle_ref,
    attn_ref,
    upstream_ref,
    mod_ref,
    offsets_ref,
    up_ref,
    up_other_ref,
    down_ref,
    down_other_ref,
    output_ref,
    hidden_ref,
    keep_ref,
    send_ref,
    grad_middle_ref,
    grad_attn_ref,
    rows_ref,
    total_ref,
    grad_total_ref,
    grad_mlp_ref,
):
    step = pl.program_id(0)
    last = pl.num_programs(0) - 1
    core, live = place_ref[0], place_ref[1] > 0
    scale = 0.7978845608028654

    @pl.when(step == 0)
    def _():
        total_ref[...] = jnp.zeros_like(total_ref)
        grad_total_ref[...] = jnp.zeros_like(grad_total_ref)
        grad_mlp = jnp.where(live, upstream_ref[...].astype(jnp.float32) * mod_ref[5:6], 0.0)
        grad_mlp_b = grad_mlp.astype(jnp.bfloat16)
        grad_mlp_ref[...] = grad_mlp_b
        keep_ref[0], send_ref[0] = split_columns(grad_mlp_b, core)
        rows_ref[...] = jnp.zeros_like(rows_ref)
        rows_ref[pl.ds(10 + last, 1)] = column_sum(grad_mlp)

    up_w = whole_weight(up_ref, up_other_ref, 0, core, up_order)
    down_w = whole_weight(down_ref, down_other_ref, 0, core, down_order)
    before = contract(lefts_ref[0], up_w, 1, 0) + offsets_ref[pl.ds(9 + step, 1)]
    square = before * before
    bend = jnp.tanh(scale * (before + 0.044715 * square * before))
    hidden = (0.5 * before * (1.0 + bend)).astype(jnp.bfloat16)
    hidden_ref[0] = hidden
    total_ref[...] += contract(hidden, down_w, 1, 0)
    slope = 0.5 * (1.0 + bend) + 0.5 * before * (1.0 - bend * bend) * scale * (
        1.0 + 3.0 * 0.044715 * square
    )
    grad_pre = jnp.where(live, contract(grad_mlp_ref[...], down_w, 1, 1) * slope, 0.0)
    grad_pre_b = grad_pre.astype(jnp.bfloat16)
    keep_ref[step + 1], send_ref[step + 1] = split_columns(grad_pre_b, core)
    rows_ref[pl.ds(9 + step, 1)] = column_sum(grad_pre)
    grad_total_ref[...] += contract(grad_pre_b, up_w, 1, 1)

    @pl.when(step == last)
    def _():
        middle = middle_ref[...]
        grad_out = upstream_ref[...].astype(jnp.float32)
        mlp_out = total_ref[...] + offsets_ref[pl.ds(10 + last, 1)]
        output = middle + mod_ref[5:6] * mlp_out
        output_ref[...] = jnp.where(live, output, 0.0).astype(jnp.bfloat16)
        rows_ref[5:6] = jnp.where(live, column_sum(grad_out * mlp_out), 0.0)
        normed, inverse = layer_norm(middle)
        grad_in = grad_total_ref[...]
        rows_ref[3:4] = column_sum(grad_in)
        rows_ref[4:5] = column_sum(grad_in * normed)
        grad_middle = grad_out + norm_back(normed, inverse, grad_in * (1.0 + mod_ref[4:5]))
        grad_middle = jnp.where(live, grad_middle, 0.0)
        grad_middle_ref[...] = grad_middle
        rows_ref[2:3] = column_sum(grad_middle * attn_ref[...])
        grad_attn = grad_middle * mod_ref[2:3]
        grad_attn_ref[...] = grad_attn.astype(jnp.bfloat16)
        rows_ref[8:9] = column_sum(grad_attn)


def attention_backward(
    order,
    place_ref,
    source_ref,
    mod_ref,
    mine_ref,
    other_ref,
    qkv_ref,
    grad_middle_ref,
    grad_attn_ref,
    rows_in_ref,
    grad_source_ref,
    keep_ref,
    send_ref,
    rows_ref,
    grads_ref,
    context_ref,
):
    seqlen, features = source_ref.shape
    width = features // HEADS
    core, live = place_ref[0], place_ref[1] > 0
    rows_ref[...] = rows_in_ref[...]
    grad_attn = grad_attn_ref[...]
    keep_ref[3], send_ref[3] = split_columns(grad_attn, core)
    context_ref[...] = contract(
        grad_attn, whole_weight(mine_ref, other_ref, 3, core, order), 1, 1
    ).astype(jnp.bfloat16)
    first = lax.broadcasted_iota(jnp.int32, (seqlen, 2 * width), 1) < width
    for pair in range(HEADS // 2):
        columns = slice(2 * width * pair, 2 * width * (pair + 1))
        query, keys, values = qkv_ref[0, :, columns], qkv_ref[1, :, columns], qkv_ref[2, :, columns]
        upstream = context_ref[:, columns]
        parts = []
        for mask in (first, jnp.logical_not(first)):
            scores = scores_of(jnp.where(mask, query, jnp.zeros_like(query)), keys, width)
            log_total = jnp.log(jnp.sum(jnp.exp(scores), axis=-1, keepdims=True))
            probs = jnp.exp(scores - log_total)
            grad_values = contract(probs.astype(jnp.bfloat16), upstream, 0, 0)
            grad_probs = contract(
                jnp.where(mask, upstream, jnp.zeros_like(upstream)), values, 1, 1
            )
            row_dot = jnp.sum(probs * grad_probs, axis=-1, keepdims=True)
            grad_scores = (probs * (grad_probs - row_dot) * width ** (-0.5)).astype(jnp.bfloat16)
            parts.append(
                (
                    contract(grad_scores, keys, 1, 0),
                    contract(grad_scores, query, 0, 0),
                    grad_values,
                )
            )
        for index in range(3):
            merged = jnp.where(live, jnp.where(first, parts[0][index], parts[1][index]), 0.0)
            grads_ref[index, :, columns] = merged.astype(jnp.bfloat16)
            if index != 1:
                row = 6 if index == 0 else 7
                rows_ref[row : row + 1, columns] = column_sum(merged)
    grad_in = jnp.zeros((seqlen, features), jnp.float32)
    for index in range(3):
        grads = grads_ref[index]
        keep_ref[index], send_ref[index] = split_columns(grads, core)
        grad_in += contract(grads, whole_weight(mine_ref, other_ref, index, core, order), 1, 1)
    normed, inverse = layer_norm(source_ref[...].astype(jnp.float32))
    rows_ref[0:1] = column_sum(grad_in)
    rows_ref[1:2] = column_sum(grad_in * normed)
    grad_source_ref[...] = jnp.where(
        live,
        grad_middle_ref[...] + norm_back(normed, inverse, grad_in * (1.0 + mod_ref[1:2])),
        0.0,
    )


def pair_products(
    chunk, mine_ref, left_ref, left_other_ref, right_ref, right_other_ref, keep_ref, send_ref
):
    total = contract(left_ref[0], right_ref[0], 0, 0) + contract(
        left_other_ref[0], right_other_ref[0], 0, 0
    )
    for start in range(0, total.shape[0] // 2, chunk):
        low = total[2 * start : 2 * start + chunk]
        high = total[2 * start + chunk : 2 * start + 2 * chunk]
        mine = mine_ref[0] == 1
        keep_ref[0, start : start + chunk] = jnp.where(mine, high, low)
        send_ref[0, start : start + chunk] = jnp.where(mine, low, high).astype(jnp.bfloat16)


def plain_products(left_ref, left_other_ref, right_ref, right_other_ref, out_ref):
    out_ref[0] = contract(left_ref[0], right_ref[0], 0, 0) + contract(
        left_other_ref[0], right_other_ref[0], 0, 0
    )


def struct(shape, dtype):
    return jax.ShapeDtypeStruct(shape, dtype)


VMEM = pl.BlockSpec(memory_space=pltpu.VMEM)
SMEM = pl.BlockSpec(memory_space=pltpu.SMEM)


def resident(shape):
    zeros = (0,) * len(shape)
    return pl.BlockSpec(shape, lambda step: zeros)


def run_attention_forward(order, place, source, modulation, offsets, attn_w, attn_w_other):
    seqlen, features = source.shape
    return pl.pallas_call(
        functools.partial(attention_forward, order),
        name="attention_forward",
        out_shape=(
            struct((3, seqlen, features), jnp.bfloat16),
            struct((3, seqlen, features), jnp.bfloat16),
            struct((seqlen, features), jnp.float32),
            struct((seqlen, features), jnp.float32),
        ),
        in_specs=[SMEM] + [VMEM] * 5,
        out_specs=(VMEM,) * 4,
        compiler_params=pltpu.CompilerParams(vmem_limit_bytes=24 << 20),
        cost_estimate=pl.CostEstimate(
            flops=8 * seqlen * features * features + 8 * HEADS * seqlen * seqlen * 128,
            bytes_accessed=attn_w.size * 4 + source.size * 20,
            transcendentals=2 * HEADS * seqlen * seqlen,
        ),
    )(place, source, modulation, offsets, attn_w, attn_w_other)


def run_mlp(mlp_orders, place, lefts, middle, attn_out, upstream, modulation, offsets, up_ws, down_ws):
    seqlen, features = middle.shape
    chips, steps, rows, _ = up_ws[0].shape
    half = features // 2
    whole = (seqlen, features)
    return pl.pallas_call(
        functools.partial(mlp_both_ways, *mlp_orders),
        name="mlp_both_ways",
        grid=(steps,),
        out_shape=(
            struct(whole, jnp.bfloat16),
            struct((steps,) + whole, jnp.bfloat16),
            struct((steps + 1, seqlen, half), jnp.bfloat16),
            struct((steps + 1, seqlen, half), jnp.bfloat16),
            struct(whole, jnp.float32),
            struct(whole, jnp.bfloat16),
            struct(offsets.shape, jnp.float32),
        ),
        in_specs=[
            SMEM,
            pl.BlockSpec((1,) + whole, lambda step: (2, 0, 0)),
            resident(whole),
            resident(whole),
            resident(whole),
            resident(modulation.shape),
            resident(offsets.shape),
        ]
        + [pl.BlockSpec((chips, 1, rows, half), lambda step: (0, step, 0, 0))] * 4,
        out_specs=(
            resident(whole),
            pl.BlockSpec((1,) + whole, lambda step: (step, 0, 0)),
            resident((steps + 1, seqlen, half)),
            resident((steps + 1, seqlen, half)),
            resident(whole),
            resident(whole),
            resident(offsets.shape),
        ),
        scratch_shapes=[
            pltpu.VMEM(whole, jnp.float32),
            pltpu.VMEM(whole, jnp.float32),
            pltpu.VMEM(whole, jnp.bfloat16),
        ],
        compiler_params=pltpu.CompilerParams(vmem_limit_bytes=28 << 20),
        cost_estimate=pl.CostEstimate(
            flops=8 * seqlen * features * features * steps,
            bytes_accessed=up_ws[0].size * 8 + seqlen * features * 40,
            transcendentals=seqlen * features * steps,
        ),
    )(place, lefts, middle, attn_out, upstream, modulation, offsets, *up_ws, *down_ws)


def run_attention_backward(
    order, place, source, modulation, attn_w, attn_w_other, qkv, grad_middle, grad_attn, rows
):
    seqlen, features = source.shape
    half = features // 2
    return pl.pallas_call(
        functools.partial(attention_backward, order),
        name="attention_backward",
        out_shape=(
            struct((seqlen, features), jnp.float32),
            struct((4, seqlen, half), jnp.bfloat16),
            struct((4, seqlen, half), jnp.bfloat16),
            struct(rows.shape, jnp.float32),
        ),
        in_specs=[SMEM] + [VMEM] * 8,
        out_specs=(VMEM,) * 4,
        scratch_shapes=[
            pltpu.VMEM((3, seqlen, features), jnp.bfloat16),
            pltpu.VMEM((seqlen, features), jnp.bfloat16),
        ],
        compiler_params=pltpu.CompilerParams(vmem_limit_bytes=24 << 20),
        cost_estimate=pl.CostEstimate(
            flops=8 * seqlen * features * features + 20 * HEADS * seqlen * seqlen * 128,
            bytes_accessed=attn_w.size * 4 + source.size * 24,
            transcendentals=2 * HEADS * seqlen * seqlen,
        ),
    )(place, source, modulation, attn_w, attn_w_other, qkv, grad_middle, grad_attn, rows)


def run_products(lefts, lefts_other, rights, rights_other, left_at, right_at, count, mine, chunk):
    _, seqlen, features = lefts.shape
    width = rights.shape[-1]
    left_spec = pl.BlockSpec((1, seqlen, features), lambda step: (left_at(step), 0, 0))
    right_spec = pl.BlockSpec((1, seqlen, width), lambda step: (right_at(step), 0, 0))
    specs = [left_spec, left_spec, right_spec, right_spec]
    cost = pl.CostEstimate(
        flops=4 * count * seqlen * features * width,
        bytes_accessed=count * features * width * 6,
        transcendentals=0,
    )
    if chunk % 16:
        total = pl.pallas_call(
            plain_products,
            name="plain_products",
            grid=(count,),
            out_shape=struct((count, features, width), jnp.float32),
            in_specs=specs,
            out_specs=pl.BlockSpec((1, features, width), lambda step: (step, 0, 0)),
            cost_estimate=cost,
        )(lefts, lefts_other, rights, rights_other)
        keep, send = split_bit(
            total.reshape(count, features // (2 * chunk), 2, chunk, width), mine, 2, jnp.bfloat16
        )
        shape = (count, features // 2, width)
        return keep.reshape(shape), send.reshape(shape)
    half_spec = pl.BlockSpec((1, features // 2, width), lambda step: (step, 0, 0))
    return pl.pallas_call(
        functools.partial(pair_products, chunk),
        name="pair_products",
        grid=(count,),
        out_shape=(
            struct((count, features // 2, width), jnp.float32),
            struct((count, features // 2, width), jnp.bfloat16),
        ),
        in_specs=[SMEM] + specs,
        out_specs=(half_spec, half_spec),
        cost_estimate=cost,
    )(mine[None], lefts, lefts_other, rights, rights_other)


def muon_steps(block):
    values = block.astype(jnp.float32)
    scaled = (values / (jnp.sqrt(jnp.sum(values * values)) + 1e-07)).astype(jnp.bfloat16)
    for _ in range(NS_ITERS):
        gram = contract(scaled, scaled, 1, 1).astype(jnp.bfloat16)
        square = contract(gram, gram, 1, 0)
        mixed = (COEF_SECOND * gram.astype(jnp.float32) + COEF_THIRD * square).astype(jnp.bfloat16)
        scaled = (
            COEF_FIRST * scaled.astype(jnp.float32) + contract(mixed, scaled, 1, 0)
        ).astype(jnp.bfloat16)
    return scaled


def orthogonalize_halves(place_ref, mine_ref, other_ref, out_ref):
    core = place_ref[0]
    mine, other = mine_ref[...], other_ref[...]
    low, high = jnp.where(core == 1, other, mine), jnp.where(core == 1, mine, other)
    scaled = muon_steps(jnp.concatenate([low, high], axis=1))
    out_ref[...] = split_columns(scaled, core)[0]


def orthogonalize_whole(block_ref, out_ref):
    out_ref[0] = muon_steps(block_ref[0])


def muon_cost(count, rows):
    return pl.CostEstimate(
        flops=6 * count * NS_ITERS * rows**3, bytes_accessed=4 * count * rows**2, transcendentals=0
    )


def run_orthogonalize_halves(place, mine, other):
    return pl.pallas_call(
        orthogonalize_halves,
        name="orthogonalize_halves",
        out_shape=struct(mine.shape, mine.dtype),
        in_specs=[SMEM, VMEM, VMEM],
        out_specs=VMEM,
        compiler_params=pltpu.CompilerParams(vmem_limit_bytes=24 << 20),
        cost_estimate=muon_cost(1, mine.shape[0]),
    )(place, mine, other)


def run_orthogonalize_whole(blocks):
    spec = pl.BlockSpec((1,) + blocks.shape[1:], lambda step: (step, 0, 0))
    return pl.pallas_call(
        orthogonalize_whole,
        name="orthogonalize_whole",
        grid=(blocks.shape[0],),
        out_shape=struct(blocks.shape, blocks.dtype),
        in_specs=[spec],
        out_specs=spec,
        compiler_params=pltpu.CompilerParams(vmem_limit_bytes=24 << 20),
        cost_estimate=muon_cost(*blocks.shape[:2]),
    )(blocks)


def all_to_all(values):
    return lax.all_to_all(values, "dp", split_axis=0, concat_axis=0, tiled=True)


def to_all(row):
    devices = lax.axis_size("dp")
    return all_to_all(jnp.broadcast_to(row[None], (devices,) + row.shape))


def on_device(latents, conditioning, cotangent, weights, biases, momenta, bias_momenta, counts):
    _, seqlen, features = latents.shape
    block_count, share, _ = weights.shape
    hidden_blocks = (block_count - 10) // 2
    bias_count = biases.shape[0]
    devices = lax.axis_size("dp")
    myself = lax.axis_index("dp")
    core = bit_of(myself, 0)
    bits = index_bits(devices)
    orders = colour_orders(devices)
    ranks = jnp.arange(devices, dtype=jnp.int32)
    live_here = jnp.sum(jnp.where(ranks == myself, counts, 0)) > 0

    lowered = weights.astype(jnp.bfloat16)
    ada_w = lowered[:ADA]
    condition = conditioning[0].astype(jnp.float32)
    silu_cond = jax.nn.silu(condition).astype(jnp.bfloat16)

    half = features // 2
    rest = lowered[ADA:]
    columns_mine = lax.dynamic_slice_in_dim(rest, core * half, half, 2)
    columns_other = lax.dynamic_slice_in_dim(rest, (1 - core) * half, half, 2)
    columns_other = flip(columns_other, 0)
    chip_rows = jnp.where(
        core == 1,
        jnp.concatenate([columns_other, columns_mine], axis=1),
        jnp.concatenate([columns_mine, columns_other], axis=1),
    )
    bounds = [0, 10 - ADA, 10 - ADA + hidden_blocks, block_count - ADA]
    stages = bits - 1
    small_all = to_all(
        jnp.concatenate([silu_cond, biases.astype(jnp.bfloat16).reshape(-1)])
    )

    def modulations(small_all):
        silu_rows = lax.dynamic_slice_in_dim(small_all[:, :features], myself * share, share, 1)
        mod_parts = product("ld,kde->lke", silu_rows, ada_w).reshape(devices, ADA * features)
        offsets = (
            small_all[:, features:]
            .reshape(devices, bias_count, share)
            .transpose(1, 0, 2)
            .reshape(bias_count, features)
            .astype(jnp.float32)
        )
        return small_all, silu_rows, offsets, all_to_all(mod_parts)

    groups, (small_all, silu_rows, offsets, mod_sums) = gather_all(
        [chip_rows[low:high] for low, high in zip(bounds[:-1], bounds[1:])],
        [tuple(reversed(order)) for order in orders],
        myself,
        small_all,
        modulations,
    )
    modulation = jnp.sum(mod_sums, axis=0).reshape(ADA, features) + offsets[:ADA]
    rows = 2 * share
    held_orders = [tuple(reversed(order)) for order in orders]
    pairs = []
    for index, order in enumerate(held_orders):
        group = groups[index].reshape(devices // 2, -1, rows, half)
        if rows % 16:
            group = jnp.stack([group[place] for place in chunk_places(order)], axis=1)
            group = group.reshape(1, -1, features, half)
            held_orders[index] = ()
        pairs.append((group, flip(group, 0)))
    attn_ws, up_ws, down_ws = pairs

    place = jnp.stack([core, live_here.astype(jnp.int32)]).astype(jnp.int32)
    lefts, qkv, attn_out, middle = run_attention_forward(
        held_orders[0], place, latents[0], modulation, offsets, *attn_ws
    )
    extra = max(0, block_count - devices // 2)
    assert extra % 2 == 0 and extra <= ADA
    main = block_count - extra
    spare = ()
    spare_bits = tuple(reversed(range(1, bits)))
    if extra:
        spare = momenta[:extra].astype(jnp.bfloat16).reshape(2, extra // 2, share, features)
        spare_mine = lax.dynamic_index_in_dim(spare, core, 0, keepdims=False)
        spare_other = flip(lax.dynamic_index_in_dim(spare, 1 - core, 0, keepdims=False), 0)
        spare = joined(spare_mine, spare_other, core, 1).reshape(extra // 2, 2 * share, features)
        lefts, spare = lax.optimization_barrier((lefts, spare))
        spare = gather_step(spare, spare_bits, spare_bits[0], myself)
    lefts_other = flip(lefts, 0)
    output, hidden, mlp_keep, mlp_send, grad_middle, grad_attn, rows = run_mlp(
        held_orders[1:],
        place,
        lefts,
        middle,
        attn_out,
        cotangent[0],
        modulation,
        offsets,
        up_ws,
        down_ws,
    )
    if extra:
        grad_attn, spare = lax.optimization_barrier((grad_attn, spare))
        for bit in spare_bits[1:-2]:
            spare = gather_step(spare, spare_bits, bit, myself)
    hidden_other = flip(hidden, 0)
    mlp_other = flip(mlp_send, 0)

    def spread(mats, count):
        return mats.reshape((mats.shape[0],) + (2,) * count + (2 * share, half))

    def products(left, left_other, right, right_other, left_at, right_at, count, order):
        return run_products(
            left,
            left_other,
            right,
            right_other,
            left_at,
            right_at,
            count,
            bit_of(myself, order[0]),
            share << order[0],
        )

    down_halves = products(
        hidden, hidden_other, mlp_keep, mlp_other, lambda b: b, lambda b: 0, hidden_blocks, orders[0]
    )
    up_halves = products(
        lefts, lefts_other, mlp_keep, mlp_other, lambda b: 2, lambda b: b + 1, hidden_blocks, orders[1]
    )
    input_grad, attn_keep, attn_send, grad_offsets = run_attention_backward(
        held_orders[0], place, latents[0], modulation, *attn_ws, qkv, grad_middle, grad_attn, rows
    )
    if extra:
        attn_send, spare = lax.optimization_barrier((attn_send, spare))
        received = flip_by_core(spare, spare_bits[-2], spare_bits[-1])
        near = jnp.stack([spare, received])
        far = flip_by_core(near, spare_bits[-1], spare_bits[-2])
        spare = corner_rows(near, far, spare_bits, myself)
        spare = spare.reshape(extra // 2, features, features)
    attn_other = flip(attn_send, 0)
    attn_halves = products(
        lefts, lefts_other, attn_keep, attn_other, lambda b: b // 3, lambda b: b, 4, orders[2]
    )

    grad_mod_b = grad_offsets[:ADA].astype(jnp.bfloat16).reshape(-1)
    by_holder = (
        grad_offsets.reshape(bias_count, devices, share)
        .transpose(1, 0, 2)
        .reshape(devices, bias_count * share)
    )
    coarse = lax.reduce_precision(by_holder, 8, 7)
    mod_and_offsets = jnp.concatenate(
        [
            jnp.broadcast_to(grad_mod_b[None], (devices, ADA * features)),
            coarse.astype(jnp.bfloat16),
            (by_holder - coarse).astype(jnp.bfloat16),
        ],
        axis=1,
    )
    mod_and_offsets = all_to_all(mod_and_offsets)

    def conditioning_grads(mod_and_offsets):
        mod_all = mod_and_offsets[:, : ADA * features].reshape(devices, ADA, features)
        silu_parts = product("lke,kde->ld", mod_all, ada_w)
        return mod_and_offsets, mod_all, all_to_all(silu_parts)

    sums, (mod_and_offsets, mod_all, grad_silu) = scatter_all(
        [attn_halves, up_halves, down_halves],
        [orders[2], orders[1], orders[0]],
        myself,
        1,
        spread,
        {stages - 1: lambda _: conditioning_grads(mod_and_offsets)},
    )
    chip_rows = jnp.concatenate(sums, axis=0)
    rows_mine = lax.dynamic_slice_in_dim(chip_rows, core * share, share, 1)
    rows_other = flip(lax.dynamic_slice_in_dim(chip_rows, (1 - core) * share, share, 1), 0)
    rest_share = jnp.where(
        core == 1,
        jnp.concatenate([rows_other, rows_mine], axis=2),
        jnp.concatenate([rows_mine, rows_other], axis=2),
    )

    ada_share = product("ld,lke->kde", silu_rows, mod_all)
    offset_share = jnp.sum(
        mod_and_offsets[:, ADA * features :]
        .astype(jnp.float32)
        .reshape(devices * 2, bias_count, share),
        axis=0,
    )

    grad_scale = lax.rsqrt((seqlen * jnp.sum(counts)).astype(jnp.float32))
    weight_grads = jnp.concatenate([ada_share, rest_share], axis=0) * grad_scale
    bias_grads = offset_share * grad_scale
    new_momenta = BETA_WEIGHT * momenta + weight_grads
    new_bias_momenta = BETA_BIAS * bias_momenta + bias_grads
    new_biases = biases - RATE_BIAS * new_bias_momenta

    outgoing = (
        new_momenta[extra:]
        .astype(jnp.bfloat16)
        .reshape(main, share, 2, half)
        .transpose(0, 2, 1, 3)
        .reshape(2 * main, share, half)
    )
    outgoing = jnp.pad(outgoing, ((0, devices - 2 * main), (0, 0), (0, 0)))
    columns_mine = all_to_all(outgoing).reshape(features, half)
    ortho_half = run_orthogonalize_halves(place, columns_mine, flip(columns_mine, 0))
    ortho_local = (
        all_to_all(ortho_half.reshape(devices, share, half))[: 2 * main]
        .reshape(main, 2, share, half)
        .transpose(0, 2, 1, 3)
        .reshape(main, share, features)
    )
    if extra:
        silu_all = small_all[:, :features]
        mod_mine = lax.dynamic_slice_in_dim(mod_all, core * (extra // 2), extra // 2, 1)
        spare_grads = product("ld,lke->kde", silu_all, mod_mine) * grad_scale
        spare = (BETA_WEIGHT * spare.astype(jnp.float32) + spare_grads).astype(jnp.bfloat16)
        spare_ortho = run_orthogonalize_whole(spare)
        chip_ortho = lax.dynamic_slice_in_dim(
            spare_ortho, (myself - core) * share, 2 * share, 1
        ).reshape(extra // 2, 2, share, features)
        ortho_mine = lax.dynamic_index_in_dim(chip_ortho, core, 1, keepdims=False)
        ortho_other = flip(
            lax.dynamic_index_in_dim(chip_ortho, 1 - core, 1, keepdims=False), 0
        )
        spare_local = joined(ortho_mine, ortho_other, core, 0).reshape(extra, share, features)
        ortho_local = jnp.concatenate([spare_local, ortho_local])
    silu_back = jax.vjp(jax.nn.silu, condition)[1]
    cond_grad = silu_back(grad_silu.reshape(features))[0] * seqlen ** (-0.5)
    new_weights = weights - RATE_WEIGHT * ortho_local.astype(jnp.float32)
    cond_grad = jnp.where(live_here, cond_grad, jnp.zeros_like(cond_grad))[None]
    return (
        output[None],
        input_grad[None],
        cond_grad,
        weight_grads,
        bias_grads,
        new_weights,
        new_momenta,
        new_biases,
        new_bias_momenta,
    )


def solution(mesh):
    return jax.shard_map(
        on_device,
        mesh=mesh,
        in_specs=(
            P("dp", None, None),
            P("dp", None),
            P("dp", None, None),
            P(None, "dp", None),
            P(None, "dp"),
            P(None, "dp", None),
            P(None, "dp"),
            P(),
        ),
        out_specs=(
            P("dp", None, None),
            P("dp", None, None),
            P("dp", None),
            P(None, "dp", None),
            P(None, "dp"),
            P(None, "dp", None),
            P(None, "dp", None),
            P(None, "dp"),
            P(None, "dp"),
        ),
        check_vma=False,
    )
```

```python
import functools

import jax
import jax.numpy as jnp
from jax import lax
from jax.experimental import pallas as pl
from jax.experimental.pallas import tpu as pltpu
from jax.sharding import PartitionSpec as P


HEADS = 12
NS_ITERS = 2
ADA = 6
COLOURS = 3

COEF_FIRST = 3.4445
COEF_SECOND = -4.775
COEF_THIRD = 2.0315
BETA_WEIGHT = 0.95
BETA_BIAS = 0.9
RATE_WEIGHT = 1.0
RATE_BIAS = 0.1
NORM_EPS = 1e-06


def product(spec, left, right):
    return jnp.einsum(spec, left, right, preferred_element_type=jnp.float32)


def flip(values, bit):
    devices = lax.axis_size("dp")
    return lax.ppermute(values, "dp", [(i, i ^ (1 << bit)) for i in range(devices)])


def bit_of(myself, bit):
    return (myself >> bit) & 1


def joined(values, other, taken, axis):
    return jnp.where(
        taken == 1, jnp.stack([other, values], axis), jnp.stack([values, other], axis)
    )


def gather_all(groups, orders, myself, first_too, last_too):
    carried = first_too
    for stage in range(len(orders[0])):
        others = [flip(group, order[stage]) for group, order in zip(groups, orders)]
        if stage == len(orders[0]) - 1:
            carried = last_too(carried)
        if stage in (0, len(orders[0]) - 1):
            others[-1], carried = lax.optimization_barrier((others[-1], carried))
        for index, order in enumerate(orders):
            bit = order[stage]
            groups[index] = joined(groups[index], others[index], bit_of(myself, bit), 0)
    return groups, carried


def gather_step(values, order, bit, myself):
    held = order[: order.index(bit)]
    position = 1 + sum(1 for before in held if before > bit)
    return joined(values, flip(values, bit), bit_of(myself, bit), position)


def flip_by_core(values, first_bit, second_bit):
    devices = lax.axis_size("dp")
    return lax.ppermute(
        values, "dp", [(i, i ^ (1 << (second_bit if i & 1 else first_bit))) for i in range(devices)]
    )


def corner_rows(near, far, order, myself):
    high, low = bit_of(myself, order[-2]), bit_of(myself, order[-1])
    core = bit_of(myself, 0)
    first, second = jnp.where(core == 1, low, high), jnp.where(core == 1, high, low)
    axis = len(order) - 1
    pairs = [
        joined(pair[0], pair[1], first, axis) for pair in (near, far)
    ]
    by_first = joined(pairs[0], pairs[1], second, axis)
    return jnp.where(core == 1, by_first, jnp.swapaxes(by_first, axis, axis + 1))


def split_bit(values, mine, position, sent_as):
    send = lax.dynamic_index_in_dim(values, 1 - mine, position, keepdims=False)
    keep = lax.dynamic_index_in_dim(values, mine, position, keepdims=False)
    return keep, send.astype(sent_as)


def scatter_all(halves, orders, myself, axis, spread, between):
    left = [sorted(order, reverse=True) for order in orders]
    carried = None
    totals = []
    for stage in range(len(orders[0])):
        others = [flip(send, order[stage]) for (_, send), order in zip(halves, orders)]
        if stage in between:
            carried = between[stage](carried)
            others[-1], carried = lax.optimization_barrier((others[-1], carried))
        totals = [
            keep + other.astype(jnp.float32) for (keep, _), other in zip(halves, others)
        ]
        for index, order in enumerate(orders):
            left[index].remove(order[stage])
            if stage == 0:
                totals[index] = spread(totals[index], len(left[index]))
            if left[index]:
                bit = order[stage + 1]
                position = axis + left[index].index(bit)
                halves[index] = split_bit(
                    totals[index], bit_of(myself, bit), position, jnp.bfloat16
                )
    return totals, carried


def index_bits(devices):
    return devices.bit_length() - 1


def colour_orders(devices):
    chip_bits = list(range(1, index_bits(devices)))
    rest, last = chip_bits[:-1], chip_bits[-1:]
    shifts = [(colour * len(rest)) // COLOURS for colour in range(COLOURS)]
    return [tuple(rest[shift:] + rest[:shift] + last) for shift in shifts]


def contract(left, right, left_dim, right_dim):
    return lax.dot_general(
        left, right, (((left_dim,), (right_dim,)), ((), ())), preferred_element_type=jnp.float32
    )


def layer_norm(stream):
    centred = stream - jnp.mean(stream, axis=-1, keepdims=True)
    inverse = lax.rsqrt(jnp.mean(centred * centred, axis=-1, keepdims=True) + NORM_EPS)
    return (centred * inverse, inverse)


def norm_back(normed, inverse, upstream):
    return inverse * (
        upstream
        - jnp.mean(upstream, axis=-1, keepdims=True)
        - normed * jnp.mean(upstream * normed, axis=-1, keepdims=True)
    )


def column_sum(values):
    return jnp.sum(values, axis=0, keepdims=True)


def scores_of(query, keys, width):
    return contract(query, keys, 1, 1) * width ** (-0.5)


def chunk_places(order):
    count = len(order)
    return [
        sum(((chip >> (bit - 1)) & 1) << place for place, bit in enumerate(order))
        for chip in range(1 << count)
    ]


def whole_weight(mine_ref, other_ref, index, core, order):
    places = chunk_places(order) if order else [0]
    mine, other = [
        jnp.concatenate([ref[place, index] for place in places], axis=0)
        for ref in (mine_ref, other_ref)
    ]
    return jnp.concatenate(
        [jnp.where(core == 1, other, mine), jnp.where(core == 1, mine, other)], axis=1
    )


def attention_forward(
    order,
    place_ref,
    source_ref,
    mod_ref,
    offsets_ref,
    mine_ref,
    other_ref,
    lefts_ref,
    qkv_ref,
    attn_ref,
    middle_ref,
):
    core = place_ref[0]
    seqlen, features = source_ref.shape
    width = features // HEADS
    stream = source_ref[...].astype(jnp.float32)
    normed, _ = layer_norm(stream)
    attn_input = (normed * (1.0 + mod_ref[1:2]) + mod_ref[0:1]).astype(jnp.bfloat16)
    lefts_ref[0] = attn_input
    qkv_ref[0] = (contract(attn_input, whole_weight(mine_ref, other_ref, 0, core, order), 1, 0) + offsets_ref[6:7]).astype(
        jnp.bfloat16
    )
    qkv_ref[1] = contract(attn_input, whole_weight(mine_ref, other_ref, 1, core, order), 1, 0).astype(jnp.bfloat16)
    qkv_ref[2] = (contract(attn_input, whole_weight(mine_ref, other_ref, 2, core, order), 1, 0) + offsets_ref[7:8]).astype(
        jnp.bfloat16
    )
    first = lax.broadcasted_iota(jnp.int32, (seqlen, 2 * width), 1) < width
    for pair in range(HEADS // 2):
        columns = slice(2 * width * pair, 2 * width * (pair + 1))
        query, keys, values = qkv_ref[0, :, columns], qkv_ref[1, :, columns], qkv_ref[2, :, columns]
        halves = []
        for mask in (first, jnp.logical_not(first)):
            scores = scores_of(jnp.where(mask, query, jnp.zeros_like(query)), keys, width)
            log_total = jnp.log(jnp.sum(jnp.exp(scores), axis=-1, keepdims=True))
            probs = jnp.exp(scores - log_total).astype(jnp.bfloat16)
            halves.append(contract(probs, values, 1, 0))
        lefts_ref[1, :, columns] = jnp.where(first, *halves).astype(jnp.bfloat16)
    attn_out = contract(lefts_ref[1], whole_weight(mine_ref, other_ref, 3, core, order), 1, 0) + offsets_ref[8:9]
    attn_ref[...] = attn_out
    middle = stream + mod_ref[2:3] * attn_out
    middle_ref[...] = middle
    normed_two, _ = layer_norm(middle)
    lefts_ref[2] = (normed_two * (1.0 + mod_ref[4:5]) + mod_ref[3:4]).astype(jnp.bfloat16)


def split_columns(values, core):
    width = values.shape[-1] // 2
    low, high = values[:, :width], values[:, width:]
    return (jnp.where(core == 1, high, low), jnp.where(core == 1, low, high))


def mlp_both_ways(
    up_order,
    down_order,
    place_ref,
    lefts_ref,
    middle_ref,
    attn_ref,
    upstream_ref,
    mod_ref,
    offsets_ref,
    up_ref,
    up_other_ref,
    down_ref,
    down_other_ref,
    output_ref,
    hidden_ref,
    keep_ref,
    send_ref,
    grad_middle_ref,
    grad_attn_ref,
    rows_ref,
    total_ref,
    grad_total_ref,
    grad_mlp_ref,
):
    step = pl.program_id(0)
    last = pl.num_programs(0) - 1
    core, live = place_ref[0], place_ref[1] > 0
    scale = 0.7978845608028654

    @pl.when(step == 0)
    def _():
        total_ref[...] = jnp.zeros_like(total_ref)
        grad_total_ref[...] = jnp.zeros_like(grad_total_ref)
        grad_mlp = jnp.where(live, upstream_ref[...].astype(jnp.float32) * mod_ref[5:6], 0.0)
        grad_mlp_b = grad_mlp.astype(jnp.bfloat16)
        grad_mlp_ref[...] = grad_mlp_b
        keep_ref[0], send_ref[0] = split_columns(grad_mlp_b, core)
        rows_ref[...] = jnp.zeros_like(rows_ref)
        rows_ref[pl.ds(10 + last, 1)] = column_sum(grad_mlp)

    up_w = whole_weight(up_ref, up_other_ref, 0, core, up_order)
    down_w = whole_weight(down_ref, down_other_ref, 0, core, down_order)
    before = contract(lefts_ref[0], up_w, 1, 0) + offsets_ref[pl.ds(9 + step, 1)]
    square = before * before
    bend = jnp.tanh(scale * (before + 0.044715 * square * before))
    hidden = (0.5 * before * (1.0 + bend)).astype(jnp.bfloat16)
    hidden_ref[0] = hidden
    total_ref[...] += contract(hidden, down_w, 1, 0)
    slope = 0.5 * (1.0 + bend) + 0.5 * before * (1.0 - bend * bend) * scale * (
        1.0 + 3.0 * 0.044715 * square
    )
    grad_pre = jnp.where(live, contract(grad_mlp_ref[...], down_w, 1, 1) * slope, 0.0)
    grad_pre_b = grad_pre.astype(jnp.bfloat16)
    keep_ref[step + 1], send_ref[step + 1] = split_columns(grad_pre_b, core)
    rows_ref[pl.ds(9 + step, 1)] = column_sum(grad_pre)
    grad_total_ref[...] += contract(grad_pre_b, up_w, 1, 1)

    @pl.when(step == last)
    def _():
        middle = middle_ref[...]
        grad_out = upstream_ref[...].astype(jnp.float32)
        mlp_out = total_ref[...] + offsets_ref[pl.ds(10 + last, 1)]
        output = middle + mod_ref[5:6] * mlp_out
        output_ref[...] = jnp.where(live, output, 0.0).astype(jnp.bfloat16)
        rows_ref[5:6] = jnp.where(live, column_sum(grad_out * mlp_out), 0.0)
        normed, inverse = layer_norm(middle)
        grad_in = grad_total_ref[...]
        rows_ref[3:4] = column_sum(grad_in)
        rows_ref[4:5] = column_sum(grad_in * normed)
        grad_middle = grad_out + norm_back(normed, inverse, grad_in * (1.0 + mod_ref[4:5]))
        grad_middle = jnp.where(live, grad_middle, 0.0)
        grad_middle_ref[...] = grad_middle
        rows_ref[2:3] = column_sum(grad_middle * attn_ref[...])
        grad_attn = grad_middle * mod_ref[2:3]
        grad_attn_ref[...] = grad_attn.astype(jnp.bfloat16)
        rows_ref[8:9] = column_sum(grad_attn)


def attention_backward(
    order,
    place_ref,
    source_ref,
    mod_ref,
    mine_ref,
    other_ref,
    qkv_ref,
    grad_middle_ref,
    grad_attn_ref,
    rows_in_ref,
    grad_source_ref,
    keep_ref,
    send_ref,
    rows_ref,
    grads_ref,
    context_ref,
):
    seqlen, features = source_ref.shape
    width = features // HEADS
    core, live = place_ref[0], place_ref[1] > 0
    rows_ref[...] = rows_in_ref[...]
    grad_attn = grad_attn_ref[...]
    keep_ref[3], send_ref[3] = split_columns(grad_attn, core)
    context_ref[...] = contract(
        grad_attn, whole_weight(mine_ref, other_ref, 3, core, order), 1, 1
    ).astype(jnp.bfloat16)
    first = lax.broadcasted_iota(jnp.int32, (seqlen, 2 * width), 1) < width
    for pair in range(HEADS // 2):
        columns = slice(2 * width * pair, 2 * width * (pair + 1))
        query, keys, values = qkv_ref[0, :, columns], qkv_ref[1, :, columns], qkv_ref[2, :, columns]
        upstream = context_ref[:, columns]
        parts = []
        for mask in (first, jnp.logical_not(first)):
            scores = scores_of(jnp.where(mask, query, jnp.zeros_like(query)), keys, width)
            log_total = jnp.log(jnp.sum(jnp.exp(scores), axis=-1, keepdims=True))
            probs = jnp.exp(scores - log_total)
            grad_values = contract(probs.astype(jnp.bfloat16), upstream, 0, 0)
            grad_probs = contract(
                jnp.where(mask, upstream, jnp.zeros_like(upstream)), values, 1, 1
            )
            row_dot = jnp.sum(probs * grad_probs, axis=-1, keepdims=True)
            grad_scores = (probs * (grad_probs - row_dot) * width ** (-0.5)).astype(jnp.bfloat16)
            parts.append(
                (
                    contract(grad_scores, keys, 1, 0),
                    contract(grad_scores, query, 0, 0),
                    grad_values,
                )
            )
        for index in range(3):
            merged = jnp.where(live, jnp.where(first, parts[0][index], parts[1][index]), 0.0)
            grads_ref[index, :, columns] = merged.astype(jnp.bfloat16)
            if index != 1:
                row = 6 if index == 0 else 7
                rows_ref[row : row + 1, columns] = column_sum(merged)
    grad_in = jnp.zeros((seqlen, features), jnp.float32)
    for index in range(3):
        grads = grads_ref[index]
        keep_ref[index], send_ref[index] = split_columns(grads, core)
        grad_in += contract(grads, whole_weight(mine_ref, other_ref, index, core, order), 1, 1)
    normed, inverse = layer_norm(source_ref[...].astype(jnp.float32))
    rows_ref[0:1] = column_sum(grad_in)
    rows_ref[1:2] = column_sum(grad_in * normed)
    grad_source_ref[...] = jnp.where(
        live,
        grad_middle_ref[...] + norm_back(normed, inverse, grad_in * (1.0 + mod_ref[1:2])),
        0.0,
    )


def pair_products(
    chunk, mine_ref, left_ref, left_other_ref, right_ref, right_other_ref, keep_ref, send_ref
):
    total = contract(left_ref[0], right_ref[0], 0, 0) + contract(
        left_other_ref[0], right_other_ref[0], 0, 0
    )
    for start in range(0, total.shape[0] // 2, chunk):
        low = total[2 * start : 2 * start + chunk]
        high = total[2 * start + chunk : 2 * start + 2 * chunk]
        mine = mine_ref[0] == 1
        keep_ref[0, start : start + chunk] = jnp.where(mine, high, low)
        send_ref[0, start : start + chunk] = jnp.where(mine, low, high).astype(jnp.bfloat16)


def plain_products(left_ref, left_other_ref, right_ref, right_other_ref, out_ref):
    out_ref[0] = contract(left_ref[0], right_ref[0], 0, 0) + contract(
        left_other_ref[0], right_other_ref[0], 0, 0
    )


def struct(shape, dtype):
    return jax.ShapeDtypeStruct(shape, dtype)


VMEM = pl.BlockSpec(memory_space=pltpu.VMEM)
SMEM = pl.BlockSpec(memory_space=pltpu.SMEM)


def resident(shape):
    zeros = (0,) * len(shape)
    return pl.BlockSpec(shape, lambda step: zeros)


def run_attention_forward(order, place, source, modulation, offsets, attn_w, attn_w_other):
    seqlen, features = source.shape
    return pl.pallas_call(
        functools.partial(attention_forward, order),
        name="attention_forward",
        out_shape=(
            struct((3, seqlen, features), jnp.bfloat16),
            struct((3, seqlen, features), jnp.bfloat16),
            struct((seqlen, features), jnp.float32),
            struct((seqlen, features), jnp.float32),
        ),
        in_specs=[SMEM] + [VMEM] * 5,
        out_specs=(VMEM,) * 4,
        compiler_params=pltpu.CompilerParams(vmem_limit_bytes=24 << 20),
        cost_estimate=pl.CostEstimate(
            flops=8 * seqlen * features * features + 8 * HEADS * seqlen * seqlen * 128,
            bytes_accessed=attn_w.size * 4 + source.size * 20,
            transcendentals=2 * HEADS * seqlen * seqlen,
        ),
    )(place, source, modulation, offsets, attn_w, attn_w_other)


def run_mlp(mlp_orders, place, lefts, middle, attn_out, upstream, modulation, offsets, up_ws, down_ws):
    seqlen, features = middle.shape
    chips, steps, rows, _ = up_ws[0].shape
    half = features // 2
    whole = (seqlen, features)
    return pl.pallas_call(
        functools.partial(mlp_both_ways, *mlp_orders),
        name="mlp_both_ways",
        grid=(steps,),
        out_shape=(
            struct(whole, jnp.bfloat16),
            struct((steps,) + whole, jnp.bfloat16),
            struct((steps + 1, seqlen, half), jnp.bfloat16),
            struct((steps + 1, seqlen, half), jnp.bfloat16),
            struct(whole, jnp.float32),
            struct(whole, jnp.bfloat16),
            struct(offsets.shape, jnp.float32),
        ),
        in_specs=[
            SMEM,
            pl.BlockSpec((1,) + whole, lambda step: (2, 0, 0)),
            resident(whole),
            resident(whole),
            resident(whole),
            resident(modulation.shape),
            resident(offsets.shape),
        ]
        + [pl.BlockSpec((chips, 1, rows, half), lambda step: (0, step, 0, 0))] * 4,
        out_specs=(
            resident(whole),
            pl.BlockSpec((1,) + whole, lambda step: (step, 0, 0)),
            resident((steps + 1, seqlen, half)),
            resident((steps + 1, seqlen, half)),
            resident(whole),
            resident(whole),
            resident(offsets.shape),
        ),
        scratch_shapes=[
            pltpu.VMEM(whole, jnp.float32),
            pltpu.VMEM(whole, jnp.float32),
            pltpu.VMEM(whole, jnp.bfloat16),
        ],
        compiler_params=pltpu.CompilerParams(vmem_limit_bytes=28 << 20),
        cost_estimate=pl.CostEstimate(
            flops=8 * seqlen * features * features * steps,
            bytes_accessed=up_ws[0].size * 8 + seqlen * features * 40,
            transcendentals=seqlen * features * steps,
        ),
    )(place, lefts, middle, attn_out, upstream, modulation, offsets, *up_ws, *down_ws)


def run_attention_backward(
    order, place, source, modulation, attn_w, attn_w_other, qkv, grad_middle, grad_attn, rows
):
    seqlen, features = source.shape
    half = features // 2
    return pl.pallas_call(
        functools.partial(attention_backward, order),
        name="attention_backward",
        out_shape=(
            struct((seqlen, features), jnp.float32),
            struct((4, seqlen, half), jnp.bfloat16),
            struct((4, seqlen, half), jnp.bfloat16),
            struct(rows.shape, jnp.float32),
        ),
        in_specs=[SMEM] + [VMEM] * 8,
        out_specs=(VMEM,) * 4,
        scratch_shapes=[
            pltpu.VMEM((3, seqlen, features), jnp.bfloat16),
            pltpu.VMEM((seqlen, features), jnp.bfloat16),
        ],
        compiler_params=pltpu.CompilerParams(vmem_limit_bytes=24 << 20),
        cost_estimate=pl.CostEstimate(
            flops=8 * seqlen * features * features + 20 * HEADS * seqlen * seqlen * 128,
            bytes_accessed=attn_w.size * 4 + source.size * 24,
            transcendentals=2 * HEADS * seqlen * seqlen,
        ),
    )(place, source, modulation, attn_w, attn_w_other, qkv, grad_middle, grad_attn, rows)


def run_products(lefts, lefts_other, rights, rights_other, left_at, right_at, count, mine, chunk):
    _, seqlen, features = lefts.shape
    width = rights.shape[-1]
    left_spec = pl.BlockSpec((1, seqlen, features), lambda step: (left_at(step), 0, 0))
    right_spec = pl.BlockSpec((1, seqlen, width), lambda step: (right_at(step), 0, 0))
    specs = [left_spec, left_spec, right_spec, right_spec]
    cost = pl.CostEstimate(
        flops=4 * count * seqlen * features * width,
        bytes_accessed=count * features * width * 6,
        transcendentals=0,
    )
    if chunk % 16:
        total = pl.pallas_call(
            plain_products,
            name="plain_products",
            grid=(count,),
            out_shape=struct((count, features, width), jnp.float32),
            in_specs=specs,
            out_specs=pl.BlockSpec((1, features, width), lambda step: (step, 0, 0)),
            cost_estimate=cost,
        )(lefts, lefts_other, rights, rights_other)
        keep, send = split_bit(
            total.reshape(count, features // (2 * chunk), 2, chunk, width), mine, 2, jnp.bfloat16
        )
        shape = (count, features // 2, width)
        return keep.reshape(shape), send.reshape(shape)
    half_spec = pl.BlockSpec((1, features // 2, width), lambda step: (step, 0, 0))
    return pl.pallas_call(
        functools.partial(pair_products, chunk),
        name="pair_products",
        grid=(count,),
        out_shape=(
            struct((count, features // 2, width), jnp.float32),
            struct((count, features // 2, width), jnp.bfloat16),
        ),
        in_specs=[SMEM] + specs,
        out_specs=(half_spec, half_spec),
        cost_estimate=cost,
    )(mine[None], lefts, lefts_other, rights, rights_other)


def muon_steps(block):
    values = block.astype(jnp.float32)
    scaled = (values / (jnp.sqrt(jnp.sum(values * values)) + 1e-07)).astype(jnp.bfloat16)
    for _ in range(NS_ITERS):
        gram = contract(scaled, scaled, 1, 1).astype(jnp.bfloat16)
        square = contract(gram, gram, 1, 0)
        mixed = (COEF_SECOND * gram.astype(jnp.float32) + COEF_THIRD * square).astype(jnp.bfloat16)
        scaled = (
            COEF_FIRST * scaled.astype(jnp.float32) + contract(mixed, scaled, 1, 0)
        ).astype(jnp.bfloat16)
    return scaled


def orthogonalize_halves(place_ref, mine_ref, other_ref, out_ref):
    core = place_ref[0]
    mine, other = mine_ref[...], other_ref[...]
    low, high = jnp.where(core == 1, other, mine), jnp.where(core == 1, mine, other)
    scaled = muon_steps(jnp.concatenate([low, high], axis=1))
    out_ref[...] = split_columns(scaled, core)[0]


def orthogonalize_whole(block_ref, out_ref):
    out_ref[0] = muon_steps(block_ref[0])


def muon_cost(count, rows):
    return pl.CostEstimate(
        flops=6 * count * NS_ITERS * rows**3, bytes_accessed=4 * count * rows**2, transcendentals=0
    )


def run_orthogonalize_halves(place, mine, other):
    return pl.pallas_call(
        orthogonalize_halves,
        name="orthogonalize_halves",
        out_shape=struct(mine.shape, mine.dtype),
        in_specs=[SMEM, VMEM, VMEM],
        out_specs=VMEM,
        compiler_params=pltpu.CompilerParams(vmem_limit_bytes=24 << 20),
        cost_estimate=muon_cost(1, mine.shape[0]),
    )(place, mine, other)


def run_orthogonalize_whole(blocks):
    spec = pl.BlockSpec((1,) + blocks.shape[1:], lambda step: (step, 0, 0))
    return pl.pallas_call(
        orthogonalize_whole,
        name="orthogonalize_whole",
        grid=(blocks.shape[0],),
        out_shape=struct(blocks.shape, blocks.dtype),
        in_specs=[spec],
        out_specs=spec,
        compiler_params=pltpu.CompilerParams(vmem_limit_bytes=24 << 20),
        cost_estimate=muon_cost(*blocks.shape[:2]),
    )(blocks)


def all_to_all(values):
    return lax.all_to_all(values, "dp", split_axis=0, concat_axis=0, tiled=True)


def to_all(row):
    devices = lax.axis_size("dp")
    return all_to_all(jnp.broadcast_to(row[None], (devices,) + row.shape))


def on_device(latents, conditioning, cotangent, weights, biases, momenta, bias_momenta, counts):
    _, seqlen, features = latents.shape
    block_count, share, _ = weights.shape
    hidden_blocks = (block_count - 10) // 2
    bias_count = biases.shape[0]
    devices = lax.axis_size("dp")
    myself = lax.axis_index("dp")
    core = bit_of(myself, 0)
    bits = index_bits(devices)
    orders = colour_orders(devices)
    ranks = jnp.arange(devices, dtype=jnp.int32)
    live_here = jnp.sum(jnp.where(ranks == myself, counts, 0)) > 0

    lowered = weights.astype(jnp.bfloat16)
    ada_w = lowered[:ADA]
    condition = conditioning[0].astype(jnp.float32)
    silu_cond = jax.nn.silu(condition).astype(jnp.bfloat16)

    half = features // 2
    rest = lowered[ADA:]
    columns_mine = lax.dynamic_slice_in_dim(rest, core * half, half, 2)
    columns_other = lax.dynamic_slice_in_dim(rest, (1 - core) * half, half, 2)
    columns_other = flip(columns_other, 0)
    chip_rows = jnp.where(
        core == 1,
        jnp.concatenate([columns_other, columns_mine], axis=1),
        jnp.concatenate([columns_mine, columns_other], axis=1),
    )
    bounds = [0, 10 - ADA, 10 - ADA + hidden_blocks, block_count - ADA]
    stages = bits - 1
    small_all = to_all(
        jnp.concatenate([silu_cond, biases.astype(jnp.bfloat16).reshape(-1)])
    )

    def modulations(small_all):
        silu_rows = lax.dynamic_slice_in_dim(small_all[:, :features], myself * share, share, 1)
        mod_parts = product("ld,kde->lke", silu_rows, ada_w).reshape(devices, ADA * features)
        offsets = (
            small_all[:, features:]
            .reshape(devices, bias_count, share)
            .transpose(1, 0, 2)
            .reshape(bias_count, features)
            .astype(jnp.float32)
        )
        return small_all, silu_rows, offsets, all_to_all(mod_parts)

    groups, (small_all, silu_rows, offsets, mod_sums) = gather_all(
        [chip_rows[low:high] for low, high in zip(bounds[:-1], bounds[1:])],
        [tuple(reversed(order)) for order in orders],
        myself,
        small_all,
        modulations,
    )
    modulation = jnp.sum(mod_sums, axis=0).reshape(ADA, features) + offsets[:ADA]
    rows = 2 * share
    held_orders = [tuple(reversed(order)) for order in orders]
    pairs = []
    for index, order in enumerate(held_orders):
        group = groups[index].reshape(devices // 2, -1, rows, half)
        if rows % 16:
            group = jnp.stack([group[place] for place in chunk_places(order)], axis=1)
            group = group.reshape(1, -1, features, half)
            held_orders[index] = ()
        pairs.append((group, flip(group, 0)))
    attn_ws, up_ws, down_ws = pairs

    place = jnp.stack([core, live_here.astype(jnp.int32)]).astype(jnp.int32)
    extra = max(0, block_count - devices // 2)
    assert extra % 2 == 0 and extra <= ADA
    main = block_count - extra
    spare = ()
    spare_bits = tuple(reversed(range(1, bits)))
    if extra:
        spare = momenta[:extra].astype(jnp.bfloat16).reshape(2, extra // 2, share, features)
        spare_mine = lax.dynamic_index_in_dim(spare, core, 0, keepdims=False)
        spare_other = flip(lax.dynamic_index_in_dim(spare, 1 - core, 0, keepdims=False), 0)
        spare = joined(spare_mine, spare_other, core, 1).reshape(extra // 2, 2 * share, features)
        modulation, spare = lax.optimization_barrier((modulation, spare))
        spare = gather_step(spare, spare_bits, spare_bits[0], myself)
        for bit in spare_bits[1:-2]:
            spare = gather_step(spare, spare_bits, bit, myself)
        received = flip_by_core(spare, spare_bits[-2], spare_bits[-1])
        near = jnp.stack([spare, received])
        far = flip_by_core(near, spare_bits[-1], spare_bits[-2])
        spare = corner_rows(near, far, spare_bits, myself)
        spare = spare.reshape(extra // 2, features, features)
    lefts, qkv, attn_out, middle = run_attention_forward(
        held_orders[0], place, latents[0], modulation, offsets, *attn_ws
    )
    lefts_other = flip(lefts, 0)
    output, hidden, mlp_keep, mlp_send, grad_middle, grad_attn, rows = run_mlp(
        held_orders[1:],
        place,
        lefts,
        middle,
        attn_out,
        cotangent[0],
        modulation,
        offsets,
        up_ws,
        down_ws,
    )
    hidden_other = flip(hidden, 0)
    mlp_other = flip(mlp_send, 0)

    def spread(mats, count):
        return mats.reshape((mats.shape[0],) + (2,) * count + (2 * share, half))

    def products(left, left_other, right, right_other, left_at, right_at, count, order):
        return run_products(
            left,
            left_other,
            right,
            right_other,
            left_at,
            right_at,
            count,
            bit_of(myself, order[0]),
            share << order[0],
        )

    down_halves = products(
        hidden, hidden_other, mlp_keep, mlp_other, lambda b: b, lambda b: 0, hidden_blocks, orders[0]
    )
    up_halves = products(
        lefts, lefts_other, mlp_keep, mlp_other, lambda b: 2, lambda b: b + 1, hidden_blocks, orders[1]
    )
    input_grad, attn_keep, attn_send, grad_offsets = run_attention_backward(
        held_orders[0], place, latents[0], modulation, *attn_ws, qkv, grad_middle, grad_attn, rows
    )
    attn_other = flip(attn_send, 0)
    attn_halves = products(
        lefts, lefts_other, attn_keep, attn_other, lambda b: b // 3, lambda b: b, 4, orders[2]
    )

    grad_mod_b = grad_offsets[:ADA].astype(jnp.bfloat16).reshape(-1)
    by_holder = (
        grad_offsets.reshape(bias_count, devices, share)
        .transpose(1, 0, 2)
        .reshape(devices, bias_count * share)
    )
    coarse = lax.reduce_precision(by_holder, 8, 7)
    mod_and_offsets = jnp.concatenate(
        [
            jnp.broadcast_to(grad_mod_b[None], (devices, ADA * features)),
            coarse.astype(jnp.bfloat16),
            (by_holder - coarse).astype(jnp.bfloat16),
        ],
        axis=1,
    )
    mod_and_offsets = all_to_all(mod_and_offsets)

    def conditioning_grads(mod_and_offsets):
        mod_all = mod_and_offsets[:, : ADA * features].reshape(devices, ADA, features)
        silu_parts = product("lke,kde->ld", mod_all, ada_w)
        return mod_and_offsets, mod_all, all_to_all(silu_parts)

    sums, (mod_and_offsets, mod_all, grad_silu) = scatter_all(
        [attn_halves, up_halves, down_halves],
        [orders[2], orders[1], orders[0]],
        myself,
        1,
        spread,
        {stages - 1: lambda _: conditioning_grads(mod_and_offsets)},
    )
    chip_rows = jnp.concatenate(sums, axis=0)
    rows_mine = lax.dynamic_slice_in_dim(chip_rows, core * share, share, 1)
    rows_other = flip(lax.dynamic_slice_in_dim(chip_rows, (1 - core) * share, share, 1), 0)
    rest_share = jnp.where(
        core == 1,
        jnp.concatenate([rows_other, rows_mine], axis=2),
        jnp.concatenate([rows_mine, rows_other], axis=2),
    )

    ada_share = product("ld,lke->kde", silu_rows, mod_all)
    offset_share = jnp.sum(
        mod_and_offsets[:, ADA * features :]
        .astype(jnp.float32)
        .reshape(devices * 2, bias_count, share),
        axis=0,
    )

    grad_scale = lax.rsqrt((seqlen * jnp.sum(counts)).astype(jnp.float32))
    weight_grads = jnp.concatenate([ada_share, rest_share], axis=0) * grad_scale
    bias_grads = offset_share * grad_scale
    new_momenta = BETA_WEIGHT * momenta + weight_grads
    new_bias_momenta = BETA_BIAS * bias_momenta + bias_grads
    new_biases = biases - RATE_BIAS * new_bias_momenta

    outgoing = (
        new_momenta[extra:]
        .astype(jnp.bfloat16)
        .reshape(main, share, 2, half)
        .transpose(0, 2, 1, 3)
        .reshape(2 * main, share, half)
    )
    outgoing = jnp.pad(outgoing, ((0, devices - 2 * main), (0, 0), (0, 0)))
    columns_mine = all_to_all(outgoing).reshape(features, half)
    ortho_half = run_orthogonalize_halves(place, columns_mine, flip(columns_mine, 0))
    ortho_local = (
        all_to_all(ortho_half.reshape(devices, share, half))[: 2 * main]
        .reshape(main, 2, share, half)
        .transpose(0, 2, 1, 3)
        .reshape(main, share, features)
    )
    if extra:
        silu_all = small_all[:, :features]
        mod_mine = lax.dynamic_slice_in_dim(mod_all, core * (extra // 2), extra // 2, 1)
        spare_grads = product("ld,lke->kde", silu_all, mod_mine) * grad_scale
        spare = (BETA_WEIGHT * spare.astype(jnp.float32) + spare_grads).astype(jnp.bfloat16)
        spare_ortho = run_orthogonalize_whole(spare)
        chip_ortho = lax.dynamic_slice_in_dim(
            spare_ortho, (myself - core) * share, 2 * share, 1
        ).reshape(extra // 2, 2, share, features)
        ortho_mine = lax.dynamic_index_in_dim(chip_ortho, core, 1, keepdims=False)
        ortho_other = flip(
            lax.dynamic_index_in_dim(chip_ortho, 1 - core, 1, keepdims=False), 0
        )
        spare_local = joined(ortho_mine, ortho_other, core, 0).reshape(extra, share, features)
        ortho_local = jnp.concatenate([spare_local, ortho_local])
    silu_back = jax.vjp(jax.nn.silu, condition)[1]
    cond_grad = silu_back(grad_silu.reshape(features))[0] * seqlen ** (-0.5)
    new_weights = weights - RATE_WEIGHT * ortho_local.astype(jnp.float32)
    cond_grad = jnp.where(live_here, cond_grad, jnp.zeros_like(cond_grad))[None]
    return (
        output[None],
        input_grad[None],
        cond_grad,
        weight_grads,
        bias_grads,
        new_weights,
        new_momenta,
        new_biases,
        new_bias_momenta,
    )


def solution(mesh):
    return jax.shard_map(
        on_device,
        mesh=mesh,
        in_specs=(
            P("dp", None, None),
            P("dp", None),
            P("dp", None, None),
            P(None, "dp", None),
            P(None, "dp"),
            P(None, "dp", None),
            P(None, "dp"),
            P(),
        ),
        out_specs=(
            P("dp", None, None),
            P("dp", None, None),
            P("dp", None),
            P(None, "dp", None),
            P(None, "dp"),
            P(None, "dp", None),
            P(None, "dp", None),
            P(None, "dp"),
            P(None, "dp"),
        ),
        check_vma=False,
    )
```

```python
import functools

import jax
import jax.numpy as jnp
from jax import lax
from jax.experimental import pallas as pl
from jax.experimental.pallas import tpu as pltpu
from jax.sharding import PartitionSpec as P


HEADS = 12
NS_ITERS = 2
ADA = 6
COLOURS = 3

COEF_FIRST = 3.4445
COEF_SECOND = -4.775
COEF_THIRD = 2.0315
BETA_WEIGHT = 0.95
BETA_BIAS = 0.9
RATE_WEIGHT = 1.0
RATE_BIAS = 0.1
NORM_EPS = 1e-06


def product(spec, left, right):
    return jnp.einsum(spec, left, right, preferred_element_type=jnp.float32)


def flip(values, bit):
    devices = lax.axis_size("dp")
    return lax.ppermute(values, "dp", [(i, i ^ (1 << bit)) for i in range(devices)])


def bit_of(myself, bit):
    return (myself >> bit) & 1


def joined(values, other, taken, axis):
    return jnp.where(
        taken == 1, jnp.stack([other, values], axis), jnp.stack([values, other], axis)
    )


def gather_all(groups, orders, myself, first_too, last_too):
    carried = first_too
    for stage in range(len(orders[0])):
        others = [flip(group, order[stage]) for group, order in zip(groups, orders)]
        if stage == len(orders[0]) - 1:
            carried = last_too(carried)
        if stage in (0, len(orders[0]) - 1):
            others[-1], carried = lax.optimization_barrier((others[-1], carried))
        for index, order in enumerate(orders):
            bit = order[stage]
            groups[index] = joined(groups[index], others[index], bit_of(myself, bit), 0)
    return groups, carried


def gather_step(values, order, bit, myself):
    held = order[: order.index(bit)]
    position = 1 + sum(1 for before in held if before > bit)
    return joined(values, flip(values, bit), bit_of(myself, bit), position)


def flip_by_core(values, first_bit, second_bit):
    devices = lax.axis_size("dp")
    return lax.ppermute(
        values, "dp", [(i, i ^ (1 << (second_bit if i & 1 else first_bit))) for i in range(devices)]
    )


def corner_rows(near, far, order, myself):
    high, low = bit_of(myself, order[-2]), bit_of(myself, order[-1])
    core = bit_of(myself, 0)
    first, second = jnp.where(core == 1, low, high), jnp.where(core == 1, high, low)
    axis = len(order) - 1
    pairs = [
        joined(pair[0], pair[1], first, axis) for pair in (near, far)
    ]
    by_first = joined(pairs[0], pairs[1], second, axis)
    return jnp.where(core == 1, by_first, jnp.swapaxes(by_first, axis, axis + 1))


def split_bit(values, mine, position, sent_as):
    send = lax.dynamic_index_in_dim(values, 1 - mine, position, keepdims=False)
    keep = lax.dynamic_index_in_dim(values, mine, position, keepdims=False)
    return keep, send.astype(sent_as)


def scatter_all(halves, orders, myself, axis, spread, between):
    left = [sorted(order, reverse=True) for order in orders]
    carried = None
    totals = []
    for stage in range(len(orders[0])):
        others = [flip(send, order[stage]) for (_, send), order in zip(halves, orders)]
        if stage in between:
            carried = between[stage](carried)
            others[-1], carried = lax.optimization_barrier((others[-1], carried))
        totals = [
            keep + other.astype(jnp.float32) for (keep, _), other in zip(halves, others)
        ]
        for index, order in enumerate(orders):
            left[index].remove(order[stage])
            if stage == 0:
                totals[index] = spread(totals[index], len(left[index]))
            if left[index]:
                bit = order[stage + 1]
                position = axis + left[index].index(bit)
                halves[index] = split_bit(
                    totals[index], bit_of(myself, bit), position, jnp.bfloat16
                )
    return totals, carried


def index_bits(devices):
    return devices.bit_length() - 1


def colour_orders(devices):
    chip_bits = list(range(1, index_bits(devices)))
    rest, last = chip_bits[:-1], chip_bits[-1:]
    shifts = [(colour * len(rest)) // COLOURS for colour in range(COLOURS)]
    return [tuple(rest[shift:] + rest[:shift] + last) for shift in shifts]


def contract(left, right, left_dim, right_dim):
    return lax.dot_general(
        left, right, (((left_dim,), (right_dim,)), ((), ())), preferred_element_type=jnp.float32
    )


def layer_norm(stream):
    centred = stream - jnp.mean(stream, axis=-1, keepdims=True)
    inverse = lax.rsqrt(jnp.mean(centred * centred, axis=-1, keepdims=True) + NORM_EPS)
    return (centred * inverse, inverse)


def norm_back(normed, inverse, upstream):
    return inverse * (
        upstream
        - jnp.mean(upstream, axis=-1, keepdims=True)
        - normed * jnp.mean(upstream * normed, axis=-1, keepdims=True)
    )


def column_sum(values):
    return jnp.sum(values, axis=0, keepdims=True)


def scores_of(query, keys, width):
    return contract(query, keys, 1, 1) * width ** (-0.5)


def chunk_places(order):
    count = len(order)
    return [
        sum(((chip >> (bit - 1)) & 1) << place for place, bit in enumerate(order))
        for chip in range(1 << count)
    ]


def whole_weight(mine_ref, other_ref, index, core, order):
    places = chunk_places(order) if order else [0]
    mine, other = [
        jnp.concatenate([ref[place, index] for place in places], axis=0)
        for ref in (mine_ref, other_ref)
    ]
    return jnp.concatenate(
        [jnp.where(core == 1, other, mine), jnp.where(core == 1, mine, other)], axis=1
    )


def attention_forward(
    order,
    place_ref,
    source_ref,
    mod_ref,
    offsets_ref,
    mine_ref,
    other_ref,
    lefts_ref,
    qkv_ref,
    attn_ref,
    middle_ref,
):
    core = place_ref[0]
    seqlen, features = source_ref.shape
    width = features // HEADS
    stream = source_ref[...].astype(jnp.float32)
    normed, _ = layer_norm(stream)
    attn_input = (normed * (1.0 + mod_ref[1:2]) + mod_ref[0:1]).astype(jnp.bfloat16)
    lefts_ref[0] = attn_input

    @pl.loop(0, 3)
    def _(index):
        row = jnp.where(index == 0, offsets_ref[6:7], offsets_ref[7:8])
        values = contract(attn_input, whole_weight(mine_ref, other_ref, index, core, order), 1, 0)
        qkv_ref[index] = (values + jnp.where(index == 1, 0.0, row)).astype(jnp.bfloat16)

    first = lax.broadcasted_iota(jnp.int32, (seqlen, 2 * width), 1) < width

    @pl.loop(0, HEADS // 2)
    def _(pair):
        columns = pl.ds(pl.multiple_of(2 * width * pair, 2 * width), 2 * width)
        query, keys, values = qkv_ref[0, :, columns], qkv_ref[1, :, columns], qkv_ref[2, :, columns]
        halves = []
        for mask in (first, jnp.logical_not(first)):
            scores = scores_of(jnp.where(mask, query, jnp.zeros_like(query)), keys, width)
            log_total = jnp.log(jnp.sum(jnp.exp(scores), axis=-1, keepdims=True))
            probs = jnp.exp(scores - log_total).astype(jnp.bfloat16)
            halves.append(contract(probs, values, 1, 0))
        lefts_ref[1, :, columns] = jnp.where(first, *halves).astype(jnp.bfloat16)

    attn_out = contract(lefts_ref[1], whole_weight(mine_ref, other_ref, 3, core, order), 1, 0) + offsets_ref[8:9]
    attn_ref[...] = attn_out
    middle = stream + mod_ref[2:3] * attn_out
    middle_ref[...] = middle
    normed_two, _ = layer_norm(middle)
    lefts_ref[2] = (normed_two * (1.0 + mod_ref[4:5]) + mod_ref[3:4]).astype(jnp.bfloat16)


def split_columns(values, core):
    width = values.shape[-1] // 2
    low, high = values[:, :width], values[:, width:]
    return (jnp.where(core == 1, high, low), jnp.where(core == 1, low, high))


def mlp_both_ways(
    up_order,
    down_order,
    place_ref,
    lefts_ref,
    middle_ref,
    attn_ref,
    upstream_ref,
    mod_ref,
    offsets_ref,
    up_ref,
    up_other_ref,
    down_ref,
    down_other_ref,
    output_ref,
    hidden_ref,
    keep_ref,
    send_ref,
    grad_middle_ref,
    grad_attn_ref,
    rows_ref,
    total_ref,
    grad_total_ref,
    grad_mlp_ref,
):
    step = pl.program_id(0)
    last = pl.num_programs(0) - 1
    core, live = place_ref[0], place_ref[1] > 0
    scale = 0.7978845608028654

    @pl.when(step == 0)
    def _():
        total_ref[...] = jnp.zeros_like(total_ref)
        grad_total_ref[...] = jnp.zeros_like(grad_total_ref)
        grad_mlp = jnp.where(live, upstream_ref[...].astype(jnp.float32) * mod_ref[5:6], 0.0)
        grad_mlp_b = grad_mlp.astype(jnp.bfloat16)
        grad_mlp_ref[...] = grad_mlp_b
        keep_ref[0], send_ref[0] = split_columns(grad_mlp_b, core)
        rows_ref[...] = jnp.zeros_like(rows_ref)
        rows_ref[pl.ds(10 + last, 1)] = column_sum(grad_mlp)

    up_w = whole_weight(up_ref, up_other_ref, 0, core, up_order)
    down_w = whole_weight(down_ref, down_other_ref, 0, core, down_order)
    before = contract(lefts_ref[0], up_w, 1, 0) + offsets_ref[pl.ds(9 + step, 1)]
    square = before * before
    bend = jnp.tanh(scale * (before + 0.044715 * square * before))
    hidden = (0.5 * before * (1.0 + bend)).astype(jnp.bfloat16)
    hidden_ref[0] = hidden
    total_ref[...] += contract(hidden, down_w, 1, 0)
    slope = 0.5 * (1.0 + bend) + 0.5 * before * (1.0 - bend * bend) * scale * (
        1.0 + 3.0 * 0.044715 * square
    )
    grad_pre = jnp.where(live, contract(grad_mlp_ref[...], down_w, 1, 1) * slope, 0.0)
    grad_pre_b = grad_pre.astype(jnp.bfloat16)
    keep_ref[step + 1], send_ref[step + 1] = split_columns(grad_pre_b, core)
    rows_ref[pl.ds(9 + step, 1)] = column_sum(grad_pre)
    grad_total_ref[...] += contract(grad_pre_b, up_w, 1, 1)

    @pl.when(step == last)
    def _():
        middle = middle_ref[...]
        grad_out = upstream_ref[...].astype(jnp.float32)
        mlp_out = total_ref[...] + offsets_ref[pl.ds(10 + last, 1)]
        output = middle + mod_ref[5:6] * mlp_out
        output_ref[...] = jnp.where(live, output, 0.0).astype(jnp.bfloat16)
        rows_ref[5:6] = jnp.where(live, column_sum(grad_out * mlp_out), 0.0)
        normed, inverse = layer_norm(middle)
        grad_in = grad_total_ref[...]
        rows_ref[3:4] = column_sum(grad_in)
        rows_ref[4:5] = column_sum(grad_in * normed)
        grad_middle = grad_out + norm_back(normed, inverse, grad_in * (1.0 + mod_ref[4:5]))
        grad_middle = jnp.where(live, grad_middle, 0.0)
        grad_middle_ref[...] = grad_middle
        rows_ref[2:3] = column_sum(grad_middle * attn_ref[...])
        grad_attn = grad_middle * mod_ref[2:3]
        grad_attn_ref[...] = grad_attn.astype(jnp.bfloat16)
        rows_ref[8:9] = column_sum(grad_attn)


def attention_backward(
    order,
    place_ref,
    source_ref,
    mod_ref,
    mine_ref,
    other_ref,
    qkv_ref,
    grad_middle_ref,
    grad_attn_ref,
    rows_in_ref,
    grad_source_ref,
    keep_ref,
    send_ref,
    rows_ref,
    grads_ref,
    context_ref,
):
    seqlen, features = source_ref.shape
    width = features // HEADS
    core, live = place_ref[0], place_ref[1] > 0
    rows_ref[...] = rows_in_ref[...]
    grad_attn = grad_attn_ref[...]
    keep_ref[3], send_ref[3] = split_columns(grad_attn, core)
    context_ref[...] = contract(
        grad_attn, whole_weight(mine_ref, other_ref, 3, core, order), 1, 1
    ).astype(jnp.bfloat16)
    first = lax.broadcasted_iota(jnp.int32, (seqlen, 2 * width), 1) < width

    @pl.loop(0, HEADS // 2)
    def _(pair):
        columns = pl.ds(pl.multiple_of(2 * width * pair, 2 * width), 2 * width)
        query, keys, values = qkv_ref[0, :, columns], qkv_ref[1, :, columns], qkv_ref[2, :, columns]
        upstream = context_ref[:, columns]
        parts = []
        for mask in (first, jnp.logical_not(first)):
            scores = scores_of(jnp.where(mask, query, jnp.zeros_like(query)), keys, width)
            log_total = jnp.log(jnp.sum(jnp.exp(scores), axis=-1, keepdims=True))
            probs = jnp.exp(scores - log_total)
            grad_values = contract(probs.astype(jnp.bfloat16), upstream, 0, 0)
            grad_probs = contract(
                jnp.where(mask, upstream, jnp.zeros_like(upstream)), values, 1, 1
            )
            row_dot = jnp.sum(probs * grad_probs, axis=-1, keepdims=True)
            grad_scores = (probs * (grad_probs - row_dot) * width ** (-0.5)).astype(jnp.bfloat16)
            parts.append(
                (
                    contract(grad_scores, keys, 1, 0),
                    contract(grad_scores, query, 0, 0),
                    grad_values,
                )
            )
        for index in range(3):
            merged = jnp.where(live, jnp.where(first, parts[0][index], parts[1][index]), 0.0)
            grads_ref[index, :, columns] = merged.astype(jnp.bfloat16)
            if index != 1:
                row = 6 if index == 0 else 7
                rows_ref[row : row + 1, columns] = column_sum(merged)

    grad_source_ref[...] = jnp.zeros_like(grad_source_ref)

    @pl.loop(0, 3)
    def _(index):
        grads = grads_ref[index]
        keep_ref[index], send_ref[index] = split_columns(grads, core)
        grad_source_ref[...] += contract(
            grads, whole_weight(mine_ref, other_ref, index, core, order), 1, 1
        )

    grad_in = grad_source_ref[...]
    normed, inverse = layer_norm(source_ref[...].astype(jnp.float32))
    rows_ref[0:1] = column_sum(grad_in)
    rows_ref[1:2] = column_sum(grad_in * normed)
    grad_source_ref[...] = jnp.where(
        live,
        grad_middle_ref[...] + norm_back(normed, inverse, grad_in * (1.0 + mod_ref[1:2])),
        0.0,
    )


def pair_products(
    chunk, mine_ref, left_ref, left_other_ref, right_ref, right_other_ref, keep_ref, send_ref
):
    features = left_ref.shape[-1]
    part = features // 2
    if part % (2 * chunk) or part % 128:
        part = features
    mine = mine_ref[0] == 1

    @pl.loop(0, features // part)
    def _(index):
        columns = pl.ds(pl.multiple_of(index * part, 128), part)
        total = contract(left_ref[0, :, columns], right_ref[0], 0, 0) + contract(
            left_other_ref[0, :, columns], right_other_ref[0], 0, 0
        )
        base = pl.multiple_of(index * (part // 2), 16)
        for start in range(0, part // 2, chunk):
            low = total[2 * start : 2 * start + chunk]
            high = total[2 * start + chunk : 2 * start + 2 * chunk]
            rows = pl.ds(base + start, chunk)
            keep_ref[0, rows] = jnp.where(mine, high, low)
            send_ref[0, rows] = jnp.where(mine, low, high).astype(jnp.bfloat16)


def plain_products(left_ref, left_other_ref, right_ref, right_other_ref, out_ref):
    out_ref[0] = contract(left_ref[0], right_ref[0], 0, 0) + contract(
        left_other_ref[0], right_other_ref[0], 0, 0
    )


def struct(shape, dtype):
    return jax.ShapeDtypeStruct(shape, dtype)


VMEM = pl.BlockSpec(memory_space=pltpu.VMEM)
SMEM = pl.BlockSpec(memory_space=pltpu.SMEM)


def resident(shape):
    zeros = (0,) * len(shape)
    return pl.BlockSpec(shape, lambda step: zeros)


def run_attention_forward(order, place, source, modulation, offsets, attn_w, attn_w_other):
    seqlen, features = source.shape
    return pl.pallas_call(
        functools.partial(attention_forward, order),
        name="attention_forward",
        out_shape=(
            struct((3, seqlen, features), jnp.bfloat16),
            struct((3, seqlen, features), jnp.bfloat16),
            struct((seqlen, features), jnp.float32),
            struct((seqlen, features), jnp.float32),
        ),
        in_specs=[SMEM] + [VMEM] * 5,
        out_specs=(VMEM,) * 4,
        compiler_params=pltpu.CompilerParams(vmem_limit_bytes=24 << 20),
        cost_estimate=pl.CostEstimate(
            flops=8 * seqlen * features * features + 8 * HEADS * seqlen * seqlen * 128,
            bytes_accessed=attn_w.size * 4 + source.size * 20,
            transcendentals=2 * HEADS * seqlen * seqlen,
        ),
    )(place, source, modulation, offsets, attn_w, attn_w_other)


def run_mlp(mlp_orders, place, lefts, middle, attn_out, upstream, modulation, offsets, up_ws, down_ws):
    seqlen, features = middle.shape
    chips, steps, rows, _ = up_ws[0].shape
    half = features // 2
    whole = (seqlen, features)
    return pl.pallas_call(
        functools.partial(mlp_both_ways, *mlp_orders),
        name="mlp_both_ways",
        grid=(steps,),
        out_shape=(
            struct(whole, jnp.bfloat16),
            struct((steps,) + whole, jnp.bfloat16),
            struct((steps + 1, seqlen, half), jnp.bfloat16),
            struct((steps + 1, seqlen, half), jnp.bfloat16),
            struct(whole, jnp.float32),
            struct(whole, jnp.bfloat16),
            struct(offsets.shape, jnp.float32),
        ),
        in_specs=[
            SMEM,
            pl.BlockSpec((1,) + whole, lambda step: (2, 0, 0)),
            resident(whole),
            resident(whole),
            resident(whole),
            resident(modulation.shape),
            resident(offsets.shape),
        ]
        + [pl.BlockSpec((chips, 1, rows, half), lambda step: (0, step, 0, 0))] * 4,
        out_specs=(
            resident(whole),
            pl.BlockSpec((1,) + whole, lambda step: (step, 0, 0)),
            resident((steps + 1, seqlen, half)),
            resident((steps + 1, seqlen, half)),
            resident(whole),
            resident(whole),
            resident(offsets.shape),
        ),
        scratch_shapes=[
            pltpu.VMEM(whole, jnp.float32),
            pltpu.VMEM(whole, jnp.float32),
            pltpu.VMEM(whole, jnp.bfloat16),
        ],
        compiler_params=pltpu.CompilerParams(vmem_limit_bytes=28 << 20),
        cost_estimate=pl.CostEstimate(
            flops=8 * seqlen * features * features * steps,
            bytes_accessed=up_ws[0].size * 8 + seqlen * features * 40,
            transcendentals=seqlen * features * steps,
        ),
    )(place, lefts, middle, attn_out, upstream, modulation, offsets, *up_ws, *down_ws)


def run_attention_backward(
    order, place, source, modulation, attn_w, attn_w_other, qkv, grad_middle, grad_attn, rows
):
    seqlen, features = source.shape
    half = features // 2
    return pl.pallas_call(
        functools.partial(attention_backward, order),
        name="attention_backward",
        out_shape=(
            struct((seqlen, features), jnp.float32),
            struct((4, seqlen, half), jnp.bfloat16),
            struct((4, seqlen, half), jnp.bfloat16),
            struct(rows.shape, jnp.float32),
        ),
        in_specs=[SMEM] + [VMEM] * 8,
        out_specs=(VMEM,) * 4,
        scratch_shapes=[
            pltpu.VMEM((3, seqlen, features), jnp.bfloat16),
            pltpu.VMEM((seqlen, features), jnp.bfloat16),
        ],
        compiler_params=pltpu.CompilerParams(vmem_limit_bytes=24 << 20),
        cost_estimate=pl.CostEstimate(
            flops=8 * seqlen * features * features + 20 * HEADS * seqlen * seqlen * 128,
            bytes_accessed=attn_w.size * 4 + source.size * 24,
            transcendentals=2 * HEADS * seqlen * seqlen,
        ),
    )(place, source, modulation, attn_w, attn_w_other, qkv, grad_middle, grad_attn, rows)


def run_products(lefts, lefts_other, rights, rights_other, left_at, right_at, count, mine, chunk):
    _, seqlen, features = lefts.shape
    width = rights.shape[-1]
    left_spec = pl.BlockSpec((1, seqlen, features), lambda step: (left_at(step), 0, 0))
    right_spec = pl.BlockSpec((1, seqlen, width), lambda step: (right_at(step), 0, 0))
    specs = [left_spec, left_spec, right_spec, right_spec]
    cost = pl.CostEstimate(
        flops=4 * count * seqlen * features * width,
        bytes_accessed=count * features * width * 6,
        transcendentals=0,
    )
    if chunk % 16:
        total = pl.pallas_call(
            plain_products,
            name="plain_products",
            grid=(count,),
            out_shape=struct((count, features, width), jnp.float32),
            in_specs=specs,
            out_specs=pl.BlockSpec((1, features, width), lambda step: (step, 0, 0)),
            cost_estimate=cost,
        )(lefts, lefts_other, rights, rights_other)
        keep, send = split_bit(
            total.reshape(count, features // (2 * chunk), 2, chunk, width), mine, 2, jnp.bfloat16
        )
        shape = (count, features // 2, width)
        return keep.reshape(shape), send.reshape(shape)
    half_spec = pl.BlockSpec((1, features // 2, width), lambda step: (step, 0, 0))
    return pl.pallas_call(
        functools.partial(pair_products, chunk),
        name="pair_products",
        grid=(count,),
        out_shape=(
            struct((count, features // 2, width), jnp.float32),
            struct((count, features // 2, width), jnp.bfloat16),
        ),
        in_specs=[SMEM] + specs,
        out_specs=(half_spec, half_spec),
        cost_estimate=cost,
    )(mine[None], lefts, lefts_other, rights, rights_other)


def muon_steps(block, scaled_ref):
    values = block.astype(jnp.float32)
    scaled_ref[...] = (values / (jnp.sqrt(jnp.sum(values * values)) + 1e-07)).astype(jnp.bfloat16)

    @pl.loop(0, NS_ITERS)
    def _(iteration):
        scaled = scaled_ref[...]
        gram = contract(scaled, scaled, 1, 1).astype(jnp.bfloat16)
        square = contract(gram, gram, 1, 0)
        mixed = (COEF_SECOND * gram.astype(jnp.float32) + COEF_THIRD * square).astype(jnp.bfloat16)
        scaled_ref[...] = (
            COEF_FIRST * scaled.astype(jnp.float32) + contract(mixed, scaled, 1, 0)
        ).astype(jnp.bfloat16)


def orthogonalize_halves(place_ref, mine_ref, other_ref, out_ref, scaled_ref):
    core = place_ref[0]
    mine, other = mine_ref[...], other_ref[...]
    low, high = jnp.where(core == 1, other, mine), jnp.where(core == 1, mine, other)
    muon_steps(jnp.concatenate([low, high], axis=1), scaled_ref)
    out_ref[...] = split_columns(scaled_ref[...], core)[0]


def orthogonalize_whole(block_ref, out_ref):
    muon_steps(block_ref[0], out_ref.at[0])


def muon_cost(count, rows):
    return pl.CostEstimate(
        flops=6 * count * NS_ITERS * rows**3, bytes_accessed=4 * count * rows**2, transcendentals=0
    )


def run_orthogonalize_halves(place, mine, other):
    return pl.pallas_call(
        orthogonalize_halves,
        name="orthogonalize_halves",
        out_shape=struct(mine.shape, mine.dtype),
        in_specs=[SMEM, VMEM, VMEM],
        out_specs=VMEM,
        scratch_shapes=[pltpu.VMEM((mine.shape[0], 2 * mine.shape[1]), mine.dtype)],
        compiler_params=pltpu.CompilerParams(vmem_limit_bytes=24 << 20),
        cost_estimate=muon_cost(1, mine.shape[0]),
    )(place, mine, other)


def run_orthogonalize_whole(blocks):
    spec = pl.BlockSpec((1,) + blocks.shape[1:], lambda step: (step, 0, 0))
    return pl.pallas_call(
        orthogonalize_whole,
        name="orthogonalize_whole",
        grid=(blocks.shape[0],),
        out_shape=struct(blocks.shape, blocks.dtype),
        in_specs=[spec],
        out_specs=spec,
        compiler_params=pltpu.CompilerParams(vmem_limit_bytes=24 << 20),
        cost_estimate=muon_cost(*blocks.shape[:2]),
    )(blocks)


def all_to_all(values):
    return lax.all_to_all(values, "dp", split_axis=0, concat_axis=0, tiled=True)


def to_all(row):
    devices = lax.axis_size("dp")
    return all_to_all(jnp.broadcast_to(row[None], (devices,) + row.shape))


def on_device(latents, conditioning, cotangent, weights, biases, momenta, bias_momenta, counts):
    _, seqlen, features = latents.shape
    block_count, share, _ = weights.shape
    hidden_blocks = (block_count - 10) // 2
    bias_count = biases.shape[0]
    devices = lax.axis_size("dp")
    myself = lax.axis_index("dp")
    core = bit_of(myself, 0)
    bits = index_bits(devices)
    orders = colour_orders(devices)
    ranks = jnp.arange(devices, dtype=jnp.int32)
    live_here = jnp.sum(jnp.where(ranks == myself, counts, 0)) > 0

    lowered = weights.astype(jnp.bfloat16)
    ada_w = lowered[:ADA]
    condition = conditioning[0].astype(jnp.float32)
    silu_cond = jax.nn.silu(condition).astype(jnp.bfloat16)

    half = features // 2
    rest = lowered[ADA:]
    columns_mine = lax.dynamic_slice_in_dim(rest, core * half, half, 2)
    columns_other = lax.dynamic_slice_in_dim(rest, (1 - core) * half, half, 2)
    columns_other = flip(columns_other, 0)
    chip_rows = jnp.where(
        core == 1,
        jnp.concatenate([columns_other, columns_mine], axis=1),
        jnp.concatenate([columns_mine, columns_other], axis=1),
    )
    bounds = [0, 10 - ADA, 10 - ADA + hidden_blocks, block_count - ADA]
    stages = bits - 1
    small_all = to_all(
        jnp.concatenate([silu_cond, biases.astype(jnp.bfloat16).reshape(-1)])
    )

    def modulations(small_all):
        silu_rows = lax.dynamic_slice_in_dim(small_all[:, :features], myself * share, share, 1)
        mod_parts = product("ld,kde->lke", silu_rows, ada_w).reshape(devices, ADA * features)
        offsets = (
            small_all[:, features:]
            .reshape(devices, bias_count, share)
            .transpose(1, 0, 2)
            .reshape(bias_count, features)
            .astype(jnp.float32)
        )
        return small_all, silu_rows, offsets, all_to_all(mod_parts)

    groups, (small_all, silu_rows, offsets, mod_sums) = gather_all(
        [chip_rows[low:high] for low, high in zip(bounds[:-1], bounds[1:])],
        [tuple(reversed(order)) for order in orders],
        myself,
        small_all,
        modulations,
    )
    modulation = jnp.sum(mod_sums, axis=0).reshape(ADA, features) + offsets[:ADA]
    rows = 2 * share
    held_orders = [tuple(reversed(order)) for order in orders]
    pairs = []
    for index, order in enumerate(held_orders):
        group = groups[index].reshape(devices // 2, -1, rows, half)
        if rows % 16:
            group = jnp.stack([group[place] for place in chunk_places(order)], axis=1)
            group = group.reshape(1, -1, features, half)
            held_orders[index] = ()
        pairs.append((group, flip(group, 0)))
    attn_ws, up_ws, down_ws = pairs

    place = jnp.stack([core, live_here.astype(jnp.int32)]).astype(jnp.int32)
    extra = max(0, block_count - devices // 2)
    assert extra % 2 == 0 and extra <= ADA
    main = block_count - extra
    spare = ()
    spare_bits = tuple(reversed(range(1, bits)))
    if extra:
        spare = momenta[:extra].astype(jnp.bfloat16).reshape(2, extra // 2, share, features)
        spare_mine = lax.dynamic_index_in_dim(spare, core, 0, keepdims=False)
        spare_other = lax.dynamic_index_in_dim(spare, 1 - core, 0, keepdims=False)
        spare_other = flip(spare_other, 0)
        spare = joined(spare_mine, spare_other, core, 1).reshape(extra // 2, 2 * share, features)
        modulation, spare = lax.optimization_barrier((modulation, spare))
        spare = gather_step(spare, spare_bits, spare_bits[0], myself)
        for bit in spare_bits[1:-2]:
            spare = gather_step(spare, spare_bits, bit, myself)
        received = flip_by_core(spare, spare_bits[-2], spare_bits[-1])
        near = jnp.stack([spare, received])
        far = flip_by_core(near, spare_bits[-1], spare_bits[-2])
        spare = corner_rows(near, far, spare_bits, myself)
        spare = spare.reshape(extra // 2, features, features)
    lefts, qkv, attn_out, middle = run_attention_forward(
        held_orders[0], place, latents[0], modulation, offsets, *attn_ws
    )
    lefts_other = flip(lefts, 0)
    output, hidden, mlp_keep, mlp_send, grad_middle, grad_attn, rows = run_mlp(
        held_orders[1:],
        place,
        lefts,
        middle,
        attn_out,
        cotangent[0],
        modulation,
        offsets,
        up_ws,
        down_ws,
    )
    hidden_other = flip(hidden, 0)
    mlp_other = flip(mlp_send, 0)

    def spread(mats, count):
        return mats.reshape((mats.shape[0],) + (2,) * count + (2 * share, half))

    def products(left, left_other, right, right_other, left_at, right_at, count, order):
        return run_products(
            left,
            left_other,
            right,
            right_other,
            left_at,
            right_at,
            count,
            bit_of(myself, order[0]),
            share << order[0],
        )

    down_halves = products(
        hidden, hidden_other, mlp_keep, mlp_other, lambda b: b, lambda b: 0, hidden_blocks, orders[0]
    )
    up_halves = products(
        lefts, lefts_other, mlp_keep, mlp_other, lambda b: 2, lambda b: b + 1, hidden_blocks, orders[1]
    )
    input_grad, attn_keep, attn_send, grad_offsets = run_attention_backward(
        held_orders[0], place, latents[0], modulation, *attn_ws, qkv, grad_middle, grad_attn, rows
    )
    attn_other = flip(attn_send, 0)
    attn_halves = products(
        lefts, lefts_other, attn_keep, attn_other, lambda b: b // 3, lambda b: b, 4, orders[2]
    )

    grad_mod_b = grad_offsets[:ADA].astype(jnp.bfloat16).reshape(-1)
    by_holder = (
        grad_offsets.reshape(bias_count, devices, share)
        .transpose(1, 0, 2)
        .reshape(devices, bias_count * share)
    )
    coarse = lax.reduce_precision(by_holder, 8, 7)
    mod_and_offsets = jnp.concatenate(
        [
            jnp.broadcast_to(grad_mod_b[None], (devices, ADA * features)),
            coarse.astype(jnp.bfloat16),
            (by_holder - coarse).astype(jnp.bfloat16),
        ],
        axis=1,
    )
    mod_and_offsets = all_to_all(mod_and_offsets)

    def conditioning_grads(mod_and_offsets):
        mod_all = mod_and_offsets[:, : ADA * features].reshape(devices, ADA, features)
        silu_parts = product("lke,kde->ld", mod_all, ada_w)
        return mod_and_offsets, mod_all, all_to_all(silu_parts)

    sums, (mod_and_offsets, mod_all, grad_silu) = scatter_all(
        [attn_halves, up_halves, down_halves],
        [orders[2], orders[1], orders[0]],
        myself,
        1,
        spread,
        {stages - 1: lambda _: conditioning_grads(mod_and_offsets)},
    )
    chip_rows = jnp.concatenate(sums, axis=0)
    rows_mine = lax.dynamic_slice_in_dim(chip_rows, core * share, share, 1)
    rows_other = flip(lax.dynamic_slice_in_dim(chip_rows, (1 - core) * share, share, 1), 0)
    rest_share = jnp.where(
        core == 1,
        jnp.concatenate([rows_other, rows_mine], axis=2),
        jnp.concatenate([rows_mine, rows_other], axis=2),
    )

    ada_share = product("ld,lke->kde", silu_rows, mod_all)
    offset_share = jnp.sum(
        mod_and_offsets[:, ADA * features :]
        .astype(jnp.float32)
        .reshape(devices * 2, bias_count, share),
        axis=0,
    )

    grad_scale = lax.rsqrt((seqlen * jnp.sum(counts)).astype(jnp.float32))
    weight_grads = jnp.concatenate([ada_share, rest_share], axis=0) * grad_scale
    bias_grads = offset_share * grad_scale
    new_momenta = BETA_WEIGHT * momenta + weight_grads
    new_bias_momenta = BETA_BIAS * bias_momenta + bias_grads
    new_biases = biases - RATE_BIAS * new_bias_momenta

    outgoing = (
        new_momenta[extra:]
        .astype(jnp.bfloat16)
        .reshape(main, share, 2, half)
        .transpose(0, 2, 1, 3)
        .reshape(2 * main, share, half)
    )
    outgoing = jnp.pad(outgoing, ((0, devices - 2 * main), (0, 0), (0, 0)))
    columns_mine = all_to_all(outgoing).reshape(features, half)
    ortho_half = run_orthogonalize_halves(place, columns_mine, flip(columns_mine, 0))
    ortho_local = (
        all_to_all(ortho_half.reshape(devices, share, half))[: 2 * main]
        .reshape(main, 2, share, half)
        .transpose(0, 2, 1, 3)
        .reshape(main, share, features)
    )
    if extra:
        silu_all = small_all[:, :features]
        mod_mine = lax.dynamic_slice_in_dim(mod_all, core * (extra // 2), extra // 2, 1)
        spare_grads = product("ld,lke->kde", silu_all, mod_mine) * grad_scale
        spare = (BETA_WEIGHT * spare.astype(jnp.float32) + spare_grads).astype(jnp.bfloat16)
        spare_ortho = run_orthogonalize_whole(spare)
        chip_ortho = lax.dynamic_slice_in_dim(
            spare_ortho, (myself - core) * share, 2 * share, 1
        ).reshape(extra // 2, 2, share, features)
        ortho_mine = lax.dynamic_index_in_dim(chip_ortho, core, 1, keepdims=False)
        ortho_other = flip(
            lax.dynamic_index_in_dim(chip_ortho, 1 - core, 1, keepdims=False), 0
        )
        spare_local = joined(ortho_mine, ortho_other, core, 0).reshape(extra, share, features)
        ortho_local = jnp.concatenate([spare_local, ortho_local])
    silu_back = jax.vjp(jax.nn.silu, condition)[1]
    cond_grad = silu_back(grad_silu.reshape(features))[0] * seqlen ** (-0.5)
    new_weights = weights - RATE_WEIGHT * ortho_local.astype(jnp.float32)
    cond_grad = jnp.where(live_here, cond_grad, jnp.zeros_like(cond_grad))[None]
    return (
        output[None],
        input_grad[None],
        cond_grad,
        weight_grads,
        bias_grads,
        new_weights,
        new_momenta,
        new_biases,
        new_bias_momenta,
    )


def solution(mesh):
    return jax.shard_map(
        on_device,
        mesh=mesh,
        in_specs=(
            P("dp", None, None),
            P("dp", None),
            P("dp", None, None),
            P(None, "dp", None),
            P(None, "dp"),
            P(None, "dp", None),
            P(None, "dp"),
            P(),
        ),
        out_specs=(
            P("dp", None, None),
            P("dp", None, None),
            P("dp", None),
            P(None, "dp", None),
            P(None, "dp"),
            P(None, "dp", None),
            P(None, "dp", None),
            P(None, "dp"),
            P(None, "dp"),
        ),
        check_vma=False,
    )
```

```python
import functools

import jax
import jax.numpy as jnp
from jax import lax
from jax.experimental import pallas as pl
from jax.experimental.pallas import tpu as pltpu
from jax.sharding import PartitionSpec as P


HEADS = 12
NS_ITERS = 2
ADA = 6
COLOURS = 3

COEF_FIRST = 3.4445
COEF_SECOND = -4.775
COEF_THIRD = 2.0315
BETA_WEIGHT = 0.95
BETA_BIAS = 0.9
RATE_WEIGHT = 1.0
RATE_BIAS = 0.1
NORM_EPS = 1e-06


def product(spec, left, right):
    return jnp.einsum(spec, left, right, preferred_element_type=jnp.float32)


def flip(values, bit):
    devices = lax.axis_size("dp")
    return lax.ppermute(values, "dp", [(i, i ^ (1 << bit)) for i in range(devices)])


def bit_of(myself, bit):
    return (myself >> bit) & 1


def joined(values, other, taken, axis):
    return jnp.where(
        taken == 1, jnp.stack([other, values], axis), jnp.stack([values, other], axis)
    )


def gather_all(groups, orders, myself, first_too, last_too):
    carried = first_too
    for stage in range(len(orders[0])):
        others = [flip(group, order[stage]) for group, order in zip(groups, orders)]
        if stage == len(orders[0]) - 1:
            carried = last_too(carried)
        if stage in (0, len(orders[0]) - 1):
            others[-1], carried = lax.optimization_barrier((others[-1], carried))
        for index, order in enumerate(orders):
            bit = order[stage]
            groups[index] = joined(groups[index], others[index], bit_of(myself, bit), 0)
    return groups, carried


def gather_step(values, order, bit, myself):
    held = order[: order.index(bit)]
    position = 1 + sum(1 for before in held if before > bit)
    return joined(values, flip(values, bit), bit_of(myself, bit), position)


def flip_by_core(values, first_bit, second_bit):
    devices = lax.axis_size("dp")
    return lax.ppermute(
        values, "dp", [(i, i ^ (1 << (second_bit if i & 1 else first_bit))) for i in range(devices)]
    )


def corner_rows(near, far, order, myself):
    high, low = bit_of(myself, order[-2]), bit_of(myself, order[-1])
    core = bit_of(myself, 0)
    first, second = jnp.where(core == 1, low, high), jnp.where(core == 1, high, low)
    axis = len(order) - 1
    pairs = [
        joined(pair[0], pair[1], first, axis) for pair in (near, far)
    ]
    by_first = joined(pairs[0], pairs[1], second, axis)
    return jnp.where(core == 1, by_first, jnp.swapaxes(by_first, axis, axis + 1))


def split_bit(values, mine, position, sent_as):
    send = lax.dynamic_index_in_dim(values, 1 - mine, position, keepdims=False)
    keep = lax.dynamic_index_in_dim(values, mine, position, keepdims=False)
    return keep, send.astype(sent_as)


def scatter_all(halves, orders, myself, axis, spread, between):
    left = [sorted(order, reverse=True) for order in orders]
    carried = None
    totals = []
    for stage in range(len(orders[0])):
        others = [flip(send, order[stage]) for (_, send), order in zip(halves, orders)]
        if stage in between:
            carried = between[stage](carried)
            others[-1], carried = lax.optimization_barrier((others[-1], carried))
        totals = [
            keep + other.astype(jnp.float32) for (keep, _), other in zip(halves, others)
        ]
        for index, order in enumerate(orders):
            left[index].remove(order[stage])
            if stage == 0:
                totals[index] = spread(totals[index], len(left[index]))
            if left[index]:
                bit = order[stage + 1]
                position = axis + left[index].index(bit)
                halves[index] = split_bit(
                    totals[index], bit_of(myself, bit), position, jnp.bfloat16
                )
    return totals, carried


def index_bits(devices):
    return devices.bit_length() - 1


def colour_orders(devices):
    chip_bits = list(range(1, index_bits(devices)))
    rest, last = chip_bits[:-1], chip_bits[-1:]
    shifts = [(colour * len(rest)) // COLOURS for colour in range(COLOURS)]
    return [tuple(rest[shift:] + rest[:shift] + last) for shift in shifts]


def contract(left, right, left_dim, right_dim):
    return lax.dot_general(
        left, right, (((left_dim,), (right_dim,)), ((), ())), preferred_element_type=jnp.float32
    )


def layer_norm(stream):
    centred = stream - jnp.mean(stream, axis=-1, keepdims=True)
    inverse = lax.rsqrt(jnp.mean(centred * centred, axis=-1, keepdims=True) + NORM_EPS)
    return (centred * inverse, inverse)


def norm_back(normed, inverse, upstream):
    return inverse * (
        upstream
        - jnp.mean(upstream, axis=-1, keepdims=True)
        - normed * jnp.mean(upstream * normed, axis=-1, keepdims=True)
    )


def column_sum(values):
    return jnp.sum(values, axis=0, keepdims=True)


def scores_of(query, keys, width):
    return contract(query, keys, 1, 1) * width ** (-0.5)


def chunk_places(order):
    count = len(order)
    return [
        sum(((chip >> (bit - 1)) & 1) << place for place, bit in enumerate(order))
        for chip in range(1 << count)
    ]


def whole_weight(mine_ref, other_ref, index, core, order):
    places = chunk_places(order) if order else [0]
    mine, other = [
        jnp.concatenate([ref[place, index] for place in places], axis=0)
        for ref in (mine_ref, other_ref)
    ]
    return jnp.concatenate(
        [jnp.where(core == 1, other, mine), jnp.where(core == 1, mine, other)], axis=1
    )


def attention_forward(
    order,
    place_ref,
    source_ref,
    mod_ref,
    offsets_ref,
    mine_ref,
    other_ref,
    lefts_ref,
    qkv_ref,
    attn_ref,
    middle_ref,
):
    core = place_ref[0]
    seqlen, features = source_ref.shape
    width = features // HEADS
    stream = source_ref[...].astype(jnp.float32)
    normed, _ = layer_norm(stream)
    attn_input = (normed * (1.0 + mod_ref[1:2]) + mod_ref[0:1]).astype(jnp.bfloat16)
    lefts_ref[0] = attn_input
    qkv_ref[0] = (contract(attn_input, whole_weight(mine_ref, other_ref, 0, core, order), 1, 0) + offsets_ref[6:7]).astype(
        jnp.bfloat16
    )
    qkv_ref[1] = contract(attn_input, whole_weight(mine_ref, other_ref, 1, core, order), 1, 0).astype(jnp.bfloat16)
    qkv_ref[2] = (contract(attn_input, whole_weight(mine_ref, other_ref, 2, core, order), 1, 0) + offsets_ref[7:8]).astype(
        jnp.bfloat16
    )
    first = lax.broadcasted_iota(jnp.int32, (seqlen, 2 * width), 1) < width
    for pair in range(HEADS // 2):
        columns = slice(2 * width * pair, 2 * width * (pair + 1))
        query, keys, values = qkv_ref[0, :, columns], qkv_ref[1, :, columns], qkv_ref[2, :, columns]
        halves = []
        for mask in (first, jnp.logical_not(first)):
            scores = scores_of(jnp.where(mask, query, jnp.zeros_like(query)), keys, width)
            log_total = jnp.log(jnp.sum(jnp.exp(scores), axis=-1, keepdims=True))
            probs = jnp.exp(scores - log_total).astype(jnp.bfloat16)
            halves.append(contract(probs, values, 1, 0))
        lefts_ref[1, :, columns] = jnp.where(first, *halves).astype(jnp.bfloat16)
    attn_out = contract(lefts_ref[1], whole_weight(mine_ref, other_ref, 3, core, order), 1, 0) + offsets_ref[8:9]
    attn_ref[...] = attn_out
    middle = stream + mod_ref[2:3] * attn_out
    middle_ref[...] = middle
    normed_two, _ = layer_norm(middle)
    lefts_ref[2] = (normed_two * (1.0 + mod_ref[4:5]) + mod_ref[3:4]).astype(jnp.bfloat16)


def split_columns(values, core):
    width = values.shape[-1] // 2
    low, high = values[:, :width], values[:, width:]
    return (jnp.where(core == 1, high, low), jnp.where(core == 1, low, high))


def mlp_both_ways(
    up_order,
    down_order,
    place_ref,
    lefts_ref,
    middle_ref,
    attn_ref,
    upstream_ref,
    mod_ref,
    offsets_ref,
    up_ref,
    up_other_ref,
    down_ref,
    down_other_ref,
    output_ref,
    hidden_ref,
    keep_ref,
    send_ref,
    grad_middle_ref,
    grad_attn_ref,
    rows_ref,
    total_ref,
    grad_total_ref,
    grad_mlp_ref,
):
    step = pl.program_id(0)
    last = pl.num_programs(0) - 1
    core, live = place_ref[0], place_ref[1] > 0
    scale = 0.7978845608028654

    @pl.when(step == 0)
    def _():
        total_ref[...] = jnp.zeros_like(total_ref)
        grad_total_ref[...] = jnp.zeros_like(grad_total_ref)
        grad_mlp = jnp.where(live, upstream_ref[...].astype(jnp.float32) * mod_ref[5:6], 0.0)
        grad_mlp_b = grad_mlp.astype(jnp.bfloat16)
        grad_mlp_ref[...] = grad_mlp_b
        keep_ref[0], send_ref[0] = split_columns(grad_mlp_b, core)
        rows_ref[...] = jnp.zeros_like(rows_ref)
        rows_ref[pl.ds(10 + last, 1)] = column_sum(grad_mlp)

    up_w = whole_weight(up_ref, up_other_ref, 0, core, up_order)
    down_w = whole_weight(down_ref, down_other_ref, 0, core, down_order)
    before = contract(lefts_ref[0], up_w, 1, 0) + offsets_ref[pl.ds(9 + step, 1)]
    square = before * before
    bend = jnp.tanh(scale * (before + 0.044715 * square * before))
    hidden = (0.5 * before * (1.0 + bend)).astype(jnp.bfloat16)
    hidden_ref[0] = hidden
    total_ref[...] += contract(hidden, down_w, 1, 0)
    slope = 0.5 * (1.0 + bend) + 0.5 * before * (1.0 - bend * bend) * scale * (
        1.0 + 3.0 * 0.044715 * square
    )
    grad_pre = jnp.where(live, contract(grad_mlp_ref[...], down_w, 1, 1) * slope, 0.0)
    grad_pre_b = grad_pre.astype(jnp.bfloat16)
    keep_ref[step + 1], send_ref[step + 1] = split_columns(grad_pre_b, core)
    rows_ref[pl.ds(9 + step, 1)] = column_sum(grad_pre)
    grad_total_ref[...] += contract(grad_pre_b, up_w, 1, 1)

    @pl.when(step == last)
    def _():
        middle = middle_ref[...]
        grad_out = upstream_ref[...].astype(jnp.float32)
        mlp_out = total_ref[...] + offsets_ref[pl.ds(10 + last, 1)]
        output = middle + mod_ref[5:6] * mlp_out
        output_ref[...] = jnp.where(live, output, 0.0).astype(jnp.bfloat16)
        rows_ref[5:6] = jnp.where(live, column_sum(grad_out * mlp_out), 0.0)
        normed, inverse = layer_norm(middle)
        grad_in = grad_total_ref[...]
        rows_ref[3:4] = column_sum(grad_in)
        rows_ref[4:5] = column_sum(grad_in * normed)
        grad_middle = grad_out + norm_back(normed, inverse, grad_in * (1.0 + mod_ref[4:5]))
        grad_middle = jnp.where(live, grad_middle, 0.0)
        grad_middle_ref[...] = grad_middle
        rows_ref[2:3] = column_sum(grad_middle * attn_ref[...])
        grad_attn = grad_middle * mod_ref[2:3]
        grad_attn_ref[...] = grad_attn.astype(jnp.bfloat16)
        rows_ref[8:9] = column_sum(grad_attn)


def attention_backward(
    order,
    place_ref,
    source_ref,
    mod_ref,
    mine_ref,
    other_ref,
    qkv_ref,
    grad_middle_ref,
    grad_attn_ref,
    rows_in_ref,
    grad_source_ref,
    keep_ref,
    send_ref,
    rows_ref,
    grads_ref,
    context_ref,
):
    seqlen, features = source_ref.shape
    width = features // HEADS
    core, live = place_ref[0], place_ref[1] > 0
    rows_ref[...] = rows_in_ref[...]
    grad_attn = grad_attn_ref[...]
    keep_ref[3], send_ref[3] = split_columns(grad_attn, core)
    context_ref[...] = contract(
        grad_attn, whole_weight(mine_ref, other_ref, 3, core, order), 1, 1
    ).astype(jnp.bfloat16)
    first = lax.broadcasted_iota(jnp.int32, (seqlen, 2 * width), 1) < width
    for pair in range(HEADS // 2):
        columns = slice(2 * width * pair, 2 * width * (pair + 1))
        query, keys, values = qkv_ref[0, :, columns], qkv_ref[1, :, columns], qkv_ref[2, :, columns]
        upstream = context_ref[:, columns]
        parts = []
        for mask in (first, jnp.logical_not(first)):
            scores = scores_of(jnp.where(mask, query, jnp.zeros_like(query)), keys, width)
            log_total = jnp.log(jnp.sum(jnp.exp(scores), axis=-1, keepdims=True))
            probs = jnp.exp(scores - log_total)
            grad_values = contract(probs.astype(jnp.bfloat16), upstream, 0, 0)
            grad_probs = contract(
                jnp.where(mask, upstream, jnp.zeros_like(upstream)), values, 1, 1
            )
            row_dot = jnp.sum(probs * grad_probs, axis=-1, keepdims=True)
            grad_scores = (probs * (grad_probs - row_dot) * width ** (-0.5)).astype(jnp.bfloat16)
            parts.append(
                (
                    contract(grad_scores, keys, 1, 0),
                    contract(grad_scores, query, 0, 0),
                    grad_values,
                )
            )
        for index in range(3):
            merged = jnp.where(live, jnp.where(first, parts[0][index], parts[1][index]), 0.0)
            grads_ref[index, :, columns] = merged.astype(jnp.bfloat16)
            if index != 1:
                row = 6 if index == 0 else 7
                rows_ref[row : row + 1, columns] = column_sum(merged)
    grad_in = jnp.zeros((seqlen, features), jnp.float32)
    for index in range(3):
        grads = grads_ref[index]
        keep_ref[index], send_ref[index] = split_columns(grads, core)
        grad_in += contract(grads, whole_weight(mine_ref, other_ref, index, core, order), 1, 1)
    normed, inverse = layer_norm(source_ref[...].astype(jnp.float32))
    rows_ref[0:1] = column_sum(grad_in)
    rows_ref[1:2] = column_sum(grad_in * normed)
    grad_source_ref[...] = jnp.where(
        live,
        grad_middle_ref[...] + norm_back(normed, inverse, grad_in * (1.0 + mod_ref[1:2])),
        0.0,
    )


def pair_products(
    chunk, mine_ref, left_ref, left_other_ref, right_ref, right_other_ref, keep_ref, send_ref
):
    total = contract(left_ref[0], right_ref[0], 0, 0) + contract(
        left_other_ref[0], right_other_ref[0], 0, 0
    )
    for start in range(0, total.shape[0] // 2, chunk):
        low = total[2 * start : 2 * start + chunk]
        high = total[2 * start + chunk : 2 * start + 2 * chunk]
        mine = mine_ref[0] == 1
        keep_ref[0, start : start + chunk] = jnp.where(mine, high, low)
        send_ref[0, start : start + chunk] = jnp.where(mine, low, high).astype(jnp.bfloat16)


def plain_products(left_ref, left_other_ref, right_ref, right_other_ref, out_ref):
    out_ref[0] = contract(left_ref[0], right_ref[0], 0, 0) + contract(
        left_other_ref[0], right_other_ref[0], 0, 0
    )


def struct(shape, dtype):
    return jax.ShapeDtypeStruct(shape, dtype)


VMEM = pl.BlockSpec(memory_space=pltpu.VMEM)
SMEM = pl.BlockSpec(memory_space=pltpu.SMEM)


def resident(shape):
    zeros = (0,) * len(shape)
    return pl.BlockSpec(shape, lambda step: zeros)


def run_attention_forward(order, place, source, modulation, offsets, attn_w, attn_w_other):
    seqlen, features = source.shape
    return pl.pallas_call(
        functools.partial(attention_forward, order),
        name="attention_forward",
        out_shape=(
            struct((3, seqlen, features), jnp.bfloat16),
            struct((3, seqlen, features), jnp.bfloat16),
            struct((seqlen, features), jnp.float32),
            struct((seqlen, features), jnp.float32),
        ),
        in_specs=[SMEM] + [VMEM] * 5,
        out_specs=(VMEM,) * 4,
        compiler_params=pltpu.CompilerParams(vmem_limit_bytes=24 << 20),
        cost_estimate=pl.CostEstimate(
            flops=8 * seqlen * features * features + 8 * HEADS * seqlen * seqlen * 128,
            bytes_accessed=attn_w.size * 4 + source.size * 20,
            transcendentals=2 * HEADS * seqlen * seqlen,
        ),
    )(place, source, modulation, offsets, attn_w, attn_w_other)


def run_mlp(mlp_orders, place, lefts, middle, attn_out, upstream, modulation, offsets, up_ws, down_ws):
    seqlen, features = middle.shape
    chips, steps, rows, _ = up_ws[0].shape
    half = features // 2
    whole = (seqlen, features)
    return pl.pallas_call(
        functools.partial(mlp_both_ways, *mlp_orders),
        name="mlp_both_ways",
        grid=(steps,),
        out_shape=(
            struct(whole, jnp.bfloat16),
            struct((steps,) + whole, jnp.bfloat16),
            struct((steps + 1, seqlen, half), jnp.bfloat16),
            struct((steps + 1, seqlen, half), jnp.bfloat16),
            struct(whole, jnp.float32),
            struct(whole, jnp.bfloat16),
            struct(offsets.shape, jnp.float32),
        ),
        in_specs=[
            SMEM,
            pl.BlockSpec((1,) + whole, lambda step: (2, 0, 0)),
            resident(whole),
            resident(whole),
            resident(whole),
            resident(modulation.shape),
            resident(offsets.shape),
        ]
        + [pl.BlockSpec((chips, 1, rows, half), lambda step: (0, step, 0, 0))] * 4,
        out_specs=(
            resident(whole),
            pl.BlockSpec((1,) + whole, lambda step: (step, 0, 0)),
            resident((steps + 1, seqlen, half)),
            resident((steps + 1, seqlen, half)),
            resident(whole),
            resident(whole),
            resident(offsets.shape),
        ),
        scratch_shapes=[
            pltpu.VMEM(whole, jnp.float32),
            pltpu.VMEM(whole, jnp.float32),
            pltpu.VMEM(whole, jnp.bfloat16),
        ],
        compiler_params=pltpu.CompilerParams(vmem_limit_bytes=28 << 20),
        cost_estimate=pl.CostEstimate(
            flops=8 * seqlen * features * features * steps,
            bytes_accessed=up_ws[0].size * 8 + seqlen * features * 40,
            transcendentals=seqlen * features * steps,
        ),
    )(place, lefts, middle, attn_out, upstream, modulation, offsets, *up_ws, *down_ws)


def run_attention_backward(
    order, place, source, modulation, attn_w, attn_w_other, qkv, grad_middle, grad_attn, rows
):
    seqlen, features = source.shape
    half = features // 2
    return pl.pallas_call(
        functools.partial(attention_backward, order),
        name="attention_backward",
        out_shape=(
            struct((seqlen, features), jnp.float32),
            struct((4, seqlen, half), jnp.bfloat16),
            struct((4, seqlen, half), jnp.bfloat16),
            struct(rows.shape, jnp.float32),
        ),
        in_specs=[SMEM] + [VMEM] * 8,
        out_specs=(VMEM,) * 4,
        scratch_shapes=[
            pltpu.VMEM((3, seqlen, features), jnp.bfloat16),
            pltpu.VMEM((seqlen, features), jnp.bfloat16),
        ],
        compiler_params=pltpu.CompilerParams(vmem_limit_bytes=24 << 20),
        cost_estimate=pl.CostEstimate(
            flops=8 * seqlen * features * features + 20 * HEADS * seqlen * seqlen * 128,
            bytes_accessed=attn_w.size * 4 + source.size * 24,
            transcendentals=2 * HEADS * seqlen * seqlen,
        ),
    )(place, source, modulation, attn_w, attn_w_other, qkv, grad_middle, grad_attn, rows)


def run_products(lefts, lefts_other, rights, rights_other, left_at, right_at, count, mine, chunk):
    _, seqlen, features = lefts.shape
    width = rights.shape[-1]
    left_spec = pl.BlockSpec((1, seqlen, features), lambda step: (left_at(step), 0, 0))
    right_spec = pl.BlockSpec((1, seqlen, width), lambda step: (right_at(step), 0, 0))
    specs = [left_spec, left_spec, right_spec, right_spec]
    cost = pl.CostEstimate(
        flops=4 * count * seqlen * features * width,
        bytes_accessed=count * features * width * 6,
        transcendentals=0,
    )
    if chunk % 16:
        total = pl.pallas_call(
            plain_products,
            name="plain_products",
            grid=(count,),
            out_shape=struct((count, features, width), jnp.float32),
            in_specs=specs,
            out_specs=pl.BlockSpec((1, features, width), lambda step: (step, 0, 0)),
            cost_estimate=cost,
        )(lefts, lefts_other, rights, rights_other)
        keep, send = split_bit(
            total.reshape(count, features // (2 * chunk), 2, chunk, width), mine, 2, jnp.bfloat16
        )
        shape = (count, features // 2, width)
        return keep.reshape(shape), send.reshape(shape)
    half_spec = pl.BlockSpec((1, features // 2, width), lambda step: (step, 0, 0))
    return pl.pallas_call(
        functools.partial(pair_products, chunk),
        name="pair_products",
        grid=(count,),
        out_shape=(
            struct((count, features // 2, width), jnp.float32),
            struct((count, features // 2, width), jnp.bfloat16),
        ),
        in_specs=[SMEM] + specs,
        out_specs=(half_spec, half_spec),
        cost_estimate=cost,
    )(mine[None], lefts, lefts_other, rights, rights_other)


def muon_steps(block, scaled_ref):
    values = block.astype(jnp.float32)
    scaled_ref[...] = (values / (jnp.sqrt(jnp.sum(values * values)) + 1e-07)).astype(jnp.bfloat16)

    @pl.loop(0, NS_ITERS)
    def _(iteration):
        scaled = scaled_ref[...]
        gram = contract(scaled, scaled, 1, 1).astype(jnp.bfloat16)
        square = contract(gram, gram, 1, 0)
        mixed = (COEF_SECOND * gram.astype(jnp.float32) + COEF_THIRD * square).astype(jnp.bfloat16)
        scaled_ref[...] = (
            COEF_FIRST * scaled.astype(jnp.float32) + contract(mixed, scaled, 1, 0)
        ).astype(jnp.bfloat16)


def orthogonalize_halves(place_ref, mine_ref, other_ref, out_ref, scaled_ref):
    core = place_ref[0]
    mine, other = mine_ref[...], other_ref[...]
    low, high = jnp.where(core == 1, other, mine), jnp.where(core == 1, mine, other)
    muon_steps(jnp.concatenate([low, high], axis=1), scaled_ref)
    out_ref[...] = split_columns(scaled_ref[...], core)[0]


def orthogonalize_whole(block_ref, out_ref):
    muon_steps(block_ref[0], out_ref.at[0])


def muon_cost(count, rows):
    return pl.CostEstimate(
        flops=6 * count * NS_ITERS * rows**3, bytes_accessed=4 * count * rows**2, transcendentals=0
    )


def run_orthogonalize_halves(place, mine, other):
    return pl.pallas_call(
        orthogonalize_halves,
        name="orthogonalize_halves",
        out_shape=struct(mine.shape, mine.dtype),
        in_specs=[SMEM, VMEM, VMEM],
        out_specs=VMEM,
        scratch_shapes=[pltpu.VMEM((mine.shape[0], 2 * mine.shape[1]), mine.dtype)],
        compiler_params=pltpu.CompilerParams(vmem_limit_bytes=24 << 20),
        cost_estimate=muon_cost(1, mine.shape[0]),
    )(place, mine, other)


def run_orthogonalize_whole(blocks):
    spec = pl.BlockSpec((1,) + blocks.shape[1:], lambda step: (step, 0, 0))
    return pl.pallas_call(
        orthogonalize_whole,
        name="orthogonalize_whole",
        grid=(blocks.shape[0],),
        out_shape=struct(blocks.shape, blocks.dtype),
        in_specs=[spec],
        out_specs=spec,
        compiler_params=pltpu.CompilerParams(vmem_limit_bytes=24 << 20),
        cost_estimate=muon_cost(*blocks.shape[:2]),
    )(blocks)


def all_to_all(values):
    return lax.all_to_all(values, "dp", split_axis=0, concat_axis=0, tiled=True)


def to_all(row):
    devices = lax.axis_size("dp")
    return all_to_all(jnp.broadcast_to(row[None], (devices,) + row.shape))


def on_device(latents, conditioning, cotangent, weights, biases, momenta, bias_momenta, counts):
    _, seqlen, features = latents.shape
    block_count, share, _ = weights.shape
    hidden_blocks = (block_count - 10) // 2
    bias_count = biases.shape[0]
    devices = lax.axis_size("dp")
    myself = lax.axis_index("dp")
    core = bit_of(myself, 0)
    bits = index_bits(devices)
    orders = colour_orders(devices)
    ranks = jnp.arange(devices, dtype=jnp.int32)
    live_here = jnp.sum(jnp.where(ranks == myself, counts, 0)) > 0

    lowered = weights.astype(jnp.bfloat16)
    ada_w = lowered[:ADA]
    condition = conditioning[0].astype(jnp.float32)
    silu_cond = jax.nn.silu(condition).astype(jnp.bfloat16)

    half = features // 2
    rest = lowered[ADA:]
    columns_mine = lax.dynamic_slice_in_dim(rest, core * half, half, 2)
    columns_other = lax.dynamic_slice_in_dim(rest, (1 - core) * half, half, 2)
    columns_other = flip(columns_other, 0)
    chip_rows = jnp.where(
        core == 1,
        jnp.concatenate([columns_other, columns_mine], axis=1),
        jnp.concatenate([columns_mine, columns_other], axis=1),
    )
    bounds = [0, 10 - ADA, 10 - ADA + hidden_blocks, block_count - ADA]
    stages = bits - 1
    small_all = to_all(
        jnp.concatenate([silu_cond, biases.astype(jnp.bfloat16).reshape(-1)])
    )

    def modulations(small_all):
        silu_rows = lax.dynamic_slice_in_dim(small_all[:, :features], myself * share, share, 1)
        mod_parts = product("ld,kde->lke", silu_rows, ada_w).reshape(devices, ADA * features)
        offsets = (
            small_all[:, features:]
            .reshape(devices, bias_count, share)
            .transpose(1, 0, 2)
            .reshape(bias_count, features)
            .astype(jnp.float32)
        )
        return small_all, silu_rows, offsets, all_to_all(mod_parts)

    groups, (small_all, silu_rows, offsets, mod_sums) = gather_all(
        [chip_rows[low:high] for low, high in zip(bounds[:-1], bounds[1:])],
        [tuple(reversed(order)) for order in orders],
        myself,
        small_all,
        modulations,
    )
    modulation = jnp.sum(mod_sums, axis=0).reshape(ADA, features) + offsets[:ADA]
    rows = 2 * share
    held_orders = [tuple(reversed(order)) for order in orders]
    pairs = []
    for index, order in enumerate(held_orders):
        group = groups[index].reshape(devices // 2, -1, rows, half)
        if rows % 16:
            group = jnp.stack([group[place] for place in chunk_places(order)], axis=1)
            group = group.reshape(1, -1, features, half)
            held_orders[index] = ()
        pairs.append((group, flip(group, 0)))
    attn_ws, up_ws, down_ws = pairs

    place = jnp.stack([core, live_here.astype(jnp.int32)]).astype(jnp.int32)
    extra = max(0, block_count - devices // 2)
    assert extra % 2 == 0 and extra <= ADA
    main = block_count - extra
    spare = ()
    spare_bits = tuple(reversed(range(1, bits)))
    if extra:
        spare = momenta[:extra].astype(jnp.bfloat16).reshape(2, extra // 2, share, features)
        spare_mine = lax.dynamic_index_in_dim(spare, core, 0, keepdims=False)
        spare_other = lax.dynamic_index_in_dim(spare, 1 - core, 0, keepdims=False)
        spare_other = flip(spare_other, 0)
        spare = joined(spare_mine, spare_other, core, 1).reshape(extra // 2, 2 * share, features)
        modulation, spare = lax.optimization_barrier((modulation, spare))
        spare = gather_step(spare, spare_bits, spare_bits[0], myself)
        for bit in spare_bits[1:-2]:
            spare = gather_step(spare, spare_bits, bit, myself)
        received = flip_by_core(spare, spare_bits[-2], spare_bits[-1])
        near = jnp.stack([spare, received])
        far = flip_by_core(near, spare_bits[-1], spare_bits[-2])
        spare = corner_rows(near, far, spare_bits, myself)
        spare = spare.reshape(extra // 2, features, features)
    lefts, qkv, attn_out, middle = run_attention_forward(
        held_orders[0], place, latents[0], modulation, offsets, *attn_ws
    )
    lefts_other = flip(lefts, 0)
    output, hidden, mlp_keep, mlp_send, grad_middle, grad_attn, rows = run_mlp(
        held_orders[1:],
        place,
        lefts,
        middle,
        attn_out,
        cotangent[0],
        modulation,
        offsets,
        up_ws,
        down_ws,
    )
    hidden_other = flip(hidden, 0)
    mlp_other = flip(mlp_send, 0)

    def spread(mats, count):
        return mats.reshape((mats.shape[0],) + (2,) * count + (2 * share, half))

    def products(left, left_other, right, right_other, left_at, right_at, count, order):
        return run_products(
            left,
            left_other,
            right,
            right_other,
            left_at,
            right_at,
            count,
            bit_of(myself, order[0]),
            share << order[0],
        )

    down_halves = products(
        hidden, hidden_other, mlp_keep, mlp_other, lambda b: b, lambda b: 0, hidden_blocks, orders[0]
    )
    up_halves = products(
        lefts, lefts_other, mlp_keep, mlp_other, lambda b: 2, lambda b: b + 1, hidden_blocks, orders[1]
    )
    input_grad, attn_keep, attn_send, grad_offsets = run_attention_backward(
        held_orders[0], place, latents[0], modulation, *attn_ws, qkv, grad_middle, grad_attn, rows
    )
    attn_other = flip(attn_send, 0)
    attn_halves = products(
        lefts, lefts_other, attn_keep, attn_other, lambda b: b // 3, lambda b: b, 4, orders[2]
    )

    grad_mod_b = grad_offsets[:ADA].astype(jnp.bfloat16).reshape(-1)
    by_holder = (
        grad_offsets.reshape(bias_count, devices, share)
        .transpose(1, 0, 2)
        .reshape(devices, bias_count * share)
    )
    coarse = lax.reduce_precision(by_holder, 8, 7)
    mod_and_offsets = jnp.concatenate(
        [
            jnp.broadcast_to(grad_mod_b[None], (devices, ADA * features)),
            coarse.astype(jnp.bfloat16),
            (by_holder - coarse).astype(jnp.bfloat16),
        ],
        axis=1,
    )
    mod_and_offsets = all_to_all(mod_and_offsets)

    def conditioning_grads(mod_and_offsets):
        mod_all = mod_and_offsets[:, : ADA * features].reshape(devices, ADA, features)
        silu_parts = product("lke,kde->ld", mod_all, ada_w)
        return mod_and_offsets, mod_all, all_to_all(silu_parts)

    sums, (mod_and_offsets, mod_all, grad_silu) = scatter_all(
        [attn_halves, up_halves, down_halves],
        [orders[2], orders[1], orders[0]],
        myself,
        1,
        spread,
        {stages - 1: lambda _: conditioning_grads(mod_and_offsets)},
    )
    chip_rows = jnp.concatenate(sums, axis=0)
    rows_mine = lax.dynamic_slice_in_dim(chip_rows, core * share, share, 1)
    rows_other = flip(lax.dynamic_slice_in_dim(chip_rows, (1 - core) * share, share, 1), 0)
    rest_share = jnp.where(
        core == 1,
        jnp.concatenate([rows_other, rows_mine], axis=2),
        jnp.concatenate([rows_mine, rows_other], axis=2),
    )

    ada_share = product("ld,lke->kde", silu_rows, mod_all)
    offset_share = jnp.sum(
        mod_and_offsets[:, ADA * features :]
        .astype(jnp.float32)
        .reshape(devices * 2, bias_count, share),
        axis=0,
    )

    grad_scale = lax.rsqrt((seqlen * jnp.sum(counts)).astype(jnp.float32))
    weight_grads = jnp.concatenate([ada_share, rest_share], axis=0) * grad_scale
    bias_grads = offset_share * grad_scale
    new_momenta = BETA_WEIGHT * momenta + weight_grads
    new_bias_momenta = BETA_BIAS * bias_momenta + bias_grads
    new_biases = biases - RATE_BIAS * new_bias_momenta

    outgoing = (
        new_momenta[extra:]
        .astype(jnp.bfloat16)
        .reshape(main, share, 2, half)
        .transpose(0, 2, 1, 3)
        .reshape(2 * main, share, half)
    )
    outgoing = jnp.pad(outgoing, ((0, devices - 2 * main), (0, 0), (0, 0)))
    columns_mine = all_to_all(outgoing).reshape(features, half)
    ortho_half = run_orthogonalize_halves(place, columns_mine, flip(columns_mine, 0))
    ortho_local = (
        all_to_all(ortho_half.reshape(devices, share, half))[: 2 * main]
        .reshape(main, 2, share, half)
        .transpose(0, 2, 1, 3)
        .reshape(main, share, features)
    )
    if extra:
        silu_all = small_all[:, :features]
        mod_mine = lax.dynamic_slice_in_dim(mod_all, core * (extra // 2), extra // 2, 1)
        spare_grads = product("ld,lke->kde", silu_all, mod_mine) * grad_scale
        spare = (BETA_WEIGHT * spare.astype(jnp.float32) + spare_grads).astype(jnp.bfloat16)
        spare_ortho = run_orthogonalize_whole(spare)
        chip_ortho = lax.dynamic_slice_in_dim(
            spare_ortho, (myself - core) * share, 2 * share, 1
        ).reshape(extra // 2, 2, share, features)
        ortho_mine = lax.dynamic_index_in_dim(chip_ortho, core, 1, keepdims=False)
        ortho_other = flip(
            lax.dynamic_index_in_dim(chip_ortho, 1 - core, 1, keepdims=False), 0
        )
        spare_local = joined(ortho_mine, ortho_other, core, 0).reshape(extra, share, features)
        ortho_local = jnp.concatenate([spare_local, ortho_local])
    silu_back = jax.vjp(jax.nn.silu, condition)[1]
    cond_grad = silu_back(grad_silu.reshape(features))[0] * seqlen ** (-0.5)
    new_weights = weights - RATE_WEIGHT * ortho_local.astype(jnp.float32)
    cond_grad = jnp.where(live_here, cond_grad, jnp.zeros_like(cond_grad))[None]
    return (
        output[None],
        input_grad[None],
        cond_grad,
        weight_grads,
        bias_grads,
        new_weights,
        new_momenta,
        new_biases,
        new_bias_momenta,
    )


def solution(mesh):
    return jax.shard_map(
        on_device,
        mesh=mesh,
        in_specs=(
            P("dp", None, None),
            P("dp", None),
            P("dp", None, None),
            P(None, "dp", None),
            P(None, "dp"),
            P(None, "dp", None),
            P(None, "dp"),
            P(),
        ),
        out_specs=(
            P("dp", None, None),
            P("dp", None, None),
            P("dp", None),
            P(None, "dp", None),
            P(None, "dp"),
            P(None, "dp", None),
            P(None, "dp", None),
            P(None, "dp"),
            P(None, "dp"),
        ),
        check_vma=False,
    )
```
